128 devices in a mesh: bx: 16 (over y, z), by: 8 (over x, core).
Axes of the slice: x: 4, y: 4, z: 4, core: 2. Of those that a mesh axis runs over, the one named last changes fastest.
Arguments:
- normals: float32 [3, 524288], P(None, ('bx', 'by')), may hold values from -60 to 60
- owners: int32 [524288, 1], P(('bx', 'by')), may hold values from 0 to 127; in each aligned block of 4096 rows (0 to 4095, 4096 to 8191, ...) at most 64 rows name the same one
- cells: int32 [524288], P(('bx', 'by')), may hold values from 0 to 262143
- levels: int32 [16, 8], P('bx', 'by'), may hold values from 0 to 3
- rows_inverse: float32 [256, 256], replicated, may hold values from 0 to 0.25
- columns_inverse: float32 [512, 512], replicated, may hold values from 0 to 0.25
- depth_inverse: float32 [256, 256], replicated, may hold values from 0 to 0.25
Outputs:
- iterate: float32 [256, 512, 256], P('bx', 'by')
- implicit: float32 [524288], P(('bx', 'by'))
The draws below stay inside these ranges and needn't reach their ends.
Inputs may be any that keep to these rules, and one draw needn't show every extreme that they name: `owners`: A brick's number is its index along bx times the number of devices along by plus its index along by. Among the 4096 points of one device at most 64 name one brick, and in every draw some brick is named by exactly 64 of them.
All inputs are finite; a program needn't handle non-finite values.
Results may differ from the reference program's by a relative error of at most 0.0001.
Values sent between devices are 32-bit elements; how exact they have to be, the bound alone decides.
A program may use at most 320 MiB of HBM per device.

```python
import math
import jax
import jax.numpy as jnp
import numpy as np
from jax import lax

CX = 16
CY = 64
NZ = 256
P_DEV = 4096
ITERS = 4
CAP = 64
NX = 256
NY = 512
POINTS = 524288
N_BX = 16
N_BY = 8


def line_matrix(key, order):
    index = jnp.arange(order)
    distance = jnp.abs(index[:, None] - index[None, :]).astype(jnp.float32)
    strength = jax.random.uniform(jax.random.fold_in(key, 3), (), jnp.float32, 2.0, 3.5)
    spread = order * jax.random.uniform(jax.random.fold_in(key, 4), (), jnp.float32, 0.125, 0.5)
    factors = jnp.exp(jax.random.uniform(jax.random.fold_in(key, 1), (order, order), jnp.float32, math.log(0.1), math.log(3.0)))
    kernel = 0.25 * strength / spread * jnp.exp(-distance / spread) * factors
    diagonal = jax.random.uniform(jax.random.fold_in(key, 2), (order,), jnp.float32, 0.4, 0.8)
    return 0.1 * (jnp.diag(diagonal) + kernel)


def draw_rows_inverse(key, part):
    return line_matrix(jax.random.fold_in(key, 11), NX)


def draw_columns_inverse(key, part):
    return line_matrix(jax.random.fold_in(key, 12), NY)


def draw_depth_inverse(key, part):
    return line_matrix(jax.random.fold_in(key, 13), NZ)


def set_ends(drawn, rng, smallest, top_value):
    index_at = [jax.random.randint(jax.random.fold_in(rng, axis), (), 0, length) for axis, length in enumerate(drawn.shape)]
    longest = drawn.shape.index(max(drawn.shape))
    neighbour = index_at[:longest] + [(index_at[longest] + 1) % drawn.shape[longest]] + index_at[longest + 1:]
    return drawn.at[tuple(index_at)].set(smallest).at[tuple(neighbour)].set(top_value)


def block_scale(stream_key, shape, cuts, smallest, top_value):
    loudness, own = 1.0, jax.random.fold_in(stream_key, 6)
    for axis_at, shards_of in cuts:
        steps = jnp.exp(jax.random.uniform(jax.random.fold_in(own, axis_at), (shards_of,), jnp.float32, smallest / len(cuts), top_value / len(cuts)))
        loudness = loudness * jnp.repeat(steps, shape[axis_at] // shards_of).reshape([-1 if axis == axis_at else 1 for axis in range(len(shape))])
    return loudness


def shared_out(key, own, number, rows, count, top, limit, slope):
    order = jax.random.permutation(key, count)
    crowded, common = shares(count, rows * top, limit, slope, True), shares(count, rows * top, limit, slope, False)
    places = jnp.arange(count)

    def named(tallies, rotation):
        used = int((tallies > 0).sum())
        fixed = max(1, used // 4)
        shifted = fixed + (places - fixed + rotation * (used - fixed)) % max(1, count - fixed)
        return jnp.zeros((count,), jnp.int32).at[order[jnp.where(places < fixed, places, shifted)]].set(jnp.asarray(tallies, jnp.int32))

    tallies = jnp.where(number % 4 == 0, named(crowded, number // 4), named(common, number - number // 4 - 1))
    mixed = jax.random.permutation(jax.random.fold_in(own, 3), count)
    giver, sink = mixed[0:count // 2 * 2:2], mixed[1:count // 2 * 2:2]
    room = jnp.minimum(tallies[giver] - 1, limit - tallies[sink]) // 2
    room = jnp.where((giver == order[0]) | (sink == order[0]) | (tallies[sink] == 0), 0, jnp.maximum(room, 0))
    shifted = jax.random.randint(jax.random.fold_in(own, 4), (count // 2,), 0, 1 << 20) % (room + 1)
    tallies = tallies.at[giver].add(-shifted).at[sink].add(shifted)
    items = jnp.searchsorted(jnp.cumsum(tallies), jnp.arange(rows * top), side="right").astype(jnp.int32)
    listing = items.reshape(top, rows).T
    listing = listing[jax.random.permutation(jax.random.fold_in(own, 1), rows)]
    rotation = jax.random.randint(jax.random.fold_in(own, 2), (rows, 1), 0, top)
    return jnp.take_along_axis(listing, (jnp.arange(top)[None, :] + rotation) % top, axis=1)


def shares(amount, total, bound, slope, full):
    loads = [(1 << 20) // math.isqrt(grade ** slope) + 1 for grade in range(1, amount + 1)]
    largest = bound if full else min(bound, max(-(-total // amount), total * loads[0] // sum(loads)))
    least = 1 if total - largest >= amount - 1 else 0
    given, spare = [largest] + [least] * (amount - 1), total - largest - least * (amount - 1)
    while spare > 0:
        movable = [i for i in range(1, amount) if given[i] < largest] or [i for i in range(1, amount) if given[i] < bound]
        whole, left = sum([loads[i] for i in movable]), spare
        for i in movable:
            addition = min(bound - given[i], max(1, left * loads[i] // whole), spare)
            given[i] = given[i] + addition
            spare = spare - addition
    return np.array(given)


def scatter_about(own_key, dims, scale, most, split=(), held_as=jnp.bfloat16):
    level = block_scale(own_key, dims, split, -0.22, 0.18) if split else 1.0
    entries = jax.random.normal(own_key, dims, jnp.float32) * scale * level
    return jnp.minimum(jnp.maximum(entries, -most), most).astype(held_as)


def setup_inputs(seed: int = 0) -> dict:
    key_list = jax.random.split(jax.random.key(seed), 8)
    normals = scatter_about(key_list[0], (3, POINTS), 10.0, 60.0, ((1, 128),), jnp.float32)
    owners_keys = jax.random.split(jax.random.fold_in(key_list[1], 1), POINTS // P_DEV)
    owners_turns = jax.random.permutation(jax.random.fold_in(key_list[1], 3), POINTS // P_DEV)
    owners = jax.vmap(lambda own, number: shared_out(jax.random.fold_in(key_list[1], 2), own, number, P_DEV, N_BX * N_BY, 1, CAP, 2))(owners_keys, owners_turns).reshape((POINTS, 1))
    cells = set_ends(jax.random.randint(key_list[2], (POINTS,), 0, CX * CY * NZ), jax.random.fold_in(key_list[2], 1), 0, (CX * CY * NZ) - 1).astype(jnp.int32)
    levels = set_ends(jax.random.randint(key_list[3], (N_BX, N_BY), 0, 4), jax.random.fold_in(key_list[3], 1), 0, 3).astype(jnp.int32)
    rows_inverse = draw_rows_inverse(jax.random.fold_in(key_list[7], 71), 0)
    columns_inverse = draw_columns_inverse(jax.random.fold_in(key_list[7], 71), 0)
    depth_inverse = draw_depth_inverse(jax.random.fold_in(key_list[7], 71), 0)
    return {"normals": normals, "owners": owners, "cells": cells, "levels": levels, "rows_inverse": rows_inverse, "columns_inverse": columns_inverse, "depth_inverse": depth_inverse}


screen_base = 1.0


def stencil(field, screening):
    padded = jnp.pad(field, 1)
    beside = padded[2:, 1:-1, 1:-1] + padded[:-2, 1:-1, 1:-1]
    beside = beside + padded[1:-1, 2:, 1:-1] + padded[1:-1, :-2, 1:-1]
    beside = beside + padded[1:-1, 1:-1, 2:] + padded[1:-1, 1:-1, :-2]
    return (6.0 + screening) * field - beside


def reference(normals, owners, cells, levels, rows_inverse, columns_inverse, depth_inverse):
    target = owners[:, 0]
    first_index = (target // N_BY) * CX + cells // (CY * NZ)
    second_index = (target % N_BY) * CY + (cells // NZ) % CY
    third_index = cells % NZ
    vector_field = jnp.zeros((3, NX, NY, NZ), jnp.float32).at[:, first_index, second_index, third_index].add(normals)
    padded = jnp.pad(vector_field, ((0, 0), (1, 1), (1, 1), (1, 1)))
    source = -0.5 * ((padded[0, 2:, 1:-1, 1:-1] - padded[0, :-2, 1:-1, 1:-1])
                     + (padded[1, 1:-1, 2:, 1:-1] - padded[1, 1:-1, :-2, 1:-1])
                     + (padded[2, 1:-1, 1:-1, 2:] - padded[2, 1:-1, 1:-1, :-2]))
    screening = screen_base * (1.0 + levels.astype(jnp.float32))
    screening = jnp.repeat(jnp.repeat(screening, CX, 0), CY, 1)[:, :, None]
    highest = lax.Precision.HIGHEST
    iterate = jnp.zeros((NX, NY, NZ), jnp.float32)
    for iteration in range(ITERS):
        remainder = source - stencil(iterate, screening)
        iterate = iterate + jnp.einsum("ab,bjk->ajk", rows_inverse, remainder, precision=highest)
        remainder = source - stencil(iterate, screening)
        iterate = iterate + jnp.einsum("ab,ibk->iak", columns_inverse, remainder, precision=highest)
        remainder = source - stencil(iterate, screening)
        iterate = iterate + jnp.einsum("ab,ijb->ija", depth_inverse, remainder, precision=highest)
    implicit = iterate[first_index, second_index, third_index]
    return iterate, implicit
```

```python
import functools
import jax
import jax.numpy as jnp
from jax import lax
from jax.experimental import pallas as pl
from jax.experimental.pallas import tpu as pltpu
from jax.sharding import PartitionSpec as P

CX, CY, NZ, ITERS = 16, 64, 256, 4
NI, NJ = 16, 8
MESH = pl.DeviceIdType.MESH
F32, BF16 = jnp.float32, jnp.bfloat16


def split(v):
    hi = v.astype(BF16)
    return hi, (v - hi.astype(F32)).astype(BF16)


def dot3(a_hi, a_lo, b_hi, b_lo, dims=(((1,), (0,)), ((), ()))):
    mul = functools.partial(lax.dot_general, dimension_numbers=dims, preferred_element_type=F32)
    return mul(a_hi, b_hi) + (mul(a_lo, b_hi) + mul(a_hi, b_lo))


def remote(src, dst, send, recv, device):
    return pltpu.make_async_remote_copy(
        src_ref=src, dst_ref=dst, send_sem=send, recv_sem=recv, device_id=device, device_id_type=MESH
    )


def bx_peer(bx, t):
    y, z = bx // 4, bx % 4
    return ((y + t // 4) % 4) * 4 + (z + t % 4) % 4


def al(v, m):
    return pl.multiple_of(v * m, m)


def greet(bx, by):
    barrier = pltpu.get_barrier_semaphore()
    count = 0
    for side in (0, 1, NJ - 1):
        for t in range(NI):
            if side == 0 and t == 0:
                continue
            pl.semaphore_signal(
                barrier, inc=1, device_id=(bx_peer(bx, t), (by + side) % NJ), device_id_type=MESH
            )
            count += 1
    for t in range(2, NJ - 1):
        pl.semaphore_signal(barrier, inc=1, device_id=(bx, (by + t) % NJ), device_id_type=MESH)
        count += 1
    pl.semaphore_wait(barrier, count)


def relax(
    f_ref, lev_ref, mx_ref, my_ref, mz_ref, u_ref,
    r, xin, dxp, dx, edge, yhx, yin, dyl, dy, ye, yhy, dz, ze, yhz,
    mxs, mys, mzs,
    xs, xr, bs, br, es, er, ys, yr, cs, cr, ns, nr, hs, hr, zs, zr,
):
    bx, by = lax.axis_index("bx"), lax.axis_index("by")
    yg, zh = bx // 2, bx % 2
    zero = jnp.zeros((8, 128), F32)
    dxp[0] = zero
    dxp[257] = zero
    for ref in (yhx, yhy, yhz):
        ref[...] = jnp.zeros(ref.shape, F32)
    ye[...] = jnp.zeros(ye.shape, F32)
    for it in range(ITERS):
        for ref in (dy, dz):
            ref[it, 0] = jnp.zeros((CY, NZ), F32)
            ref[it, CX + 1] = jnp.zeros((CY, NZ), F32)
    r[...] = f_ref[...]
    u_ref[...] = jnp.zeros(u_ref.shape, F32)
    for m, ms in ((mx_ref, mxs), (my_ref, mys), (mz_ref, mzs)):
        ms[0], ms[1] = split(m[...])
    greet(bx, by)
    diagonal = 6.0 + (1.0 + lev_ref[0, 0].astype(F32))

    def stencil(d, low, high):
        @pl.loop(0, CX)
        def _(x):
            c = d[x + 1]
            zi = lax.broadcasted_iota(jnp.int32, (CY, NZ), 1)
            yi = lax.broadcasted_iota(jnp.int32, (CY, NZ), 0)
            near = d[x] + d[x + 2]
            near = near + jnp.where(zi == 0, 0.0, pltpu.roll(c, 1, 1))
            near = near + jnp.where(zi == NZ - 1, 0.0, pltpu.roll(c, NZ - 1, 1))
            near = near + jnp.where(yi == 0, low(x), pltpu.roll(c, 1, 0))
            near = near + jnp.where(yi == CY - 1, high(x), pltpu.roll(c, CY - 1, 0))
            r[x] = r[x] - (diagonal * c - near)
            u_ref[x] = u_ref[x] + c

    def x_planes(d, send, recv):
        down = remote(d.at[1], d.at[CX + 1], send.at[0], recv.at[0], (jnp.maximum(bx - 1, 0), by))
        up = remote(d.at[CX], d.at[0], send.at[1], recv.at[1], (jnp.minimum(bx + 1, NI - 1), by))
        return down, up

    @pl.loop(0, ITERS)
    def _(it):
        copies = []
        for t in range(NI):
            k = bx_peer(bx, t)
            src = r.at[:, pl.ds(al(k // 2, 8), 8), pl.ds(al(k % 2, 128), 128)]
            dst = xin.at[it, pl.ds(bx * 16, 16)]
            if t:
                copies.append(remote(src, dst, xs.at[t], xr.at[t], (k, by)))
            else:
                copies.append(pltpu.make_async_copy(src, dst, xs.at[0]))
            copies[-1].start()
        for c in copies:
            c.wait()
        lines = xin.at[it].reshape(NI * CX * 8, 128)
        moved = dxp.reshape((NI * CX + 2) * 8, 128)
        for s in range(0, 8, 2):
            v = jnp.concatenate(
                [lines[pl.ds(s, 256, stride=8), :], lines[pl.ds(s + 1, 256, stride=8), :]], axis=1
            )
            d = dot3(mxs[0], mxs[1], *split(v))
            moved[pl.ds(8 + s, 256, stride=8), :] = d[:, :128]
            moved[pl.ds(9 + s, 256, stride=8), :] = d[:, 128:]
            if s == 0:
                edge[0] = d[:, :128]
            if s == 6:
                edge[1] = d[:, 128:]
        copies = []
        for t in range(NI):
            k = bx_peer(bx, t)
            src = dxp.at[pl.ds(k * 16, 18)]
            dst = dx.at[it, :, pl.ds(al(yg, 8), 8), pl.ds(al(zh, 128), 128)]
            if t:
                copies.append(remote(src, dst, bs.at[t], br.at[t], (k, by)))
            else:
                copies.append(pltpu.make_async_copy(src, dst, bs.at[0]))
            copies[-1].start()

        def edges(side, beside):
            out = []
            for t in range(NI):
                k = bx_peer(bx, t)
                out.append(
                    remote(
                        edge.at[side, pl.ds(al(k, 16), 16)],
                        yhx.at[it, side, :, pl.ds(al(zh, 128), 128)],
                        es.at[side, t],
                        er.at[side, zh],
                        (k, beside),
                    )
                )
            return out

        def half(side, z):
            return remote(
                edge.at[side, pl.ds(0, 16)], yhx.at[it, side, :, pl.ds(128 * z, 128)],
                es.at[side, 0], er.at[side, z], (bx, by),
            )

        below, above = jnp.maximum(by - 1, 0), jnp.minimum(by + 1, NJ - 1)

        @pl.when((yg == 0) & (by > 0))
        def _():
            for c in edges(0, below):
                c.start()

        @pl.when((yg == 7) & (by < NJ - 1))
        def _():
            for c in edges(1, above):
                c.start()

        for c in copies:
            c.wait()

        @pl.when((yg == 0) & (by > 0))
        def _():
            for c in edges(0, below):
                c.wait_send()

        @pl.when((yg == 7) & (by < NJ - 1))
        def _():
            for c in edges(1, above):
                c.wait_send()

        @pl.when(by < NJ - 1)
        def _():
            half(0, 0).wait_recv()
            half(0, 1).wait_recv()

        @pl.when(by > 0)
        def _():
            half(1, 0).wait_recv()
            half(1, 1).wait_recv()

        stencil(
            dx.at[it],
            lambda x: yhx[it, 1, pl.ds(x, 1), :],
            lambda x: yhx[it, 0, pl.ds(x, 1), :],
        )

        copies = []
        for t in range(NJ):
            j = (by + t) % NJ
            src = r.at[pl.ds(2 * j, 2)]
            dst = yin.at[it, :, pl.ds(al(by, 64), 64), :]
            if t:
                copies.append(remote(src, dst, ys.at[t], yr.at[t], (bx, j)))
            else:
                copies.append(pltpu.make_async_copy(src, dst, ys.at[0]))
            copies[-1].start()
        for c in copies:
            c.wait()
        for e in range(2):
            d = dot3(mys[0], mys[1], *split(yin[it, e]))
            dyl[e] = d
            for j in range(NJ):
                if j:
                    ye[j, e : e + 1] = d[64 * j - 1 : 64 * j]
                if j < NJ - 1:
                    ye[j, 2 + e : 3 + e] = d[64 * j + 64 : 64 * j + 65]
        copies = []
        for t in range(NJ):
            j = (by + t) % NJ
            main = (dyl.at[:, pl.ds(al(j, 64), 64), :], dy.at[it, pl.ds(1 + 2 * by, 2)])
            rows = (ye.at[j], yhy.at[it, by])
            if t:
                copies.append(remote(*main, cs.at[t], cr.at[by], (bx, j)))
                copies.append(remote(*rows, ns.at[t], nr.at[t], (bx, j)))
            else:
                copies.append(pltpu.make_async_copy(*main, cr.at[by]))
                copies.append(pltpu.make_async_copy(*rows, ns.at[0]))
            copies[-2].start()
            copies[-1].start()

        def arrived(m):
            remote(
                dyl.at[:, pl.ds(0, 64), :], dy.at[it, pl.ds(1 + 2 * m, 2)], cs.at[0], cr.at[m], (bx, by)
            ).wait_recv()

        down, up = x_planes(dy.at[it], hs, hr)
        arrived(0)

        @pl.when(bx > 0)
        def _():
            down.start()

        arrived(NJ - 1)

        @pl.when(bx < NI - 1)
        def _():
            up.start()

        for m in range(1, NJ - 1):
            arrived(m)
        for t in range(1, NJ):
            copies[2 * t].wait_send()
            copies[2 * t + 1].wait()
        copies[1].wait()

        @pl.when(bx > 0)
        def _():
            down.wait_send()
            up.wait_recv()

        @pl.when(bx < NI - 1)
        def _():
            up.wait_send()
            down.wait_recv()

        stencil(
            dy.at[it],
            lambda x: yhy[it, x // 2, pl.ds(x % 2, 1), :],
            lambda x: yhy[it, x // 2, pl.ds(2 + x % 2, 1), :],
        )

        nt = (((1,), (1,)), ((), ()))

        def z_planes(x, n):
            v = r[pl.ds(x, n)].reshape(n * CY, NZ)
            d = dot3(*split(v), mzs[0], mzs[1], nt)
            dz[it, pl.ds(x + 1, n)] = d.reshape(n, CY, NZ)

        z_planes(0, 1)
        z_planes(CX - 1, 1)
        down, up = x_planes(dz.at[it], zs, zr)
        more = it < ITERS - 1

        @pl.when(more & (bx > 0))
        def _():
            down.start()

        @pl.when(more & (bx < NI - 1))
        def _():
            up.start()

        for x in range(1, CX - 1, 2):
            z_planes(x, 2)

        @pl.when(more)
        def _():
            for x in range(CX):
                ze[0, x : x + 1] = dz[it, x + 1, 0:1]
                ze[1, x : x + 1] = dz[it, x + 1, CY - 1 : CY]
            low = remote(ze.at[0], yhz.at[it, 0], zs.at[2], zr.at[2], (bx, below))
            high = remote(ze.at[1], yhz.at[it, 1], zs.at[3], zr.at[3], (bx, above))

            @pl.when(by > 0)
            def _():
                low.start()

            @pl.when(by < NJ - 1)
            def _():
                high.start()

            @pl.when(by > 0)
            def _():
                low.wait_send()
                high.wait_recv()

            @pl.when(by < NJ - 1)
            def _():
                high.wait_send()
                low.wait_recv()

            @pl.when(bx > 0)
            def _():
                down.wait_send()
                up.wait_recv()

            @pl.when(bx < NI - 1)
            def _():
                up.wait_send()
                down.wait_recv()

            stencil(
                dz.at[it],
                lambda x: yhz[it, 1, pl.ds(x, 1), :],
                lambda x: yhz[it, 0, pl.ds(x, 1), :],
            )

        @pl.when(it == ITERS - 1)
        def _():
            u_ref[...] = u_ref[...] + dz[it, pl.ds(1, CX)]


def relaxed(source, levels, rows, columns, depth):
    vm = pl.BlockSpec(memory_space=pltpu.VMEM)
    brick = (CX, CY, NZ)
    tall = (ITERS, CX + 2, CY, NZ)
    dma = pltpu.SemaphoreType.DMA
    return pl.pallas_call(
        relax,
        name="relax",
        out_shape=jax.ShapeDtypeStruct(brick, F32),
        in_specs=[vm, pl.BlockSpec(memory_space=pltpu.SMEM), vm, vm, vm],
        out_specs=vm,
        scratch_shapes=[
            pltpu.VMEM(brick, F32),
            pltpu.VMEM((ITERS, NI * CX, 8, 128), F32),
            pltpu.VMEM((NI * CX + 2, 8, 128), F32),
            pltpu.VMEM(tall, F32),
            pltpu.VMEM((2, NI * CX, 128), F32),
            pltpu.VMEM((ITERS, 2, CX, NZ), F32),
            pltpu.VMEM((ITERS, 2, NJ * CY, NZ), F32),
            pltpu.VMEM((2, NJ * CY, NZ), F32),
            pltpu.VMEM(tall, F32),
            pltpu.VMEM((NJ, 8, NZ), F32),
            pltpu.VMEM((ITERS, NJ, 8, NZ), F32),
            pltpu.VMEM(tall, F32),
            pltpu.VMEM((2, CX, NZ), F32),
            pltpu.VMEM((ITERS, 2, CX, NZ), F32),
            pltpu.VMEM((2, 256, 256), BF16),
            pltpu.VMEM((2, 512, 512), BF16),
            pltpu.VMEM((2, 256, 256), BF16),
            dma((NI,)), dma((NI,)), dma((NI,)), dma((NI,)),
            dma((2, NI)), dma((2, 2)),
            dma((NJ,)), dma((NJ,)), dma((NJ,)), dma((NJ,)), dma((NJ,)), dma((NJ,)),
            dma((2,)), dma((2,)), dma((4,)), dma((4,)),
        ],
        compiler_params=pltpu.CompilerParams(
            collective_id=0, has_side_effects=True, vmem_limit_bytes=52 << 20
        ),
    )(source, levels, rows, columns, depth)


screen_base = 1.0


def padded(shard, sides, width):
    for axis, dim in sides:
        peers, length = (lax.axis_size(axis), shard.shape[dim])
        up = [(i, (i + 1) % peers) for i in range(peers - 1)]
        down = [(j, i) for i, j in up]
        last = lax.slice_in_dim(shard, length - width, length, axis=dim)
        initial = lax.slice_in_dim(shard, 0, width, axis=dim)
        before = lax.ppermute(last, axis, up)
        after = lax.ppermute(initial, axis, down)
        shard = jnp.concatenate([before, shard, after], axis=dim)
    return shard


def local(normals, owners, cells, levels, rows_inverse, columns_inverse, depth_inverse):
    first_count = lax.axis_size("bx")
    second_count = lax.axis_size("by")
    bricks = first_count * second_count
    point_count = cells.shape[0]
    capacity = 2 * point_count // bricks
    brick_cells = CX * CY * NZ
    target = owners[:, 0]
    onehot = (target[:, None] == jnp.arange(bricks, dtype=jnp.int32)[None, :]).astype(jnp.int32)
    ranking = jnp.sum(onehot * (jnp.cumsum(onehot, axis=0) - 1), axis=1)
    slot_index = target * capacity + ranking
    send_normals = jnp.zeros((3, bricks * capacity), jnp.float32).at[:, slot_index].set(normals)
    send_cells = jnp.zeros((bricks * capacity,), jnp.int32).at[slot_index].set(cells)
    arrived_normals, arrived_cells = (
        lax.all_to_all(
            send_normals.reshape(3, bricks, capacity),
            ("bx", "by"),
            split_axis=1,
            concat_axis=1,
            tiled=True,
        ),
        lax.all_to_all(
            send_cells.reshape(1, bricks, capacity),
            ("bx", "by"),
            split_axis=1,
            concat_axis=1,
            tiled=True,
        ),
    )
    flat_cells = arrived_cells.reshape(-1)
    vector_field = (
        jnp.zeros((3, brick_cells), jnp.float32)
        .at[:, flat_cells]
        .add(arrived_normals.reshape(3, -1))
    )
    vector_field = vector_field.reshape(3, CX, CY, NZ)
    stretched = padded(vector_field, (("bx", 1), ("by", 2)), 1)
    z_padded = jnp.pad(vector_field[2], ((0, 0), (0, 0), (1, 1)))
    source = -0.5 * (
        stretched[0, 2:, 1:-1]
        - stretched[0, :-2, 1:-1]
        + (stretched[1, 1:-1, 2:] - stretched[1, 1:-1, :-2])
        + (z_padded[:, :, 2:] - z_padded[:, :, :-2])
    )
    iterate = relaxed(source, levels, rows_inverse, columns_inverse, depth_inverse)
    sampled = iterate.reshape(-1)[flat_cells]
    returned = lax.all_to_all(
        sampled.reshape(1, bricks, capacity), ("bx", "by"), split_axis=1, concat_axis=1, tiled=True
    )
    implicit = returned.reshape(-1)[slot_index]
    return (iterate, implicit)


def solution(mesh):
    placed = (
        P(None, ("bx", "by")),
        P(("bx", "by"), None),
        P(("bx", "by")),
        P("bx", "by"),
        P(),
        P(),
        P(),
    )
    return jax.shard_map(
        local,
        mesh=mesh,
        in_specs=placed,
        out_specs=(P("bx", "by", None), P(("bx", "by"))),
        check_vma=False,
    )
```

```python
import functools
import jax
import jax.numpy as jnp
from jax import lax
from jax.experimental import pallas as pl
from jax.experimental.pallas import tpu as pltpu
from jax.sharding import PartitionSpec as P

CX, CY, NZ, ITERS = 16, 64, 256, 4
NI, NJ = 16, 8
NB, P_DEV, CAP = 128, 4096, 64
MESH = pl.DeviceIdType.MESH
F32, BF16 = jnp.float32, jnp.bfloat16


def split(v):
    hi = v.astype(BF16)
    return hi, (v - hi.astype(F32)).astype(BF16)


def dot3(a_hi, a_lo, b_hi, b_lo, dims=(((1,), (0,)), ((), ()))):
    mul = functools.partial(lax.dot_general, dimension_numbers=dims, preferred_element_type=F32)
    return mul(a_hi, b_hi) + (mul(a_lo, b_hi) + mul(a_hi, b_lo))


def remote(src, dst, send, recv, device):
    return pltpu.make_async_remote_copy(
        src_ref=src, dst_ref=dst, send_sem=send, recv_sem=recv, device_id=device, device_id_type=MESH
    )


def bx_peer(bx, t):
    y, z = bx // 4, bx % 4
    return ((y + t // 4) % 4) * 4 + (z + t % 4) % 4


def al(v, m):
    return pl.multiple_of(v * m, m)


def greet(bx, by):
    barrier = pltpu.get_barrier_semaphore()
    count = 0
    for side in (0, 1, NJ - 1):
        for t in range(NI):
            if side == 0 and t == 0:
                continue
            pl.semaphore_signal(
                barrier, inc=1, device_id=(bx_peer(bx, t), (by + side) % NJ), device_id_type=MESH
            )
            count += 1
    for t in range(2, NJ - 1):
        pl.semaphore_signal(barrier, inc=1, device_id=(bx, (by + t) % NJ), device_id_type=MESH)
        count += 1
    pl.semaphore_wait(barrier, count)


def relax(
    nrm, own, cel, lev_ref, mx_ref, my_ref, mz_ref, u_ref, imp_ref,
    r, xin, dxp, dx, edge, yhx, yin, dyl, dy, ye, yhy, dz, ze, yhz,
    mxs, mys, mzs,
    box, rank, in1, out2, in2, slot, part, vx, vy, vz, fe, fh, smp, ut, back1, got1, back2, got2,
    xs, xr, bs, br, es, er, ys, yr, cs, cr, ns, nr, hs, hr, zs, zr,
    ps, pr, qs, qr, fs, fr, gs, gr, ks, kr,
):
    bx, by = lax.axis_index("bx"), lax.axis_index("by")
    yg, zh = bx // 2, bx % 2
    zero = jnp.zeros((8, 128), F32)
    dxp[0] = zero
    dxp[257] = zero
    for ref in (yhx, yhy, yhz):
        ref[...] = jnp.zeros(ref.shape, F32)
    ye[...] = jnp.zeros(ye.shape, F32)
    for it in range(ITERS):
        for ref in (dy, dz):
            ref[it, 0] = jnp.zeros((CY, NZ), F32)
            ref[it, CX + 1] = jnp.zeros((CY, NZ), F32)
    vx[0] = jnp.zeros((CY, NZ), F32)
    vx[CX + 1] = jnp.zeros((CY, NZ), F32)
    vx[pl.ds(1, CX)] = jnp.zeros((CX, CY, NZ), F32)
    vy[...] = jnp.zeros(vy.shape, F32)
    vz[...] = jnp.zeros(vz.shape, F32)
    fh[...] = jnp.zeros(fh.shape, F32)
    u_ref[...] = jnp.zeros(u_ref.shape, F32)
    for m, ms in ((mx_ref, mxs), (my_ref, mys), (mz_ref, mzs)):
        ms[0], ms[1] = split(m[...])
    greet(bx, by)
    below, above = jnp.maximum(by - 1, 0), jnp.minimum(by + 1, NJ - 1)
    lanes = (((1,), (1,)), ((), ()))

    def fit(rows, index):
        return lax.broadcasted_iota(jnp.int32, (rows, index.shape[1]), 0) == index

    def hot(mask):
        return jnp.where(mask, 1.0, 0.0).astype(BF16)

    def chop(v, n):
        pieces = []
        for _ in range(n):
            pieces.append(v.astype(BF16).astype(F32))
            v = v - pieces[-1]
        return pieces

    before = lax.broadcasted_iota(jnp.int32, (256, 256), 0) < lax.broadcasted_iota(jnp.int32, (256, 256), 1)
    counter = jnp.concatenate([hot(before), jnp.ones((256, 256), BF16)], axis=1)
    box[...] = jnp.zeros(box.shape, F32)

    def dispatch(c, seen):
        at = pl.ds(al(c, 256), 256)
        mine = fit(NB, own[:, at])
        ones = hot(mine)
        counts = jnp.dot(ones, counter, preferred_element_type=F32)
        place = jnp.sum(jnp.where(mine, counts[:, :256] + seen, 0.0), axis=0, keepdims=True)
        place = place.astype(jnp.int32)
        rank[:, at] = place
        there = fit(CAP, place)
        values = [nrm[k : k + 1, at] for k in range(3)] + [cel[:, at].astype(F32)]
        pieces = [chop(v, 3) for v in values]
        for n in range(3):
            w = jnp.concatenate([jnp.where(there, p[n], 0.0) for p in pieces], axis=0).astype(BF16)
            d = lax.dot_general(ones, w, lanes, preferred_element_type=F32)
            box[0] += d[:, :128]
            box[1] += d[:, 128:]
        return seen + counts[:, 256:]

    lax.fori_loop(0, P_DEV // 256, dispatch, jnp.zeros((NB, 256), F32))

    copies = []
    for t in range(NI):
        k = bx_peer(bx, t)
        src, dst = box.at[:, pl.ds(al(k, 8), 8)], in1.at[:, pl.ds(al(bx, 8), 8)]
        if t:
            copies.append(remote(src, dst, ps.at[t], pr.at[t], (k, by)))
        else:
            copies.append(pltpu.make_async_copy(src, dst, ps.at[0]))
        copies[-1].start()
    for c in copies:
        c.wait()
    for j in range(NJ):
        for h in range(2):
            out2[j, h] = in1.at[h][pl.ds(j, NI, stride=NJ), :]
    copies = []
    for t in range(NJ):
        j = (by + t) % NJ
        if t:
            copies.append(remote(out2.at[j], in2.at[by], qs.at[t], qr.at[t], (bx, j)))
        else:
            copies.append(pltpu.make_async_copy(out2.at[j], in2.at[by], qs.at[0]))
        copies[-1].start()
    for c in copies:
        c.wait()

    for k in range(4):
        v = in2[:, k // 2].reshape(NB, 128)[:, CAP * (k % 2) : CAP * (k % 2 + 1)]
        v = jnp.concatenate([v[: NB // 2], v[NB // 2 :]], axis=1)
        v = jnp.concatenate([v[: NB // 4], v[NB // 4 :]], axis=1)
        if k < 3:
            part[2 * k], part[2 * k + 1] = chop(v, 2)
        else:
            slot[...] = v.astype(jnp.int32)

    @pl.loop(0, NB // 4)
    def _(c):
        cell = slot[pl.ds(c, 1), :]
        depth = fit(NZ, cell % NZ)
        weighted = jnp.concatenate(
            [
                jnp.concatenate(
                    [jnp.where(depth, part[2 * k + n, pl.ds(c, 1), :], 0.0).astype(BF16) for n in range(2)],
                    axis=1,
                )
                for k in range(3)
            ],
            axis=0,
        )
        for q in range(4):
            a = hot(fit(256, cell // NZ - 256 * q))
            d = lax.dot_general(
                jnp.concatenate([a, a], axis=1), weighted, lanes, preferred_element_type=F32
            ).reshape(4, CY, 3 * NZ)
            vx[pl.ds(1 + 4 * q, 4)] += d[:, :, :NZ]
            vy[pl.ds(4 * q, 4)] += d[:, :, NZ : 2 * NZ]
            vz[pl.ds(4 * q, 4)] += d[:, :, 2 * NZ :]

    down = remote(vx.at[1], vx.at[CX + 1], fs.at[0], fr.at[0], (jnp.maximum(bx - 1, 0), by))
    up = remote(vx.at[CX], vx.at[0], fs.at[1], fr.at[1], (jnp.minimum(bx + 1, NI - 1), by))
    for x in range(CX):
        fe[0, x : x + 1] = vy[x, 0:1]
        fe[1, x : x + 1] = vy[x, CY - 1 : CY]
    low = remote(fe.at[0], fh.at[0], fs.at[2], fr.at[2], (bx, below))
    high = remote(fe.at[1], fh.at[1], fs.at[3], fr.at[3], (bx, above))

    @pl.when(bx > 0)
    def _():
        down.start()

    @pl.when(bx < NI - 1)
    def _():
        up.start()

    @pl.when(by > 0)
    def _():
        low.start()

    @pl.when(by < NJ - 1)
    def _():
        high.start()

    @pl.when(by > 0)
    def _():
        low.wait_send()
        high.wait_recv()

    @pl.when(by < NJ - 1)
    def _():
        high.wait_send()
        low.wait_recv()

    @pl.when(bx > 0)
    def _():
        down.wait_send()
        up.wait_recv()

    @pl.when(bx < NI - 1)
    def _():
        up.wait_send()
        down.wait_recv()

    @pl.loop(0, CX)
    def _(x):
        zi = lax.broadcasted_iota(jnp.int32, (CY, NZ), 1)
        yi = lax.broadcasted_iota(jnp.int32, (CY, NZ), 0)
        b, c = vy[x], vz[x]
        total = vx[x + 2] - vx[x]
        total = total + jnp.where(yi == CY - 1, fh[0, pl.ds(x, 1), :], pltpu.roll(b, CY - 1, 0))
        total = total - jnp.where(yi == 0, fh[1, pl.ds(x, 1), :], pltpu.roll(b, 1, 0))
        total = total + jnp.where(zi == NZ - 1, 0.0, pltpu.roll(c, NZ - 1, 1))
        total = total - jnp.where(zi == 0, 0.0, pltpu.roll(c, 1, 1))
        r[x] = -0.5 * total

    diagonal = 6.0 + (1.0 + lev_ref[0, 0].astype(F32))

    def stencil(d, low, high):
        @pl.loop(0, CX)
        def _(x):
            c = d[x + 1]
            zi = lax.broadcasted_iota(jnp.int32, (CY, NZ), 1)
            yi = lax.broadcasted_iota(jnp.int32, (CY, NZ), 0)
            near = d[x] + d[x + 2]
            near = near + jnp.where(zi == 0, 0.0, pltpu.roll(c, 1, 1))
            near = near + jnp.where(zi == NZ - 1, 0.0, pltpu.roll(c, NZ - 1, 1))
            near = near + jnp.where(yi == 0, low(x), pltpu.roll(c, 1, 0))
            near = near + jnp.where(yi == CY - 1, high(x), pltpu.roll(c, CY - 1, 0))
            r[x] = r[x] - (diagonal * c - near)
            u_ref[x] = u_ref[x] + c

    def x_planes(d, send, recv):
        down = remote(d.at[1], d.at[CX + 1], send.at[0], recv.at[0], (jnp.maximum(bx - 1, 0), by))
        up = remote(d.at[CX], d.at[0], send.at[1], recv.at[1], (jnp.minimum(bx + 1, NI - 1), by))
        return down, up

    @pl.loop(0, ITERS)
    def _(it):
        copies = []
        for t in range(NI):
            k = bx_peer(bx, t)
            src = r.at[:, pl.ds(al(k // 2, 8), 8), pl.ds(al(k % 2, 128), 128)]
            dst = xin.at[it, pl.ds(bx * 16, 16)]
            if t:
                copies.append(remote(src, dst, xs.at[t], xr.at[t], (k, by)))
            else:
                copies.append(pltpu.make_async_copy(src, dst, xs.at[0]))
            copies[-1].start()
        for c in copies:
            c.wait()
        lines = xin.at[it].reshape(NI * CX * 8, 128)
        moved = dxp.reshape((NI * CX + 2) * 8, 128)
        for s in range(0, 8, 2):
            v = jnp.concatenate(
                [lines[pl.ds(s, 256, stride=8), :], lines[pl.ds(s + 1, 256, stride=8), :]], axis=1
            )
            d = dot3(mxs[0], mxs[1], *split(v))
            moved[pl.ds(8 + s, 256, stride=8), :] = d[:, :128]
            moved[pl.ds(9 + s, 256, stride=8), :] = d[:, 128:]
            if s == 0:
                edge[0] = d[:, :128]
            if s == 6:
                edge[1] = d[:, 128:]
        copies = []
        for t in range(NI):
            k = bx_peer(bx, t)
            src = dxp.at[pl.ds(k * 16, 18)]
            dst = dx.at[it, :, pl.ds(al(yg, 8), 8), pl.ds(al(zh, 128), 128)]
            if t:
                copies.append(remote(src, dst, bs.at[t], br.at[t], (k, by)))
            else:
                copies.append(pltpu.make_async_copy(src, dst, bs.at[0]))
            copies[-1].start()

        def edges(side, beside):
            out = []
            for t in range(NI):
                k = bx_peer(bx, t)
                out.append(
                    remote(
                        edge.at[side, pl.ds(al(k, 16), 16)],
                        yhx.at[it, side, :, pl.ds(al(zh, 128), 128)],
                        es.at[side, t],
                        er.at[side, zh],
                        (k, beside),
                    )
                )
            return out

        def half(side, z):
            return remote(
                edge.at[side, pl.ds(0, 16)], yhx.at[it, side, :, pl.ds(128 * z, 128)],
                es.at[side, 0], er.at[side, z], (bx, by),
            )

        @pl.when((yg == 0) & (by > 0))
        def _():
            for c in edges(0, below):
                c.start()

        @pl.when((yg == 7) & (by < NJ - 1))
        def _():
            for c in edges(1, above):
                c.start()

        for c in copies:
            c.wait()

        @pl.when((yg == 0) & (by > 0))
        def _():
            for c in edges(0, below):
                c.wait_send()

        @pl.when((yg == 7) & (by < NJ - 1))
        def _():
            for c in edges(1, above):
                c.wait_send()

        @pl.when(by < NJ - 1)
        def _():
            half(0, 0).wait_recv()
            half(0, 1).wait_recv()

        @pl.when(by > 0)
        def _():
            half(1, 0).wait_recv()
            half(1, 1).wait_recv()

        stencil(
            dx.at[it],
            lambda x: yhx[it, 1, pl.ds(x, 1), :],
            lambda x: yhx[it, 0, pl.ds(x, 1), :],
        )

        copies = []
        for t in range(NJ):
            j = (by + t) % NJ
            src = r.at[pl.ds(2 * j, 2)]
            dst = yin.at[it, :, pl.ds(al(by, 64), 64), :]
            if t:
                copies.append(remote(src, dst, ys.at[t], yr.at[t], (bx, j)))
            else:
                copies.append(pltpu.make_async_copy(src, dst, ys.at[0]))
            copies[-1].start()
        for c in copies:
            c.wait()
        for e in range(2):
            d = dot3(mys[0], mys[1], *split(yin[it, e]))
            dyl[e] = d
            for j in range(NJ):
                if j:
                    ye[j, e : e + 1] = d[64 * j - 1 : 64 * j]
                if j < NJ - 1:
                    ye[j, 2 + e : 3 + e] = d[64 * j + 64 : 64 * j + 65]
        copies = []
        for t in range(NJ):
            j = (by + t) % NJ
            main = (dyl.at[:, pl.ds(al(j, 64), 64), :], dy.at[it, pl.ds(1 + 2 * by, 2)])
            rows = (ye.at[j], yhy.at[it, by])
            if t:
                copies.append(remote(*main, cs.at[t], cr.at[by], (bx, j)))
                copies.append(remote(*rows, ns.at[t], nr.at[t], (bx, j)))
            else:
                copies.append(pltpu.make_async_copy(*main, cr.at[by]))
                copies.append(pltpu.make_async_copy(*rows, ns.at[0]))
            copies[-2].start()
            copies[-1].start()

        def arrived(m):
            remote(
                dyl.at[:, pl.ds(0, 64), :], dy.at[it, pl.ds(1 + 2 * m, 2)], cs.at[0], cr.at[m], (bx, by)
            ).wait_recv()

        down, up = x_planes(dy.at[it], hs, hr)
        arrived(0)

        @pl.when(bx > 0)
        def _():
            down.start()

        arrived(NJ - 1)

        @pl.when(bx < NI - 1)
        def _():
            up.start()

        for m in range(1, NJ - 1):
            arrived(m)
        for t in range(1, NJ):
            copies[2 * t].wait_send()
            copies[2 * t + 1].wait()
        copies[1].wait()

        @pl.when(bx > 0)
        def _():
            down.wait_send()
            up.wait_recv()

        @pl.when(bx < NI - 1)
        def _():
            up.wait_send()
            down.wait_recv()

        stencil(
            dy.at[it],
            lambda x: yhy[it, x // 2, pl.ds(x % 2, 1), :],
            lambda x: yhy[it, x // 2, pl.ds(2 + x % 2, 1), :],
        )


        def z_planes(x, n):
            v = r[pl.ds(x, n)].reshape(n * CY, NZ)
            d = dot3(*split(v), mzs[0], mzs[1], lanes)
            dz[it, pl.ds(x + 1, n)] = d.reshape(n, CY, NZ)

        z_planes(0, 1)
        z_planes(CX - 1, 1)
        down, up = x_planes(dz.at[it], zs, zr)
        more = it < ITERS - 1

        @pl.when(more & (bx > 0))
        def _():
            down.start()

        @pl.when(more & (bx < NI - 1))
        def _():
            up.start()

        for x in range(1, CX - 1, 2):
            z_planes(x, 2)

        @pl.when(more)
        def _():
            for x in range(CX):
                ze[0, x : x + 1] = dz[it, x + 1, 0:1]
                ze[1, x : x + 1] = dz[it, x + 1, CY - 1 : CY]
            low = remote(ze.at[0], yhz.at[it, 0], zs.at[2], zr.at[2], (bx, below))
            high = remote(ze.at[1], yhz.at[it, 1], zs.at[3], zr.at[3], (bx, above))

            @pl.when(by > 0)
            def _():
                low.start()

            @pl.when(by < NJ - 1)
            def _():
                high.start()

            @pl.when(by > 0)
            def _():
                low.wait_send()
                high.wait_recv()

            @pl.when(by < NJ - 1)
            def _():
                high.wait_send()
                low.wait_recv()

            @pl.when(bx > 0)
            def _():
                down.wait_send()
                up.wait_recv()

            @pl.when(bx < NI - 1)
            def _():
                up.wait_send()
                down.wait_recv()

            stencil(
                dz.at[it],
                lambda x: yhz[it, 1, pl.ds(x, 1), :],
                lambda x: yhz[it, 0, pl.ds(x, 1), :],
            )

        @pl.when(it == ITERS - 1)
        def _():
            u_ref[...] = u_ref[...] + dz[it, pl.ds(1, CX)]

    for q in range(4):
        block = jnp.transpose(u_ref[pl.ds(4 * q, 4)].reshape(256, NZ))
        for n, piece in enumerate(chop(block, 2)):
            ut[pl.ds(256 * n, 256), pl.ds(256 * q, 256)] = piece.astype(BF16)

    @pl.loop(0, NB // 4)
    def _(c):
        cell = slot[pl.ds(c, 1), :]
        a = hot(fit(CX * CY, cell // NZ))
        v = jnp.dot(ut[...], a, preferred_element_type=F32)
        v = jnp.where(fit(NZ, cell % NZ), v[:NZ] + v[NZ:], 0.0)
        smp[pl.ds(c, 1), :] = jnp.sum(v, axis=0, keepdims=True)

    v = smp[...]
    v = jnp.concatenate([v[:, : 2 * CAP], v[:, 2 * CAP :]], axis=0)
    v = jnp.concatenate([v[:, :CAP], v[:, CAP:]], axis=0)
    v = jnp.concatenate([v, jnp.zeros((NB, 128 - CAP), F32)], axis=1)
    back1[...] = v.reshape(NJ, NI, 128)

    copies = []
    for t in range(NJ):
        j = (by + t) % NJ
        src, dst = back1.at[j], got1.at[pl.ds(al(by, 16), 16)]
        if t:
            copies.append(remote(src, dst, gs.at[t], gr.at[t], (bx, j)))
        else:
            copies.append(pltpu.make_async_copy(src, dst, gs.at[0]))
        copies[-1].start()
    for c in copies:
        c.wait()
    for k in range(NI):
        back2[k] = got1[pl.ds(k, NJ, stride=NI), :]
    copies = []
    for t in range(NI):
        k = bx_peer(bx, t)
        src, dst = back2.at[k], got2.at[pl.ds(al(bx, 8), 8)]
        if t:
            copies.append(remote(src, dst, ks.at[t], kr.at[t], (k, by)))
        else:
            copies.append(pltpu.make_async_copy(src, dst, ks.at[0]))
        copies[-1].start()
    for c in copies:
        c.wait()
    found = [p.astype(BF16) for p in chop(jnp.transpose(got2[...])[:CAP], 3)]

    @pl.loop(0, P_DEV // 256)
    def _(c):
        at = pl.ds(al(c, 256), 256)
        ones = hot(fit(NB, own[:, at]))
        v = sum(jnp.dot(p, ones, preferred_element_type=F32) for p in found)
        imp_ref[:, at] = jnp.sum(jnp.where(fit(CAP, rank[:, at]), v, 0.0), axis=0, keepdims=True)


def local(normals, owners, cells, levels, rows, columns, depth):
    vm = pl.BlockSpec(memory_space=pltpu.VMEM)
    brick = (CX, CY, NZ)
    tall = (ITERS, CX + 2, CY, NZ)
    dma = pltpu.SemaphoreType.DMA
    iterate, implicit = pl.pallas_call(
        relax,
        name="relax",
        out_shape=(jax.ShapeDtypeStruct(brick, F32), jax.ShapeDtypeStruct((1, P_DEV), F32)),
        in_specs=[vm, vm, vm, pl.BlockSpec(memory_space=pltpu.SMEM), vm, vm, vm],
        out_specs=(vm, vm),
        scratch_shapes=[
            pltpu.VMEM(brick, F32),
            pltpu.VMEM((ITERS, NI * CX, 8, 128), F32),
            pltpu.VMEM((NI * CX + 2, 8, 128), F32),
            pltpu.VMEM(tall, F32),
            pltpu.VMEM((2, NI * CX, 128), F32),
            pltpu.VMEM((ITERS, 2, CX, NZ), F32),
            pltpu.VMEM((ITERS, 2, NJ * CY, NZ), F32),
            pltpu.VMEM((2, NJ * CY, NZ), F32),
            pltpu.VMEM(tall, F32),
            pltpu.VMEM((NJ, 8, NZ), F32),
            pltpu.VMEM((ITERS, NJ, 8, NZ), F32),
            pltpu.VMEM(tall, F32),
            pltpu.VMEM((2, CX, NZ), F32),
            pltpu.VMEM((ITERS, 2, CX, NZ), F32),
            pltpu.VMEM((2, 256, 256), BF16),
            pltpu.VMEM((2, 512, 512), BF16),
            pltpu.VMEM((2, 256, 256), BF16),
            pltpu.VMEM((2, NB, 128), F32),
            pltpu.VMEM((1, P_DEV), jnp.int32),
            pltpu.VMEM((2, NB, 128), F32),
            pltpu.VMEM((NJ, 2, NI, 128), F32),
            pltpu.VMEM((NJ, 2, NI, 128), F32),
            pltpu.VMEM((NB // 4, 256), jnp.int32),
            pltpu.VMEM((6, NB // 4, 256), F32),
            pltpu.VMEM((CX + 2, CY, NZ), F32),
            pltpu.VMEM(brick, F32),
            pltpu.VMEM(brick, F32),
            pltpu.VMEM((2, CX, NZ), F32),
            pltpu.VMEM((2, CX, NZ), F32),
            pltpu.VMEM((NB // 4, 256), F32),
            pltpu.VMEM((512, CX * CY), BF16),
            pltpu.VMEM((NJ, NI, 128), F32),
            pltpu.VMEM((NB, 128), F32),
            pltpu.VMEM((NI, NJ, 128), F32),
            pltpu.VMEM((NB, 128), F32),
            dma((NI,)), dma((NI,)), dma((NI,)), dma((NI,)),
            dma((2, NI)), dma((2, 2)),
            dma((NJ,)), dma((NJ,)), dma((NJ,)), dma((NJ,)), dma((NJ,)), dma((NJ,)),
            dma((2,)), dma((2,)), dma((4,)), dma((4,)),
            dma((NI,)), dma((NI,)), dma((NJ,)), dma((NJ,)), dma((4,)), dma((4,)),
            dma((NJ,)), dma((NJ,)), dma((NI,)), dma((NI,)),
        ],
        compiler_params=pltpu.CompilerParams(
            collective_id=0, has_side_effects=True, vmem_limit_bytes=52 << 20
        ),
    )(normals, owners.reshape(1, P_DEV), cells.reshape(1, P_DEV), levels, rows, columns, depth)
    return iterate, implicit.reshape(P_DEV)


def solution(mesh):
    placed = (
        P(None, ("bx", "by")),
        P(("bx", "by"), None),
        P(("bx", "by")),
        P("bx", "by"),
        P(),
        P(),
        P(),
    )
    return jax.shard_map(
        local,
        mesh=mesh,
        in_specs=placed,
        out_specs=(P("bx", "by", None), P(("bx", "by"))),
        check_vma=False,
    )
```

```python
import functools
import jax
import jax.numpy as jnp
from jax import lax
from jax.experimental import pallas as pl
from jax.experimental.pallas import tpu as pltpu
from jax.sharding import PartitionSpec as P

CX, CY, NZ, ITERS = 16, 64, 256, 4
NI, NJ = 16, 8
NB, P_DEV, CAP = 128, 4096, 64
MESH = pl.DeviceIdType.MESH
F32, BF16 = jnp.float32, jnp.bfloat16


def split(v):
    hi = v.astype(BF16)
    return hi, (v - hi.astype(F32)).astype(BF16)


def dot3(a_hi, a_lo, b_hi, b_lo, dims=(((1,), (0,)), ((), ()))):
    mul = functools.partial(lax.dot_general, dimension_numbers=dims, preferred_element_type=F32)
    return mul(a_hi, b_hi) + (mul(a_lo, b_hi) + mul(a_hi, b_lo))


def remote(src, dst, send, recv, device):
    return pltpu.make_async_remote_copy(
        src_ref=src, dst_ref=dst, send_sem=send, recv_sem=recv, device_id=device, device_id_type=MESH
    )


def bx_peer(bx, t):
    y, z = bx // 4, bx % 4
    return ((y + t // 4) % 4) * 4 + (z + t % 4) % 4


def al(v, m):
    return pl.multiple_of(v * m, m)


def greet(bx, by):
    barrier = pltpu.get_barrier_semaphore()
    count = 0
    for side in (0, 1, NJ - 1):
        for t in range(NI):
            if side == 0 and t == 0:
                continue
            pl.semaphore_signal(
                barrier, inc=1, device_id=(bx_peer(bx, t), (by + side) % NJ), device_id_type=MESH
            )
            count += 1
    for t in range(2, NJ - 1):
        pl.semaphore_signal(barrier, inc=1, device_id=(bx, (by + t) % NJ), device_id_type=MESH)
        count += 1
    return functools.partial(pl.semaphore_wait, barrier, count)


def relax(
    nrm, own, cel, lev_ref, mx_ref, my_ref, mz_ref, u_ref, imp_ref,
    r, xin, dxp, dx, edge, yhx, yin, dyl, dy, ye, yhy, dz, ze, yhz,
    mxv, myv, mzv, mxs, mys, mzs,
    box, rank, in1, out2, in2, slot, vx, vy, vz, fe, fh, ut, back1, got1, back2, got2,
    xs, xr, bs, br, es, er, ys, yr, cs, cr, ns, nr, hs, hr, zs, zr,
    ps, pr, qs, qr, fs, fr, gs, gr, ks, kr, ms,
):
    bx, by = lax.axis_index("bx"), lax.axis_index("by")
    yg, zh = bx // 2, bx % 2
    zero = jnp.zeros((8, 128), F32)
    dxp[0] = zero
    dxp[257] = zero
    for ref in (yhx, yhy, yhz):
        ref[...] = jnp.zeros(ref.shape, F32)
    ye[...] = jnp.zeros(ye.shape, F32)
    for it in range(ITERS):
        for ref in (dy, dz):
            ref[it, 0] = jnp.zeros((CY, NZ), F32)
            ref[it, CX + 1] = jnp.zeros((CY, NZ), F32)
    vx[0] = jnp.zeros((CY, NZ), F32)
    vx[CX + 1] = jnp.zeros((CY, NZ), F32)
    fh[...] = jnp.zeros(fh.shape, F32)
    back1[...] = jnp.zeros(back1.shape, F32)
    all_here = greet(bx, by)
    fetches = [
        pltpu.make_async_copy(m, v, ms.at[n])
        for n, (m, v) in enumerate(((mx_ref, mxv), (my_ref, myv), (mz_ref, mzv)))
    ]
    for c in fetches:
        c.start()
    vx[pl.ds(1, CX)] = jnp.zeros((CX, CY, NZ), F32)
    vy[...] = jnp.zeros(vy.shape, F32)
    vz[...] = jnp.zeros(vz.shape, F32)
    u_ref[...] = jnp.zeros(u_ref.shape, F32)
    below, above = jnp.maximum(by - 1, 0), jnp.minimum(by + 1, NJ - 1)
    lanes = (((1,), (1,)), ((), ()))

    def fit(rows, index):
        return lax.broadcasted_iota(jnp.int32, (rows, index.shape[1]), 0) == index

    def hot(mask):
        return jnp.where(mask, 1.0, 0.0).astype(BF16)

    def chop(v, n):
        pieces = []
        for _ in range(n):
            pieces.append(v.astype(BF16).astype(F32))
            v = v - pieces[-1]
        return pieces

    before = lax.broadcasted_iota(jnp.int32, (256, 256), 0) < lax.broadcasted_iota(jnp.int32, (256, 256), 1)
    counter = jnp.concatenate([hot(before), jnp.ones((256, 256), BF16)], axis=1)
    box[...] = jnp.zeros(box.shape, F32)

    def dispatch(c, seen):
        at = pl.ds(al(c, 256), 256)
        mine = fit(NB, own[:, at])
        ones = hot(mine)
        counts = jnp.dot(ones, counter, preferred_element_type=F32)
        place = jnp.sum(jnp.where(mine, counts[:, :256] + seen, 0.0), axis=0, keepdims=True)
        place = place.astype(jnp.int32)
        rank[:, at] = place
        there = fit(CAP, place)
        values = [nrm[k : k + 1, at] for k in range(3)] + [cel[:, at].astype(F32)]
        pieces = [chop(v, 3) for v in values]
        for n in range(3):
            w = jnp.concatenate([jnp.where(there, p[n], 0.0) for p in pieces], axis=0).astype(BF16)
            d = lax.dot_general(ones, w, lanes, preferred_element_type=F32)
            box[0] += d[:, :128]
            box[1] += d[:, 128:]
        return seen + counts[:, 256:]

    lax.fori_loop(0, P_DEV // 256, dispatch, jnp.zeros((NB, 256), F32))

    all_here()
    copies = []
    for t in range(NI):
        k = bx_peer(bx, t)
        src, dst = box.at[:, pl.ds(al(k, 8), 8)], in1.at[:, pl.ds(al(bx, 8), 8)]
        if t:
            copies.append(remote(src, dst, ps.at[t], pr.at[t], (k, by)))
        else:
            copies.append(pltpu.make_async_copy(src, dst, ps.at[0]))
        copies[-1].start()
    for c in copies:
        c.wait()
    for j in range(NJ):
        for h in range(2):
            out2[j, h] = in1.at[h][pl.ds(j, NI, stride=NJ), :]
    copies = []
    for t in range(NJ):
        j = (by + t) % NJ
        if t:
            copies.append(remote(out2.at[j], in2.at[by], qs.at[t], qr.at[t], (bx, j)))
        else:
            copies.append(pltpu.make_async_copy(out2.at[j], in2.at[by], qr.at[0]))
        copies[-1].start()
    for c, (v, vs) in zip(fetches, ((mxv, mxs), (myv, mys), (mzv, mzs))):
        c.wait()
        vs[0], vs[1] = split(v[...])

    @pl.loop(0, NJ)
    def _(t):
        j = (by + NJ - t) % NJ
        remote(out2.at[0], in2.at[j], qs.at[0], qr.at[t], (bx, by)).wait_recv()
        rows = []
        for k in range(4):
            v = in2[j, k // 2][:, CAP * (k % 2) : CAP * (k % 2 + 1)]
            rows.append(jnp.concatenate([v[i : i + 1] for i in range(NI)], axis=1))
        cell = rows[3].astype(jnp.int32)
        slot[pl.ds(j, 1), :] = cell
        depth = fit(NZ, cell % NZ)
        weighted = jnp.concatenate(
            [
                jnp.concatenate([jnp.where(depth, p, 0.0).astype(BF16) for p in chop(v, 2)], axis=1)
                for v in rows[:3]
            ],
            axis=0,
        )
        for q in range(4):
            a = hot(fit(256, cell // NZ - 256 * q))
            d = lax.dot_general(
                jnp.concatenate([a, a], axis=1), weighted, lanes, preferred_element_type=F32
            ).reshape(4, CY, 3 * NZ)
            vx[pl.ds(1 + 4 * q, 4)] += d[:, :, :NZ]
            vy[pl.ds(4 * q, 4)] += d[:, :, NZ : 2 * NZ]
            vz[pl.ds(4 * q, 4)] += d[:, :, 2 * NZ :]

    for c in copies[1:]:
        c.wait_send()

    down = remote(vx.at[1], vx.at[CX + 1], fs.at[0], fr.at[0], (jnp.maximum(bx - 1, 0), by))
    up = remote(vx.at[CX], vx.at[0], fs.at[1], fr.at[1], (jnp.minimum(bx + 1, NI - 1), by))
    for x in range(CX):
        fe[0, x : x + 1] = vy[x, 0:1]
        fe[1, x : x + 1] = vy[x, CY - 1 : CY]
    low = remote(fe.at[0], fh.at[0], fs.at[2], fr.at[2], (bx, below))
    high = remote(fe.at[1], fh.at[1], fs.at[3], fr.at[3], (bx, above))

    @pl.when(bx > 0)
    def _():
        down.start()

    @pl.when(bx < NI - 1)
    def _():
        up.start()

    @pl.when(by > 0)
    def _():
        low.start()

    @pl.when(by < NJ - 1)
    def _():
        high.start()

    @pl.when(by > 0)
    def _():
        low.wait_send()
        high.wait_recv()

    @pl.when(by < NJ - 1)
    def _():
        high.wait_send()
        low.wait_recv()

    @pl.when(bx > 0)
    def _():
        down.wait_send()
        up.wait_recv()

    @pl.when(bx < NI - 1)
    def _():
        up.wait_send()
        down.wait_recv()

    @pl.loop(0, CX)
    def _(x):
        zi = lax.broadcasted_iota(jnp.int32, (CY, NZ), 1)
        yi = lax.broadcasted_iota(jnp.int32, (CY, NZ), 0)
        b, c = vy[x], vz[x]
        total = vx[x + 2] - vx[x]
        total = total + jnp.where(yi == CY - 1, fh[0, pl.ds(x, 1), :], pltpu.roll(b, CY - 1, 0))
        total = total - jnp.where(yi == 0, fh[1, pl.ds(x, 1), :], pltpu.roll(b, 1, 0))
        total = total + jnp.where(zi == NZ - 1, 0.0, pltpu.roll(c, NZ - 1, 1))
        total = total - jnp.where(zi == 0, 0.0, pltpu.roll(c, 1, 1))
        r[x] = -0.5 * total

    diagonal = 6.0 + (1.0 + lev_ref[0, 0].astype(F32))

    def plane(d, x, low=None, high=None):
        c = d[x + 1]
        zi = lax.broadcasted_iota(jnp.int32, (CY, NZ), 1)
        yi = lax.broadcasted_iota(jnp.int32, (CY, NZ), 0)
        near = d[x] + d[x + 2]
        near = near + jnp.where(zi == 0, 0.0, pltpu.roll(c, 1, 1))
        near = near + jnp.where(zi == NZ - 1, 0.0, pltpu.roll(c, NZ - 1, 1))
        near = near + jnp.where(yi == 0, low(x) if low else 0.0, pltpu.roll(c, 1, 0))
        near = near + jnp.where(yi == CY - 1, high(x) if high else 0.0, pltpu.roll(c, CY - 1, 0))
        r[x] = r[x] - (diagonal * c - near)
        u_ref[x] = u_ref[x] + c

    def x_planes(d, send, recv):
        down = remote(d.at[1], d.at[CX + 1], send.at[0], recv.at[0], (jnp.maximum(bx - 1, 0), by))
        up = remote(d.at[CX], d.at[0], send.at[1], recv.at[1], (jnp.minimum(bx + 1, NI - 1), by))
        return down, up

    @pl.loop(0, ITERS)
    def _(it):
        copies = []
        for t in range(NI):
            k = bx_peer(bx, t)
            src = r.at[:, pl.ds(al(k // 2, 8), 8), pl.ds(al(k % 2, 128), 128)]
            dst = xin.at[it, pl.ds(bx * 16, 16)]
            if t:
                copies.append(remote(src, dst, xs.at[t], xr.at[t], (k, by)))
            else:
                copies.append(pltpu.make_async_copy(src, dst, xs.at[0]))
            copies[-1].start()
        for c in copies:
            c.wait()
        lines = xin.at[it].reshape(NI * CX * 8, 128)
        moved = dxp.reshape((NI * CX + 2) * 8, 128)
        for s in range(0, 8, 2):
            v = jnp.concatenate(
                [lines[pl.ds(s, 256, stride=8), :], lines[pl.ds(s + 1, 256, stride=8), :]], axis=1
            )
            d = dot3(mxs[0], mxs[1], *split(v))
            moved[pl.ds(8 + s, 256, stride=8), :] = d[:, :128]
            moved[pl.ds(9 + s, 256, stride=8), :] = d[:, 128:]
            if s == 0:
                edge[0] = d[:, :128]
            if s == 6:
                edge[1] = d[:, 128:]
        copies = []
        for t in range(NI):
            k = bx_peer(bx, t)
            src = dxp.at[pl.ds(k * 16, 18)]
            dst = dx.at[it, :, pl.ds(al(yg, 8), 8), pl.ds(al(zh, 128), 128)]
            if t:
                copies.append(remote(src, dst, bs.at[t], br.at[t], (k, by)))
            else:
                copies.append(pltpu.make_async_copy(src, dst, bs.at[0]))
            copies[-1].start()

        def edges(side, beside):
            out = []
            for t in range(NI):
                k = bx_peer(bx, t)
                out.append(
                    remote(
                        edge.at[side, pl.ds(al(k, 16), 16)],
                        yhx.at[it, side, :, pl.ds(al(zh, 128), 128)],
                        es.at[side, t],
                        er.at[side, zh],
                        (k, beside),
                    )
                )
            return out

        def half(side, z):
            return remote(
                edge.at[side, pl.ds(0, 16)], yhx.at[it, side, :, pl.ds(128 * z, 128)],
                es.at[side, 0], er.at[side, z], (bx, by),
            )

        @pl.when((yg == 0) & (by > 0))
        def _():
            for c in edges(0, below):
                c.start()

        @pl.when((yg == 7) & (by < NJ - 1))
        def _():
            for c in edges(1, above):
                c.start()

        for c in copies:
            c.wait()

        @pl.when((yg == 0) & (by > 0))
        def _():
            for c in edges(0, below):
                c.wait_send()

        @pl.when((yg == 7) & (by < NJ - 1))
        def _():
            for c in edges(1, above):
                c.wait_send()

        @pl.when(by < NJ - 1)
        def _():
            half(0, 0).wait_recv()
            half(0, 1).wait_recv()

        @pl.when(by > 0)
        def _():
            half(1, 0).wait_recv()
            half(1, 1).wait_recv()

        copies = []
        for t in [*range(1, NJ), 0]:
            j = (by + t) % NJ
            for e in range(2):
                plane(
                    dx.at[it],
                    2 * j + e,
                    lambda x: yhx[it, 1, pl.ds(x, 1), :],
                    lambda x: yhx[it, 0, pl.ds(x, 1), :],
                )
            src = r.at[pl.ds(2 * j, 2)]
            dst = yin.at[it, :, pl.ds(al(by, 64), 64), :]
            if t:
                copies.append(remote(src, dst, ys.at[t], yr.at[t], (bx, j)))
            else:
                copies.append(pltpu.make_async_copy(src, dst, ys.at[0]))
            copies[-1].start()
        for c in copies:
            c.wait()
        for e in range(2):
            d = dot3(mys[0], mys[1], *split(yin[it, e]))
            dyl[e] = d
            for j in range(NJ):
                if j:
                    ye[j, e : e + 1] = d[64 * j - 1 : 64 * j]
                if j < NJ - 1:
                    ye[j, 2 + e : 3 + e] = d[64 * j + 64 : 64 * j + 65]
        copies = []
        for t in range(NJ):
            j = (by + t) % NJ
            main = (dyl.at[:, pl.ds(al(j, 64), 64), :], dy.at[it, pl.ds(1 + 2 * by, 2)])
            rows = (ye.at[j], yhy.at[it, by])
            if t:
                copies.append(remote(*main, cs.at[t], cr.at[by], (bx, j)))
                copies.append(remote(*rows, ns.at[t], nr.at[t], (bx, j)))
            else:
                copies.append(pltpu.make_async_copy(*main, cr.at[by]))
                copies.append(pltpu.make_async_copy(*rows, ns.at[0]))
            copies[-2].start()
            copies[-1].start()

        def arrived(m):
            remote(
                dyl.at[:, pl.ds(0, 64), :], dy.at[it, pl.ds(1 + 2 * m, 2)], cs.at[0], cr.at[m], (bx, by)
            ).wait_recv()

        down, up = x_planes(dy.at[it], hs, hr)
        arrived(0)

        @pl.when(bx > 0)
        def _():
            down.start()

        arrived(NJ - 1)

        @pl.when(bx < NI - 1)
        def _():
            up.start()

        for m in range(1, NJ - 1):
            arrived(m)
        for t in range(1, NJ):
            copies[2 * t].wait_send()
            copies[2 * t + 1].wait()
        copies[1].wait()

        rows = (lambda x: yhy[it, x // 2, pl.ds(x % 2, 1), :], lambda x: yhy[it, x // 2, pl.ds(2 + x % 2, 1), :])

        @pl.loop(1, CX - 1)
        def _(x):
            plane(dy.at[it], x, *rows)

        @pl.when(bx > 0)
        def _():
            down.wait_send()
            up.wait_recv()

        @pl.when(bx < NI - 1)
        def _():
            up.wait_send()
            down.wait_recv()

        for x in (0, CX - 1):
            plane(dy.at[it], x, *rows)

        def z_planes(x, n):
            v = r[pl.ds(x, n)].reshape(n * CY, NZ)
            d = dot3(*split(v), mzs[0], mzs[1], lanes)
            dz[it, pl.ds(x + 1, n)] = d.reshape(n, CY, NZ)

        z_planes(0, 1)
        z_planes(CX - 1, 1)
        down, up = x_planes(dz.at[it], zs, zr)
        low = remote(ze.at[0], yhz.at[it, 0], zs.at[2], zr.at[2], (bx, below))
        high = remote(ze.at[1], yhz.at[it, 1], zs.at[3], zr.at[3], (bx, above))
        more = it < ITERS - 1

        @pl.when(more & (bx > 0))
        def _():
            down.start()

        @pl.when(more & (bx < NI - 1))
        def _():
            up.start()

        outer = jnp.concatenate(
            [r[x, y : y + 1, :] for y in (0, CY - 1) for x in range(CX)], axis=0
        )
        outer = dot3(*split(outer), mzs[0], mzs[1], lanes)
        ze[0] = outer[:CX]
        ze[1] = outer[CX:]

        @pl.when(more & (by > 0))
        def _():
            low.start()

        @pl.when(more & (by < NJ - 1))
        def _():
            high.start()

        for x in range(1, CX - 1, 2):
            z_planes(x, 2)

        @pl.when(more)
        def _():
            @pl.loop(1, CX - 1)
            def _(x):
                plane(dz.at[it], x)

            @pl.when(bx > 0)
            def _():
                down.wait_send()
                up.wait_recv()

            @pl.when(bx < NI - 1)
            def _():
                up.wait_send()
                down.wait_recv()

            for x in (0, CX - 1):
                plane(dz.at[it], x)

            @pl.when(by > 0)
            def _():
                low.wait_send()
                high.wait_recv()

            @pl.when(by < NJ - 1)
            def _():
                high.wait_send()
                low.wait_recv()

            for x in range(CX):
                r[x, 0:1] += yhz[it, 1, x : x + 1, :]
                r[x, CY - 1 : CY] += yhz[it, 0, x : x + 1, :]

        @pl.when(it == ITERS - 1)
        def _():
            u_ref[...] = u_ref[...] + dz[it, pl.ds(1, CX)]

    for q in range(4):
        block = jnp.transpose(u_ref[pl.ds(4 * q, 4)].reshape(256, NZ))
        for n, piece in enumerate(chop(block, 2)):
            ut[pl.ds(256 * n, 256), pl.ds(256 * q, 256)] = piece.astype(BF16)

    def returned(j, t):
        return remote(back1.at[j], got1.at[pl.ds(al(by, 16), 16)], gs.at[t], gr.at[t], (bx, j))

    def sampled(t):
        j = (by + t) % NJ
        cell = slot[pl.ds(j, 1), :]
        a = hot(fit(CX * CY, cell // NZ))
        v = jnp.dot(ut[...], a, preferred_element_type=F32)
        v = jnp.where(fit(NZ, cell % NZ), v[:NZ] + v[NZ:], 0.0)
        v = jnp.sum(v, axis=0, keepdims=True)
        for i in range(NI):
            back1[j, i : i + 1, :CAP] = v[:, CAP * i : CAP * (i + 1)]

    @pl.loop(1, NJ)
    def _(t):
        sampled(t)
        returned((by + t) % NJ, t).start()

    sampled(0)
    mine = pltpu.make_async_copy(back1.at[by], got1.at[pl.ds(al(by, 16), 16)], gs.at[0])
    mine.start()
    for t in range(1, NJ):
        returned((by + t) % NJ, t).wait()
    mine.wait()
    for k in range(NI):
        back2[k] = got1[pl.ds(k, NJ, stride=NI), :]
    copies = []
    for t in range(NI):
        k = bx_peer(bx, t)
        src, dst = back2.at[k], got2.at[pl.ds(al(bx, 8), 8)]
        if t:
            copies.append(remote(src, dst, ks.at[t], kr.at[t], (k, by)))
        else:
            copies.append(pltpu.make_async_copy(src, dst, ks.at[0]))
        copies[-1].start()
    for c in copies:
        c.wait()
    found = [p.astype(BF16) for p in chop(jnp.transpose(got2[...])[:CAP], 3)]

    @pl.loop(0, P_DEV // 256)
    def _(c):
        at = pl.ds(al(c, 256), 256)
        ones = hot(fit(NB, own[:, at]))
        v = sum(jnp.dot(p, ones, preferred_element_type=F32) for p in found)
        imp_ref[:, at] = jnp.sum(jnp.where(fit(CAP, rank[:, at]), v, 0.0), axis=0, keepdims=True)


def local(normals, owners, cells, levels, rows, columns, depth):
    vm = pl.BlockSpec(memory_space=pltpu.VMEM)
    hb = pl.BlockSpec(memory_space=pl.ANY)
    brick = (CX, CY, NZ)
    tall = (ITERS, CX + 2, CY, NZ)
    dma = pltpu.SemaphoreType.DMA
    iterate, implicit = pl.pallas_call(
        relax,
        name="relax",
        out_shape=(jax.ShapeDtypeStruct(brick, F32), jax.ShapeDtypeStruct((1, P_DEV), F32)),
        in_specs=[vm, vm, vm, pl.BlockSpec(memory_space=pltpu.SMEM), hb, hb, hb],
        out_specs=(vm, vm),
        scratch_shapes=[
            pltpu.VMEM(brick, F32),
            pltpu.VMEM((ITERS, NI * CX, 8, 128), F32),
            pltpu.VMEM((NI * CX + 2, 8, 128), F32),
            pltpu.VMEM(tall, F32),
            pltpu.VMEM((2, NI * CX, 128), F32),
            pltpu.VMEM((ITERS, 2, CX, NZ), F32),
            pltpu.VMEM((ITERS, 2, NJ * CY, NZ), F32),
            pltpu.VMEM((2, NJ * CY, NZ), F32),
            pltpu.VMEM(tall, F32),
            pltpu.VMEM((NJ, 8, NZ), F32),
            pltpu.VMEM((ITERS, NJ, 8, NZ), F32),
            pltpu.VMEM(tall, F32),
            pltpu.VMEM((2, CX, NZ), F32),
            pltpu.VMEM((ITERS, 2, CX, NZ), F32),
            pltpu.VMEM((256, 256), F32),
            pltpu.VMEM((512, 512), F32),
            pltpu.VMEM((256, 256), F32),
            pltpu.VMEM((2, 256, 256), BF16),
            pltpu.VMEM((2, 512, 512), BF16),
            pltpu.VMEM((2, 256, 256), BF16),
            pltpu.VMEM((2, NB, 128), F32),
            pltpu.VMEM((1, P_DEV), jnp.int32),
            pltpu.VMEM((2, NB, 128), F32),
            pltpu.VMEM((NJ, 2, NI, 128), F32),
            pltpu.VMEM((NJ, 2, NI, 128), F32),
            pltpu.VMEM((NJ, NI * CAP), jnp.int32),
            pltpu.VMEM((CX + 2, CY, NZ), F32),
            pltpu.VMEM(brick, F32),
            pltpu.VMEM(brick, F32),
            pltpu.VMEM((2, CX, NZ), F32),
            pltpu.VMEM((2, CX, NZ), F32),
            pltpu.VMEM((512, CX * CY), BF16),
            pltpu.VMEM((NJ, NI, 128), F32),
            pltpu.VMEM((NB, 128), F32),
            pltpu.VMEM((NI, NJ, 128), F32),
            pltpu.VMEM((NB, 128), F32),
            dma((NI,)), dma((NI,)), dma((NI,)), dma((NI,)),
            dma((2, NI)), dma((2, 2)),
            dma((NJ,)), dma((NJ,)), dma((NJ,)), dma((NJ,)), dma((NJ,)), dma((NJ,)),
            dma((2,)), dma((2,)), dma((4,)), dma((4,)),
            dma((NI,)), dma((NI,)), dma((NJ,)), dma((NJ,)), dma((4,)), dma((4,)),
            dma((NJ,)), dma((NJ,)), dma((NI,)), dma((NI,)), dma((3,)),
        ],
        compiler_params=pltpu.CompilerParams(
            collective_id=0, has_side_effects=True, vmem_limit_bytes=52 << 20
        ),
    )(normals, owners.reshape(1, P_DEV), cells.reshape(1, P_DEV), levels, rows, columns, depth)
    return iterate, implicit.reshape(P_DEV)


def solution(mesh):
    placed = (
        P(None, ("bx", "by")),
        P(("bx", "by"), None),
        P(("bx", "by")),
        P("bx", "by"),
        P(),
        P(),
        P(),
    )
    return jax.shard_map(
        local,
        mesh=mesh,
        in_specs=placed,
        out_specs=(P("bx", "by", None), P(("bx", "by"))),
        check_vma=False,
    )
```

```python
import functools
import jax
import jax.numpy as jnp
from jax import lax
from jax.experimental import pallas as pl
from jax.experimental.pallas import tpu as pltpu
from jax.sharding import PartitionSpec as P

CX, CY, NZ, ITERS = 16, 64, 256, 4
NI, NJ = 16, 8
NB, P_DEV, CAP = 128, 4096, 64
MESH = pl.DeviceIdType.MESH
F32, BF16 = jnp.float32, jnp.bfloat16


def split(v):
    hi = v.astype(BF16)
    return hi, (v - hi.astype(F32)).astype(BF16)


def dot3(a_hi, a_lo, b_hi, b_lo, dims=(((1,), (0,)), ((), ()))):
    mul = functools.partial(lax.dot_general, dimension_numbers=dims, preferred_element_type=F32)
    return mul(a_hi, b_hi) + (mul(a_lo, b_hi) + mul(a_hi, b_lo))


def remote(src, dst, send, recv, device):
    return pltpu.make_async_remote_copy(
        src_ref=src, dst_ref=dst, send_sem=send, recv_sem=recv, device_id=device, device_id_type=MESH
    )


def bx_peer(bx, t):
    y, z = bx // 4, bx % 4
    return ((y + t // 4) % 4) * 4 + (z + t % 4) % 4


BX_ORDER = (5, 10, 15, 1, 6, 11, 12, 2, 7, 8, 13, 3, 4, 9, 14, 0)


def al(v, m):
    return pl.multiple_of(v * m, m)


def greet(bx, by):
    barrier = pltpu.get_barrier_semaphore()
    count = 0
    for side in (0, 1, NJ - 1):
        for t in range(NI):
            if side == 0 and t == 0:
                continue
            pl.semaphore_signal(
                barrier, inc=1, device_id=(bx_peer(bx, t), (by + side) % NJ), device_id_type=MESH
            )
            count += 1
    for t in range(2, NJ - 1):
        pl.semaphore_signal(barrier, inc=1, device_id=(bx, (by + t) % NJ), device_id_type=MESH)
        count += 1
    return functools.partial(pl.semaphore_wait, barrier, count)


def relax(
    nrm, own, cel, lev_ref, mx_ref, my_ref, mz_ref, u_ref, imp_ref,
    r, xin, dxp, dx, edge, yhx, yin, dyl, dy, ye, yhy, dz, ze, yhz,
    mxv, myv, mzv, mxs, mys, mzs,
    box, rank, in1, out2, in2, slot, vx, vy, vz, fe, fh, ut, back1, got1, back2, got2,
    xs, xr, bs, br, es, er, ys, yr, cs, cr, ns, nr, hs, hr, zs, zr,
    ps, pr, qs, qr, fs, fr, gs, gr, ks, kr, ms,
):
    bx, by = lax.axis_index("bx"), lax.axis_index("by")
    yg, zh = bx // 2, bx % 2
    zero = jnp.zeros((8, 128), F32)
    dxp[0] = zero
    dxp[257] = zero
    for ref in (yhx, yhy, yhz):
        ref[...] = jnp.zeros(ref.shape, F32)
    ye[...] = jnp.zeros(ye.shape, F32)
    for it in range(ITERS):
        for ref in (dy, dz):
            ref[it, 0] = jnp.zeros((CY, NZ), F32)
            ref[it, CX + 1] = jnp.zeros((CY, NZ), F32)
    vx[0] = jnp.zeros((CY, NZ), F32)
    vx[CX + 1] = jnp.zeros((CY, NZ), F32)
    fh[...] = jnp.zeros(fh.shape, F32)
    back1[...] = jnp.zeros(back1.shape, F32)
    all_here = greet(bx, by)
    fetches = [
        pltpu.make_async_copy(m, v, ms.at[n])
        for n, (m, v) in enumerate(((mx_ref, mxv), (my_ref, myv), (mz_ref, mzv)))
    ]
    for c in fetches:
        c.start()
    vx[pl.ds(1, CX)] = jnp.zeros((CX, CY, NZ), F32)
    vy[...] = jnp.zeros(vy.shape, F32)
    vz[...] = jnp.zeros(vz.shape, F32)
    u_ref[...] = jnp.zeros(u_ref.shape, F32)
    below, above = jnp.maximum(by - 1, 0), jnp.minimum(by + 1, NJ - 1)
    lanes = (((1,), (1,)), ((), ()))

    def fit(rows, index):
        return lax.broadcasted_iota(jnp.int32, (rows, index.shape[1]), 0) == index

    def hot(mask):
        return jnp.where(mask, 1.0, 0.0).astype(BF16)

    def chop(v, n):
        pieces = []
        for _ in range(n):
            pieces.append(v.astype(BF16).astype(F32))
            v = v - pieces[-1]
        return pieces

    before = lax.broadcasted_iota(jnp.int32, (256, 256), 0) < lax.broadcasted_iota(jnp.int32, (256, 256), 1)
    counter = jnp.concatenate([hot(before), jnp.ones((256, 256), BF16)], axis=1)
    box[...] = jnp.zeros(box.shape, F32)

    def dispatch(c, seen):
        at = pl.ds(al(c, 256), 256)
        mine = fit(NB, own[:, at])
        ones = hot(mine)
        counts = jnp.dot(ones, counter, preferred_element_type=F32)
        place = jnp.sum(jnp.where(mine, counts[:, :256] + seen, 0.0), axis=0, keepdims=True)
        place = place.astype(jnp.int32)
        rank[:, at] = place
        there = fit(CAP, place)
        values = [nrm[k : k + 1, at] for k in range(3)] + [cel[:, at].astype(F32)]
        pieces = [chop(v, 3) for v in values]
        for n in range(3):
            w = jnp.concatenate([jnp.where(there, p[n], 0.0) for p in pieces], axis=0).astype(BF16)
            d = lax.dot_general(ones, w, lanes, preferred_element_type=F32)
            box[0] += d[:, :128]
            box[1] += d[:, 128:]
        return seen + counts[:, 256:]

    lax.fori_loop(0, P_DEV // 256, dispatch, jnp.zeros((NB, 256), F32))

    all_here()
    copies = []
    for t in range(NI):
        k = bx_peer(bx, t)
        src, dst = box.at[:, pl.ds(al(k, 8), 8)], in1.at[:, pl.ds(al(bx, 8), 8)]
        if t:
            copies.append(remote(src, dst, ps.at[t], pr.at[t], (k, by)))
        else:
            copies.append(pltpu.make_async_copy(src, dst, ps.at[0]))
        copies[-1].start()
    for c in copies:
        c.wait()
    for j in range(NJ):
        for h in range(2):
            out2[j, h] = in1.at[h][pl.ds(j, NI, stride=NJ), :]
    copies = []
    for t in range(NJ):
        j = (by + t) % NJ
        if t:
            copies.append(remote(out2.at[j], in2.at[by], qs.at[t], qr.at[t], (bx, j)))
        else:
            copies.append(pltpu.make_async_copy(out2.at[j], in2.at[by], qr.at[0]))
        copies[-1].start()
    for c, (v, vs) in zip(fetches, ((mxv, mxs), (myv, mys), (mzv, mzs))):
        c.wait()
        vs[0], vs[1] = split(v[...])

    @pl.loop(0, NJ)
    def _(t):
        j = (by + NJ - t) % NJ
        remote(out2.at[0], in2.at[j], qs.at[0], qr.at[t], (bx, by)).wait_recv()
        rows = []
        for k in range(4):
            v = in2[j, k // 2][:, CAP * (k % 2) : CAP * (k % 2 + 1)]
            rows.append(jnp.concatenate([v[i : i + 1] for i in range(NI)], axis=1))
        cell = rows[3].astype(jnp.int32)
        slot[pl.ds(j, 1), :] = cell
        depth = fit(NZ, cell % NZ)
        weighted = jnp.concatenate(
            [
                jnp.concatenate([jnp.where(depth, p, 0.0).astype(BF16) for p in chop(v, 2)], axis=1)
                for v in rows[:3]
            ],
            axis=0,
        )
        for q in range(4):
            a = hot(fit(256, cell // NZ - 256 * q))
            d = lax.dot_general(
                jnp.concatenate([a, a], axis=1), weighted, lanes, preferred_element_type=F32
            ).reshape(4, CY, 3 * NZ)
            vx[pl.ds(1 + 4 * q, 4)] += d[:, :, :NZ]
            vy[pl.ds(4 * q, 4)] += d[:, :, NZ : 2 * NZ]
            vz[pl.ds(4 * q, 4)] += d[:, :, 2 * NZ :]

    for c in copies[1:]:
        c.wait_send()

    down = remote(vx.at[1], vx.at[CX + 1], fs.at[0], fr.at[0], (jnp.maximum(bx - 1, 0), by))
    up = remote(vx.at[CX], vx.at[0], fs.at[1], fr.at[1], (jnp.minimum(bx + 1, NI - 1), by))
    for x in range(CX):
        fe[0, x : x + 1] = vy[x, 0:1]
        fe[1, x : x + 1] = vy[x, CY - 1 : CY]
    low = remote(fe.at[0], fh.at[0], fs.at[2], fr.at[2], (bx, below))
    high = remote(fe.at[1], fh.at[1], fs.at[3], fr.at[3], (bx, above))

    @pl.when(bx > 0)
    def _():
        down.start()

    @pl.when(bx < NI - 1)
    def _():
        up.start()

    @pl.when(by > 0)
    def _():
        low.start()

    @pl.when(by < NJ - 1)
    def _():
        high.start()

    @pl.when(by > 0)
    def _():
        low.wait_send()
        high.wait_recv()

    @pl.when(by < NJ - 1)
    def _():
        high.wait_send()
        low.wait_recv()

    @pl.when(bx > 0)
    def _():
        down.wait_send()
        up.wait_recv()

    @pl.when(bx < NI - 1)
    def _():
        up.wait_send()
        down.wait_recv()

    @pl.loop(0, CX)
    def _(x):
        zi = lax.broadcasted_iota(jnp.int32, (CY, NZ), 1)
        yi = lax.broadcasted_iota(jnp.int32, (CY, NZ), 0)
        b, c = vy[x], vz[x]
        total = vx[x + 2] - vx[x]
        total = total + jnp.where(yi == CY - 1, fh[0, pl.ds(x, 1), :], pltpu.roll(b, CY - 1, 0))
        total = total - jnp.where(yi == 0, fh[1, pl.ds(x, 1), :], pltpu.roll(b, 1, 0))
        total = total + jnp.where(zi == NZ - 1, 0.0, pltpu.roll(c, NZ - 1, 1))
        total = total - jnp.where(zi == 0, 0.0, pltpu.roll(c, 1, 1))
        r[x] = -0.5 * total

    diagonal = 6.0 + (1.0 + lev_ref[0, 0].astype(F32))

    def plane(d, x, low=None, high=None):
        c = d[x + 1]
        zi = lax.broadcasted_iota(jnp.int32, (CY, NZ), 1)
        yi = lax.broadcasted_iota(jnp.int32, (CY, NZ), 0)
        near = d[x] + d[x + 2]
        near = near + jnp.where(zi == 0, 0.0, pltpu.roll(c, 1, 1))
        near = near + jnp.where(zi == NZ - 1, 0.0, pltpu.roll(c, NZ - 1, 1))
        near = near + jnp.where(yi == 0, low(x) if low else 0.0, pltpu.roll(c, 1, 0))
        near = near + jnp.where(yi == CY - 1, high(x) if high else 0.0, pltpu.roll(c, CY - 1, 0))
        r[x] = r[x] - (diagonal * c - near)
        u_ref[x] = u_ref[x] + c

    def x_planes(d, send, recv):
        down = remote(d.at[1], d.at[CX + 1], send.at[0], recv.at[0], (jnp.maximum(bx - 1, 0), by))
        up = remote(d.at[CX], d.at[0], send.at[1], recv.at[1], (jnp.minimum(bx + 1, NI - 1), by))
        return down, up

    @pl.loop(0, ITERS)
    def _(it):
        there = []
        for h in range(2):
            for t in BX_ORDER:
                k = bx_peer(bx, t)
                src = r.at[:, pl.ds(al(2 * (k // 2) + h, 4), 4), pl.ds(al(k % 2, 128), 128)]
                dst = xin.at[it, pl.ds(bx * 16, 16), pl.ds(4 * h, 4)]
                if t:
                    there.append(remote(src, dst, xs.at[h, t], xr.at[h, t], (k, by)))
                else:
                    there.append(pltpu.make_async_copy(src, dst, xs.at[h, 0]))
                there[-1].start()
        lines = xin.at[it].reshape(NI * CX * 8, 128)
        moved = dxp.reshape((NI * CX + 2) * 8, 128)
        copies = []

        def edges(side, beside):
            out = []
            for t in range(NI):
                k = bx_peer(bx, t)
                out.append(
                    remote(
                        edge.at[side, pl.ds(al(k, 16), 16)],
                        yhx.at[it, side, :, pl.ds(al(zh, 128), 128)],
                        es.at[side, t],
                        er.at[side, zh],
                        (k, beside),
                    )
                )
            return out

        def half(side, z):
            return remote(
                edge.at[side, pl.ds(0, 16)], yhx.at[it, side, :, pl.ds(128 * z, 128)],
                es.at[side, 0], er.at[side, z], (bx, by),
            )

        for h in range(2):
            for c in there[NI * h : NI * (h + 1)]:
                c.wait()
            for y in range(4 * h, 4 * h + 4, 2):
                v = jnp.concatenate([lines[pl.ds(y + n, 256, stride=8), :] for n in range(2)], axis=1)
                d = dot3(mxs[0], mxs[1], *split(v))
                moved[pl.ds(8 + y, 256, stride=8), :] = d[:, :128]
                moved[pl.ds(9 + y, 256, stride=8), :] = d[:, 128:]
                if y == 0:
                    edge[0] = d[:, :128]
                if y == 6:
                    edge[1] = d[:, 128:]
            for t in BX_ORDER:
                k = bx_peer(bx, t)
                src = dxp.at[pl.ds(k * 16, 18), pl.ds(4 * h, 4)]
                dst = dx.at[it, :, pl.ds(al(2 * yg + h, 4), 4), pl.ds(al(zh, 128), 128)]
                if t:
                    copies.append(remote(src, dst, bs.at[h, t], br.at[h, t], (k, by)))
                else:
                    copies.append(pltpu.make_async_copy(src, dst, bs.at[h, 0]))
                copies[-1].start()

            if h == 0:

                @pl.when((yg == 0) & (by > 0))
                def _():
                    for c in edges(0, below):
                        c.start()

            else:

                @pl.when((yg == 7) & (by < NJ - 1))
                def _():
                    for c in edges(1, above):
                        c.start()

        for c in copies:
            c.wait()

        @pl.when((yg == 0) & (by > 0))
        def _():
            for c in edges(0, below):
                c.wait_send()

        @pl.when((yg == 7) & (by < NJ - 1))
        def _():
            for c in edges(1, above):
                c.wait_send()

        @pl.when(by < NJ - 1)
        def _():
            half(0, 0).wait_recv()
            half(0, 1).wait_recv()

        @pl.when(by > 0)
        def _():
            half(1, 0).wait_recv()
            half(1, 1).wait_recv()

        def there(j, t, h):
            src = r.at[pl.ds(2 * j, 2), :, pl.ds(128 * h, 128)]
            dst = yin.at[it, h, :, pl.ds(al(by, 64), 64), :]
            if t:
                return remote(src, dst, ys.at[h, t], yr.at[h, t], (bx, j))
            return pltpu.make_async_copy(src, dst, ys.at[h, 0])

        copies = []
        for t in [*range(1, NJ), 0]:
            j = (by + t) % NJ
            for e in range(2):
                plane(
                    dx.at[it],
                    2 * j + e,
                    lambda x: yhx[it, 1, pl.ds(x, 1), :],
                    lambda x: yhx[it, 0, pl.ds(x, 1), :],
                )
            copies.append(there(j, t, 0))
            copies[-1].start()
        for t in [*range(1, NJ), 0]:
            copies.append(there((by + t) % NJ, t, 1))
            copies[-1].start()
        for h in range(2):
            for c in copies[NJ * h : NJ * (h + 1)]:
                c.wait()
            d = dot3(mys[0], mys[1], *split(jnp.concatenate([yin[it, h, 0], yin[it, h, 1]], axis=1)))
            for e in range(2):
                part = d[:, 128 * e : 128 * (e + 1)]
                dyl[h, e] = part
                for j in range(NJ):
                    if j:
                        ye[h, j, e : e + 1] = part[64 * j - 1 : 64 * j]
                    if j < NJ - 1:
                        ye[h, j, 2 + e : 3 + e] = part[64 * j + 64 : 64 * j + 65]
            for t in [*range(1, NJ), 0]:
                j = (by + t) % NJ
                half_z = pl.ds(128 * h, 128)
                main = (dyl.at[h, :, pl.ds(al(j, 64), 64), :], dy.at[it, pl.ds(1 + 2 * by, 2), :, half_z])
                rows = (ye.at[h, j], yhy.at[it, by, :, half_z])
                if t:
                    copies.append(remote(*main, cs.at[h, t], cr.at[h, by], (bx, j)))
                    copies.append(remote(*rows, ns.at[h, t], nr.at[h, t], (bx, j)))
                else:
                    copies.append(pltpu.make_async_copy(*main, cr.at[h, by]))
                    copies.append(pltpu.make_async_copy(*rows, ns.at[h, 0]))
                copies[-2].start()
                copies[-1].start()

        def arrived(m):
            for h in range(2):
                remote(
                    dyl.at[h, :, pl.ds(0, 64), :],
                    dy.at[it, pl.ds(1 + 2 * m, 2), :, pl.ds(128 * h, 128)],
                    cs.at[h, 0], cr.at[h, m], (bx, by),
                ).wait_recv()

        down, up = x_planes(dy.at[it], hs, hr)
        arrived(0)

        @pl.when(bx > 0)
        def _():
            down.start()

        arrived(NJ - 1)

        @pl.when(bx < NI - 1)
        def _():
            up.start()

        for m in range(1, NJ - 1):
            arrived(m)
        for h in range(2):
            back = copies[2 * NJ * (h + 1) : 2 * NJ * (h + 2)]
            for t in range(NJ - 1):
                back[2 * t].wait_send()
                back[2 * t + 1].wait()
            back[-1].wait()

        rows = (lambda x: yhy[it, x // 2, pl.ds(x % 2, 1), :], lambda x: yhy[it, x // 2, pl.ds(2 + x % 2, 1), :])

        @pl.loop(1, CX - 1)
        def _(x):
            plane(dy.at[it], x, *rows)

        @pl.when(bx > 0)
        def _():
            down.wait_send()
            up.wait_recv()

        @pl.when(bx < NI - 1)
        def _():
            up.wait_send()
            down.wait_recv()

        for x in (0, CX - 1):
            plane(dy.at[it], x, *rows)

        def z_planes(x, n):
            v = r[pl.ds(x, n)].reshape(n * CY, NZ)
            d = dot3(*split(v), mzs[0], mzs[1], lanes)
            dz[it, pl.ds(x + 1, n)] = d.reshape(n, CY, NZ)

        z_planes(0, 1)
        z_planes(CX - 1, 1)
        down, up = x_planes(dz.at[it], zs, zr)
        low = remote(ze.at[0], yhz.at[it, 0], zs.at[2], zr.at[2], (bx, below))
        high = remote(ze.at[1], yhz.at[it, 1], zs.at[3], zr.at[3], (bx, above))
        more = it < ITERS - 1

        @pl.when(more & (bx > 0))
        def _():
            down.start()

        @pl.when(more & (bx < NI - 1))
        def _():
            up.start()

        outer = jnp.concatenate(
            [r[x, y : y + 1, :] for y in (0, CY - 1) for x in range(CX)], axis=0
        )
        outer = dot3(*split(outer), mzs[0], mzs[1], lanes)
        ze[0] = outer[:CX]
        ze[1] = outer[CX:]

        @pl.when(more & (by > 0))
        def _():
            low.start()

        @pl.when(more & (by < NJ - 1))
        def _():
            high.start()

        for x in range(1, CX - 1, 2):
            z_planes(x, 2)

        @pl.when(more)
        def _():
            @pl.loop(1, CX - 1)
            def _(x):
                plane(dz.at[it], x)

            @pl.when(bx > 0)
            def _():
                down.wait_send()
                up.wait_recv()

            @pl.when(bx < NI - 1)
            def _():
                up.wait_send()
                down.wait_recv()

            for x in (0, CX - 1):
                plane(dz.at[it], x)

            @pl.when(by > 0)
            def _():
                low.wait_send()
                high.wait_recv()

            @pl.when(by < NJ - 1)
            def _():
                high.wait_send()
                low.wait_recv()

            for x in range(CX):
                r[x, 0:1] += yhz[it, 1, x : x + 1, :]
                r[x, CY - 1 : CY] += yhz[it, 0, x : x + 1, :]

        @pl.when(it == ITERS - 1)
        def _():
            u_ref[...] = u_ref[...] + dz[it, pl.ds(1, CX)]

    for q in range(4):
        block = jnp.transpose(u_ref[pl.ds(4 * q, 4)].reshape(256, NZ))
        for n, piece in enumerate(chop(block, 2)):
            ut[pl.ds(256 * n, 256), pl.ds(256 * q, 256)] = piece.astype(BF16)

    def returned(j, t):
        return remote(back1.at[j], got1.at[pl.ds(al(by, 16), 16)], gs.at[t], gr.at[t], (bx, j))

    def sampled(t):
        j = (by + t) % NJ
        cell = slot[pl.ds(j, 1), :]
        a = hot(fit(CX * CY, cell // NZ))
        v = jnp.dot(ut[...], a, preferred_element_type=F32)
        v = jnp.where(fit(NZ, cell % NZ), v[:NZ] + v[NZ:], 0.0)
        v = jnp.sum(v, axis=0, keepdims=True)
        for i in range(NI):
            back1[j, i : i + 1, :CAP] = v[:, CAP * i : CAP * (i + 1)]

    @pl.loop(1, NJ)
    def _(t):
        sampled(t)
        returned((by + t) % NJ, t).start()

    sampled(0)
    mine = pltpu.make_async_copy(back1.at[by], got1.at[pl.ds(al(by, 16), 16)], gs.at[0])
    mine.start()
    for t in range(1, NJ):
        returned((by + t) % NJ, t).wait()
    mine.wait()
    for k in range(NI):
        back2[k] = got1[pl.ds(k, NJ, stride=NI), :]
    copies = []
    for t in range(NI):
        k = bx_peer(bx, t)
        src, dst = back2.at[k], got2.at[pl.ds(al(bx, 8), 8)]
        if t:
            copies.append(remote(src, dst, ks.at[t], kr.at[t], (k, by)))
        else:
            copies.append(pltpu.make_async_copy(src, dst, ks.at[0]))
        copies[-1].start()
    for c in copies:
        c.wait()
    found = [p.astype(BF16) for p in chop(jnp.transpose(got2[...])[:CAP], 3)]

    @pl.loop(0, P_DEV // 256)
    def _(c):
        at = pl.ds(al(c, 256), 256)
        ones = hot(fit(NB, own[:, at]))
        v = sum(jnp.dot(p, ones, preferred_element_type=F32) for p in found)
        imp_ref[:, at] = jnp.sum(jnp.where(fit(CAP, rank[:, at]), v, 0.0), axis=0, keepdims=True)


def local(normals, owners, cells, levels, rows, columns, depth):
    vm = pl.BlockSpec(memory_space=pltpu.VMEM)
    hb = pl.BlockSpec(memory_space=pl.ANY)
    brick = (CX, CY, NZ)
    tall = (ITERS, CX + 2, CY, NZ)
    dma = pltpu.SemaphoreType.DMA
    iterate, implicit = pl.pallas_call(
        relax,
        name="relax",
        out_shape=(jax.ShapeDtypeStruct(brick, F32), jax.ShapeDtypeStruct((1, P_DEV), F32)),
        in_specs=[vm, vm, vm, pl.BlockSpec(memory_space=pltpu.SMEM), hb, hb, hb],
        out_specs=(vm, vm),
        scratch_shapes=[
            pltpu.VMEM(brick, F32),
            pltpu.VMEM((ITERS, NI * CX, 8, 128), F32),
            pltpu.VMEM((NI * CX + 2, 8, 128), F32),
            pltpu.VMEM(tall, F32),
            pltpu.VMEM((2, NI * CX, 128), F32),
            pltpu.VMEM((ITERS, 2, CX, NZ), F32),
            pltpu.VMEM((ITERS, 2, 2, NJ * CY, 128), F32),
            pltpu.VMEM((2, 2, NJ * CY, 128), F32),
            pltpu.VMEM(tall, F32),
            pltpu.VMEM((2, NJ, 8, 128), F32),
            pltpu.VMEM((ITERS, NJ, 8, NZ), F32),
            pltpu.VMEM(tall, F32),
            pltpu.VMEM((2, CX, NZ), F32),
            pltpu.VMEM((ITERS, 2, CX, NZ), F32),
            pltpu.VMEM((256, 256), F32),
            pltpu.VMEM((512, 512), F32),
            pltpu.VMEM((256, 256), F32),
            pltpu.VMEM((2, 256, 256), BF16),
            pltpu.VMEM((2, 512, 512), BF16),
            pltpu.VMEM((2, 256, 256), BF16),
            pltpu.VMEM((2, NB, 128), F32),
            pltpu.VMEM((1, P_DEV), jnp.int32),
            pltpu.VMEM((2, NB, 128), F32),
            pltpu.VMEM((NJ, 2, NI, 128), F32),
            pltpu.VMEM((NJ, 2, NI, 128), F32),
            pltpu.VMEM((NJ, NI * CAP), jnp.int32),
            pltpu.VMEM((CX + 2, CY, NZ), F32),
            pltpu.VMEM(brick, F32),
            pltpu.VMEM(brick, F32),
            pltpu.VMEM((2, CX, NZ), F32),
            pltpu.VMEM((2, CX, NZ), F32),
            pltpu.VMEM((512, CX * CY), BF16),
            pltpu.VMEM((NJ, NI, 128), F32),
            pltpu.VMEM((NB, 128), F32),
            pltpu.VMEM((NI, NJ, 128), F32),
            pltpu.VMEM((NB, 128), F32),
            dma((2, NI)), dma((2, NI)), dma((2, NI)), dma((2, NI)),
            dma((2, NI)), dma((2, 2)),
            dma((2, NJ)), dma((2, NJ)), dma((2, NJ)), dma((2, NJ)), dma((2, NJ)), dma((2, NJ)),
            dma((2,)), dma((2,)), dma((4,)), dma((4,)),
            dma((NI,)), dma((NI,)), dma((NJ,)), dma((NJ,)), dma((4,)), dma((4,)),
            dma((NJ,)), dma((NJ,)), dma((NI,)), dma((NI,)), dma((3,)),
        ],
        compiler_params=pltpu.CompilerParams(
            collective_id=0, has_side_effects=True, vmem_limit_bytes=62 << 20
        ),
    )(normals, owners.reshape(1, P_DEV), cells.reshape(1, P_DEV), levels, rows, columns, depth)
    return iterate, implicit.reshape(P_DEV)


def solution(mesh):
    placed = (
        P(None, ("bx", "by")),
        P(("bx", "by"), None),
        P(("bx", "by")),
        P("bx", "by"),
        P(),
        P(),
        P(),
    )
    return jax.shard_map(
        local,
        mesh=mesh,
        in_specs=placed,
        out_specs=(P("bx", "by", None), P(("bx", "by"))),
        check_vma=False,
    )
```

```python
import functools
import jax
import jax.numpy as jnp
from jax import lax
from jax.experimental import pallas as pl
from jax.experimental.pallas import tpu as pltpu
from jax.sharding import PartitionSpec as P

CX, CY, NZ, ITERS = 16, 64, 256, 4
NI, NJ = 16, 8
NB, P_DEV, CAP = 128, 4096, 64
MESH = pl.DeviceIdType.MESH
F32, BF16 = jnp.float32, jnp.bfloat16


def split(v):
    hi = v.astype(BF16)
    return hi, (v - hi.astype(F32)).astype(BF16)


def dot3(a_hi, a_lo, b_hi, b_lo, dims=(((1,), (0,)), ((), ()))):
    mul = functools.partial(lax.dot_general, dimension_numbers=dims, preferred_element_type=F32)
    return mul(a_hi, b_hi) + (mul(a_lo, b_hi) + mul(a_hi, b_lo))


def remote(src, dst, send, recv, device):
    return pltpu.make_async_remote_copy(
        src_ref=src, dst_ref=dst, send_sem=send, recv_sem=recv, device_id=device, device_id_type=MESH
    )


def bx_peer(bx, t):
    y, z = bx // 4, bx % 4
    return ((y + t // 4) % 4) * 4 + (z + t % 4) % 4


BX_ORDER = (5, 10, 15, 1, 6, 11, 12, 2, 7, 8, 13, 3, 4, 9, 14, 0)


def al(v, m):
    return pl.multiple_of(v * m, m)


def greet(bx, by):
    barrier = pltpu.get_barrier_semaphore()
    count = 0
    for side in (0, 1, NJ - 1):
        for t in range(NI):
            if side == 0 and t == 0:
                continue
            pl.semaphore_signal(
                barrier, inc=1, device_id=(bx_peer(bx, t), (by + side) % NJ), device_id_type=MESH
            )
            count += 1
    for t in range(2, NJ - 1):
        pl.semaphore_signal(barrier, inc=1, device_id=(bx, (by + t) % NJ), device_id_type=MESH)
        count += 1
    return functools.partial(pl.semaphore_wait, barrier, count)


def relax(
    nrm, own, cel, lev_ref, mx_ref, my_ref, mz_ref, u_ref, imp_ref,
    r, xin, dxp, dx, edge, yhx, yin, dyl, dy, ye, yhy, dz, ze, yhz,
    mxv, myv, mzv, mxs, mys, mzs,
    box, rank, in1, out2, in2, slot, vx, vy, vz, fe, fh, ut, back1, got1, back2, got2,
    xs, xr, bs, br, es, er, ys, yr, cs, cr, ns, nr, hs, hr, zs, zr,
    ps, pr, qs, qr, fs, fr, gs, gr, ks, kr, ms,
):
    bx, by = lax.axis_index("bx"), lax.axis_index("by")
    yg, zh = bx // 2, bx % 2
    zero = jnp.zeros((8, 128), F32)
    dxp[0] = zero
    dxp[257] = zero
    for ref in (yhx, yhy, yhz):
        ref[...] = jnp.zeros(ref.shape, F32)
    ye[...] = jnp.zeros(ye.shape, F32)
    for it in range(ITERS):
        for ref in (dy, dz):
            ref[it, 0] = jnp.zeros((CY, NZ), F32)
            ref[it, CX + 1] = jnp.zeros((CY, NZ), F32)
    vx[0] = jnp.zeros((CY, NZ), F32)
    vx[CX + 1] = jnp.zeros((CY, NZ), F32)
    fh[...] = jnp.zeros(fh.shape, F32)
    back1[...] = jnp.zeros(back1.shape, F32)
    all_here = greet(bx, by)
    fetches = [
        pltpu.make_async_copy(m, v, ms.at[n])
        for n, (m, v) in enumerate(((mx_ref, mxv), (my_ref, myv), (mz_ref, mzv)))
    ]
    for c in fetches:
        c.start()
    vx[pl.ds(1, CX)] = jnp.zeros((CX, CY, NZ), F32)
    vy[...] = jnp.zeros(vy.shape, F32)
    vz[...] = jnp.zeros(vz.shape, F32)
    u_ref[...] = jnp.zeros(u_ref.shape, F32)
    below, above = jnp.maximum(by - 1, 0), jnp.minimum(by + 1, NJ - 1)
    lanes = (((1,), (1,)), ((), ()))

    def fit(rows, index):
        return lax.broadcasted_iota(jnp.int32, (rows, index.shape[1]), 0) == index

    def hot(mask):
        return jnp.where(mask, 1.0, 0.0).astype(BF16)

    def chop(v, n):
        pieces = []
        for _ in range(n):
            pieces.append(v.astype(BF16).astype(F32))
            v = v - pieces[-1]
        return pieces

    before = lax.broadcasted_iota(jnp.int32, (256, 256), 0) < lax.broadcasted_iota(jnp.int32, (256, 256), 1)
    counter = jnp.concatenate([hot(before), jnp.ones((256, 256), BF16)], axis=1)
    box[...] = jnp.zeros(box.shape, F32)

    def dispatch(c, seen):
        at = pl.ds(al(c, 256), 256)
        mine = fit(NB, own[:, at])
        ones = hot(mine)
        counts = jnp.dot(ones, counter, preferred_element_type=F32)
        place = jnp.sum(jnp.where(mine, counts[:, :256] + seen, 0.0), axis=0, keepdims=True)
        place = place.astype(jnp.int32)
        rank[:, at] = place
        there = fit(CAP, place)
        values = [nrm[k : k + 1, at] for k in range(3)] + [cel[:, at].astype(F32)]
        pieces = [chop(v, 3) for v in values]
        for n in range(3):
            w = jnp.concatenate([jnp.where(there, p[n], 0.0) for p in pieces], axis=0).astype(BF16)
            d = lax.dot_general(ones, w, lanes, preferred_element_type=F32)
            box[0] += d[:, :128]
            box[1] += d[:, 128:]
        return seen + counts[:, 256:]

    lax.fori_loop(0, P_DEV // 256, dispatch, jnp.zeros((NB, 256), F32), unroll=4)

    all_here()
    copies = []
    for t in range(NI):
        k = bx_peer(bx, t)
        src, dst = box.at[:, pl.ds(al(k, 8), 8)], in1.at[:, pl.ds(al(bx, 8), 8)]
        if t:
            copies.append(remote(src, dst, ps.at[t], pr.at[t], (k, by)))
        else:
            copies.append(pltpu.make_async_copy(src, dst, ps.at[0]))
        copies[-1].start()
    for c in copies:
        c.wait()
    for j in range(NJ):
        for h in range(2):
            out2[j, h] = in1.at[h][pl.ds(j, NI, stride=NJ), :]
    copies = []
    for t in range(NJ):
        j = (by + t) % NJ
        if t:
            copies.append(remote(out2.at[j], in2.at[by], qs.at[t], qr.at[t], (bx, j)))
        else:
            copies.append(pltpu.make_async_copy(out2.at[j], in2.at[by], qr.at[0]))
        copies[-1].start()
    for c, (v, vs) in zip(fetches, ((mxv, mxs), (myv, mys), (mzv, mzs))):
        c.wait()
        vs[0], vs[1] = split(v[...])

    @pl.loop(0, NJ)
    def _(t):
        j = (by + NJ - t) % NJ
        remote(out2.at[0], in2.at[j], qs.at[0], qr.at[t], (bx, by)).wait_recv()
        rows = []
        for k in range(4):
            v = in2[j, k // 2][:, CAP * (k % 2) : CAP * (k % 2 + 1)]
            rows.append(jnp.concatenate([v[i : i + 1] for i in range(NI)], axis=1))
        cell = rows[3].astype(jnp.int32)
        slot[pl.ds(j, 1), :] = cell
        depth = fit(NZ, cell % NZ)
        weighted = jnp.concatenate(
            [
                jnp.concatenate([jnp.where(depth, p, 0.0).astype(BF16) for p in chop(v, 2)], axis=1)
                for v in rows[:3]
            ],
            axis=0,
        )
        for q in range(4):
            a = hot(fit(256, cell // NZ - 256 * q))
            d = lax.dot_general(
                jnp.concatenate([a, a], axis=1), weighted, lanes, preferred_element_type=F32
            ).reshape(4, CY, 3 * NZ)
            vx[pl.ds(1 + 4 * q, 4)] += d[:, :, :NZ]
            vy[pl.ds(4 * q, 4)] += d[:, :, NZ : 2 * NZ]
            vz[pl.ds(4 * q, 4)] += d[:, :, 2 * NZ :]

    for c in copies[1:]:
        c.wait_send()

    down = remote(vx.at[1], vx.at[CX + 1], fs.at[0], fr.at[0], (jnp.maximum(bx - 1, 0), by))
    up = remote(vx.at[CX], vx.at[0], fs.at[1], fr.at[1], (jnp.minimum(bx + 1, NI - 1), by))
    for x in range(CX):
        fe[0, x : x + 1] = vy[x, 0:1]
        fe[1, x : x + 1] = vy[x, CY - 1 : CY]
    low = remote(fe.at[0], fh.at[0], fs.at[2], fr.at[2], (bx, below))
    high = remote(fe.at[1], fh.at[1], fs.at[3], fr.at[3], (bx, above))

    @pl.when(bx > 0)
    def _():
        down.start()

    @pl.when(bx < NI - 1)
    def _():
        up.start()

    @pl.when(by > 0)
    def _():
        low.start()

    @pl.when(by < NJ - 1)
    def _():
        high.start()

    @pl.when(by > 0)
    def _():
        low.wait_send()
        high.wait_recv()

    @pl.when(by < NJ - 1)
    def _():
        high.wait_send()
        low.wait_recv()

    @pl.when(bx > 0)
    def _():
        down.wait_send()
        up.wait_recv()

    @pl.when(bx < NI - 1)
    def _():
        up.wait_send()
        down.wait_recv()

    @pl.loop(0, CX)
    def _(x):
        zi = lax.broadcasted_iota(jnp.int32, (CY, NZ), 1)
        yi = lax.broadcasted_iota(jnp.int32, (CY, NZ), 0)
        b, c = vy[x], vz[x]
        total = vx[x + 2] - vx[x]
        total = total + jnp.where(yi == CY - 1, fh[0, pl.ds(x, 1), :], pltpu.roll(b, CY - 1, 0))
        total = total - jnp.where(yi == 0, fh[1, pl.ds(x, 1), :], pltpu.roll(b, 1, 0))
        total = total + jnp.where(zi == NZ - 1, 0.0, pltpu.roll(c, NZ - 1, 1))
        total = total - jnp.where(zi == 0, 0.0, pltpu.roll(c, 1, 1))
        r[x] = -0.5 * total

    diagonal = 6.0 + (1.0 + lev_ref[0, 0].astype(F32))

    def plane(d, x, low=None, high=None):
        c = d[x + 1]
        zi = lax.broadcasted_iota(jnp.int32, (CY, NZ), 1)
        yi = lax.broadcasted_iota(jnp.int32, (CY, NZ), 0)
        near = d[x] + d[x + 2]
        near = near + jnp.where(zi == 0, 0.0, pltpu.roll(c, 1, 1))
        near = near + jnp.where(zi == NZ - 1, 0.0, pltpu.roll(c, NZ - 1, 1))
        near = near + jnp.where(yi == 0, low(x) if low else 0.0, pltpu.roll(c, 1, 0))
        near = near + jnp.where(yi == CY - 1, high(x) if high else 0.0, pltpu.roll(c, CY - 1, 0))
        r[x] = r[x] - (diagonal * c - near)
        u_ref[x] = u_ref[x] + c

    def x_planes(d, send, recv):
        down = remote(d.at[1], d.at[CX + 1], send.at[0], recv.at[0], (jnp.maximum(bx - 1, 0), by))
        up = remote(d.at[CX], d.at[0], send.at[1], recv.at[1], (jnp.minimum(bx + 1, NI - 1), by))
        return down, up

    @pl.loop(0, ITERS)
    def _(it):
        there = []
        for h in range(2):
            for t in BX_ORDER:
                k = bx_peer(bx, t)
                src = r.at[:, pl.ds(al(2 * (k // 2) + h, 4), 4), pl.ds(al(k % 2, 128), 128)]
                dst = xin.at[it, pl.ds(bx * 16, 16), pl.ds(4 * h, 4)]
                if t:
                    there.append(remote(src, dst, xs.at[h, t], xr.at[h, t], (k, by)))
                else:
                    there.append(pltpu.make_async_copy(src, dst, xs.at[h, 0]))
                there[-1].start()
        lines = xin.at[it].reshape(NI * CX * 8, 128)
        moved = dxp.reshape((NI * CX + 2) * 8, 128)
        copies = []

        def edges(side, beside):
            out = []
            for t in range(NI):
                k = bx_peer(bx, t)
                out.append(
                    remote(
                        edge.at[side, pl.ds(al(k, 16), 16)],
                        yhx.at[it, side, :, pl.ds(al(zh, 128), 128)],
                        es.at[side, t],
                        er.at[side, zh],
                        (k, beside),
                    )
                )
            return out

        def half(side, z):
            return remote(
                edge.at[side, pl.ds(0, 16)], yhx.at[it, side, :, pl.ds(128 * z, 128)],
                es.at[side, 0], er.at[side, z], (bx, by),
            )

        def back(h, part):
            for t in BX_ORDER:
                k = bx_peer(bx, t)
                src = dxp.at[pl.ds(k * 16 + 10 * part, 10 - 2 * part), pl.ds(4 * h, 4)]
                dst = dx.at[
                    it, pl.ds(10 * part, 10 - 2 * part), pl.ds(al(2 * yg + h, 4), 4), pl.ds(al(zh, 128), 128)
                ]
                n = 2 * part + h
                if t:
                    copies.append(remote(src, dst, bs.at[n, t], br.at[n, t], (k, by)))
                else:
                    copies.append(pltpu.make_async_copy(src, dst, bs.at[n, 0]))
                copies[-1].start()

        for h in range(2):
            for c in there[NI * h : NI * (h + 1)]:
                c.wait()
            for y in range(4 * h, 4 * h + 4, 2):
                v = jnp.concatenate([lines[pl.ds(y + n, 256, stride=8), :] for n in range(2)], axis=1)
                d = dot3(mxs[0], mxs[1], *split(v))
                moved[pl.ds(8 + y, 256, stride=8), :] = d[:, :128]
                moved[pl.ds(9 + y, 256, stride=8), :] = d[:, 128:]
                if y == 0:
                    edge[0] = d[:, :128]
                if y == 6:
                    edge[1] = d[:, 128:]
            back(h, 0)
            if h == 0:

                @pl.when((yg == 0) & (by > 0))
                def _():
                    for c in edges(0, below):
                        c.start()

            else:

                @pl.when((yg == 7) & (by < NJ - 1))
                def _():
                    for c in edges(1, above):
                        c.start()

        back(0, 1)
        back(1, 1)
        for c in copies[: 2 * NI]:
            c.wait()

        @pl.when(by < NJ - 1)
        def _():
            half(0, 0).wait_recv()
            half(0, 1).wait_recv()

        @pl.when(by > 0)
        def _():
            half(1, 0).wait_recv()
            half(1, 1).wait_recv()

        forth = []
        for e in range(2):
            if e:
                for c in copies[2 * NI :]:
                    c.wait()
            for t in [*range(1, NJ), 0]:
                j = (by + t) % NJ
                plane(
                    dx.at[it],
                    j + NJ * e,
                    lambda x: yhx[it, 1, pl.ds(x, 1), :],
                    lambda x: yhx[it, 0, pl.ds(x, 1), :],
                )
                src, dst = r.at[j + NJ * e], yin.at[it, e, pl.ds(al(by, 64), 64)]
                if t:
                    forth.append(remote(src, dst, ys.at[e, t], yr.at[e, t], (bx, j)))
                else:
                    forth.append(pltpu.make_async_copy(src, dst, ys.at[e, 0]))
                forth[-1].start()

        @pl.when((yg == 0) & (by > 0))
        def _():
            for c in edges(0, below):
                c.wait_send()

        @pl.when((yg == 7) & (by < NJ - 1))
        def _():
            for c in edges(1, above):
                c.wait_send()

        copies = []
        for e in range(2):
            for c in forth[NJ * e : NJ * (e + 1)]:
                c.wait()
            d = dot3(mys[0], mys[1], *split(yin[it, e]))
            dyl[e] = d
            for j in range(NJ):
                for n in range(2):
                    if j:
                        ye[e, j, n : n + 1] = d[64 * j - 1 : 64 * j, 128 * n : 128 * (n + 1)]
                    if j < NJ - 1:
                        ye[e, j, 2 + n : 3 + n] = d[64 * j + 64 : 64 * j + 65, 128 * n : 128 * (n + 1)]
            for t in [*range(1, NJ), 0]:
                j = (by + t) % NJ
                main = (dyl.at[e, pl.ds(al(j, 64), 64)], dy.at[it, 1 + by + NJ * e])
                outer = (ye.at[e, j], yhy.at[it, e, by])
                if t:
                    copies.append(remote(*main, cs.at[e, t], cr.at[e, by], (bx, j)))
                    copies.append(remote(*outer, ns.at[e, t], nr.at[e, t], (bx, j)))
                else:
                    copies.append(pltpu.make_async_copy(*main, cr.at[e, by]))
                    copies.append(pltpu.make_async_copy(*outer, ns.at[e, 0]))
                copies[-2].start()
                copies[-1].start()

        def arrived(e, m):
            remote(
                dyl.at[e, pl.ds(0, 64)], dy.at[it, 1 + m + NJ * e], cs.at[e, 0], cr.at[e, m], (bx, by)
            ).wait_recv()

        def rest(e):
            for n in range(2 * NJ * e, 2 * NJ * (e + 1) - 2, 2):
                copies[n].wait_send()
                copies[n + 1].wait()
            copies[2 * NJ * (e + 1) - 1].wait()

        def outer_row(side):
            def load(x):
                at = (it, x // NJ, x % NJ)
                return jnp.concatenate(
                    [yhy[(*at, pl.ds(2 * side + n, 1), slice(None))] for n in range(2)], axis=1
                )

            return load

        rows = (outer_row(0), outer_row(1))
        down, up = x_planes(dy.at[it], hs, hr)
        arrived(0, 0)

        @pl.when(bx > 0)
        def _():
            down.start()

        for m in range(1, NJ):
            arrived(0, m)
        rest(0)

        def z_planes(x, n):
            v = r[pl.ds(x, n)].reshape(n * CY, NZ)
            d = dot3(*split(v), mzs[0], mzs[1], lanes)
            dz[it, pl.ds(x + 1, n)] = d.reshape(n, CY, NZ)

        @pl.loop(1, NJ - 1)
        def _(x):
            plane(dy.at[it], x, *rows)

        for x in range(1, NJ - 1, 2):
            z_planes(x, 2)
        arrived(1, NJ - 1)

        @pl.when(bx < NI - 1)
        def _():
            up.start()

        for m in range(NJ - 1):
            arrived(1, m)
        rest(1)

        @pl.loop(NJ - 1, CX - 1)
        def _(x):
            plane(dy.at[it], x, *rows)

        @pl.when(bx > 0)
        def _():
            down.wait_send()
            up.wait_recv()

        @pl.when(bx < NI - 1)
        def _():
            up.wait_send()
            down.wait_recv()

        for x in (0, CX - 1):
            plane(dy.at[it], x, *rows)

        z_planes(0, 1)
        z_planes(CX - 1, 1)
        down, up = x_planes(dz.at[it], zs, zr)
        low = remote(ze.at[0], yhz.at[it, 0], zs.at[2], zr.at[2], (bx, below))
        high = remote(ze.at[1], yhz.at[it, 1], zs.at[3], zr.at[3], (bx, above))
        more = it < ITERS - 1

        @pl.when(more & (bx > 0))
        def _():
            down.start()

        @pl.when(more & (bx < NI - 1))
        def _():
            up.start()

        outer = jnp.concatenate(
            [r[x, y : y + 1, :] for y in (0, CY - 1) for x in range(CX)], axis=0
        )
        outer = dot3(*split(outer), mzs[0], mzs[1], lanes)
        ze[0] = outer[:CX]
        ze[1] = outer[CX:]

        @pl.when(more & (by > 0))
        def _():
            low.start()

        @pl.when(more & (by < NJ - 1))
        def _():
            high.start()

        for x in range(NJ - 1, CX - 1, 2):
            z_planes(x, 2)

        @pl.when(more)
        def _():
            @pl.loop(1, CX - 1)
            def _(x):
                plane(dz.at[it], x)

            @pl.when(bx > 0)
            def _():
                down.wait_send()
                up.wait_recv()

            @pl.when(bx < NI - 1)
            def _():
                up.wait_send()
                down.wait_recv()

            for x in (0, CX - 1):
                plane(dz.at[it], x)

            @pl.when(by > 0)
            def _():
                low.wait_send()
                high.wait_recv()

            @pl.when(by < NJ - 1)
            def _():
                high.wait_send()
                low.wait_recv()

            for x in range(CX):
                r[x, 0:1] += yhz[it, 1, x : x + 1, :]
                r[x, CY - 1 : CY] += yhz[it, 0, x : x + 1, :]

        @pl.when(it == ITERS - 1)
        def _():
            u_ref[...] = u_ref[...] + dz[it, pl.ds(1, CX)]

    for q in range(4):
        block = jnp.transpose(u_ref[pl.ds(4 * q, 4)].reshape(256, NZ))
        for n, piece in enumerate(chop(block, 2)):
            ut[pl.ds(256 * n, 256), pl.ds(256 * q, 256)] = piece.astype(BF16)

    def returned(j, t):
        return remote(back1.at[j], got1.at[pl.ds(al(by, 16), 16)], gs.at[t], gr.at[t], (bx, j))

    def sampled(t):
        j = (by + t) % NJ
        cell = slot[pl.ds(j, 1), :]
        a = hot(fit(CX * CY, cell // NZ))
        v = jnp.dot(ut[...], a, preferred_element_type=F32)
        v = jnp.where(fit(NZ, cell % NZ), v[:NZ] + v[NZ:], 0.0)
        v = jnp.sum(v, axis=0, keepdims=True)
        for i in range(NI):
            back1[j, i : i + 1, :CAP] = v[:, CAP * i : CAP * (i + 1)]

    @pl.loop(1, NJ)
    def _(t):
        sampled(t)
        returned((by + t) % NJ, t).start()

    sampled(0)
    mine = pltpu.make_async_copy(back1.at[by], got1.at[pl.ds(al(by, 16), 16)], gs.at[0])
    mine.start()
    for t in range(1, NJ):
        returned((by + t) % NJ, t).wait()
    mine.wait()
    for k in range(NI):
        back2[k] = got1[pl.ds(k, NJ, stride=NI), :]
    copies = []
    for t in range(NI):
        k = bx_peer(bx, t)
        src, dst = back2.at[k], got2.at[pl.ds(al(bx, 8), 8)]
        if t:
            copies.append(remote(src, dst, ks.at[t], kr.at[t], (k, by)))
        else:
            copies.append(pltpu.make_async_copy(src, dst, ks.at[0]))
        copies[-1].start()
    for c in copies:
        c.wait()
    found = [p.astype(BF16) for p in chop(jnp.transpose(got2[...])[:CAP], 3)]

    @pl.loop(0, P_DEV // 256, unroll=4)
    def _(c):
        at = pl.ds(al(c, 256), 256)
        ones = hot(fit(NB, own[:, at]))
        v = sum(jnp.dot(p, ones, preferred_element_type=F32) for p in found)
        imp_ref[:, at] = jnp.sum(jnp.where(fit(CAP, rank[:, at]), v, 0.0), axis=0, keepdims=True)


def local(normals, owners, cells, levels, rows, columns, depth):
    vm = pl.BlockSpec(memory_space=pltpu.VMEM)
    hb = pl.BlockSpec(memory_space=pl.ANY)
    brick = (CX, CY, NZ)
    tall = (ITERS, CX + 2, CY, NZ)
    dma = pltpu.SemaphoreType.DMA
    iterate, implicit = pl.pallas_call(
        relax,
        name="relax",
        out_shape=(jax.ShapeDtypeStruct(brick, F32), jax.ShapeDtypeStruct((1, P_DEV), F32)),
        in_specs=[vm, vm, vm, pl.BlockSpec(memory_space=pltpu.SMEM), hb, hb, hb],
        out_specs=(vm, vm),
        scratch_shapes=[
            pltpu.VMEM(brick, F32),
            pltpu.VMEM((ITERS, NI * CX, 8, 128), F32),
            pltpu.VMEM((NI * CX + 2, 8, 128), F32),
            pltpu.VMEM(tall, F32),
            pltpu.VMEM((2, NI * CX, 128), F32),
            pltpu.VMEM((ITERS, 2, CX, NZ), F32),
            pltpu.VMEM((ITERS, 2, NJ * CY, NZ), F32),
            pltpu.VMEM((2, NJ * CY, NZ), F32),
            pltpu.VMEM(tall, F32),
            pltpu.VMEM((2, NJ, 8, 128), F32),
            pltpu.VMEM((ITERS, 2, NJ, 8, 128), F32),
            pltpu.VMEM(tall, F32),
            pltpu.VMEM((2, CX, NZ), F32),
            pltpu.VMEM((ITERS, 2, CX, NZ), F32),
            pltpu.VMEM((256, 256), F32),
            pltpu.VMEM((512, 512), F32),
            pltpu.VMEM((256, 256), F32),
            pltpu.VMEM((2, 256, 256), BF16),
            pltpu.VMEM((2, 512, 512), BF16),
            pltpu.VMEM((2, 256, 256), BF16),
            pltpu.VMEM((2, NB, 128), F32),
            pltpu.VMEM((1, P_DEV), jnp.int32),
            pltpu.VMEM((2, NB, 128), F32),
            pltpu.VMEM((NJ, 2, NI, 128), F32),
            pltpu.VMEM((NJ, 2, NI, 128), F32),
            pltpu.VMEM((NJ, NI * CAP), jnp.int32),
            pltpu.VMEM((CX + 2, CY, NZ), F32),
            pltpu.VMEM(brick, F32),
            pltpu.VMEM(brick, F32),
            pltpu.VMEM((2, CX, NZ), F32),
            pltpu.VMEM((2, CX, NZ), F32),
            pltpu.VMEM((512, CX * CY), BF16),
            pltpu.VMEM((NJ, NI, 128), F32),
            pltpu.VMEM((NB, 128), F32),
            pltpu.VMEM((NI, NJ, 128), F32),
            pltpu.VMEM((NB, 128), F32),
            dma((2, NI)), dma((2, NI)), dma((4, NI)), dma((4, NI)),
            dma((2, NI)), dma((2, 2)),
            dma((2, NJ)), dma((2, NJ)), dma((2, NJ)), dma((2, NJ)), dma((2, NJ)), dma((2, NJ)),
            dma((2,)), dma((2,)), dma((4,)), dma((4,)),
            dma((NI,)), dma((NI,)), dma((NJ,)), dma((NJ,)), dma((4,)), dma((4,)),
            dma((NJ,)), dma((NJ,)), dma((NI,)), dma((NI,)), dma((3,)),
        ],
        compiler_params=pltpu.CompilerParams(
            collective_id=0, has_side_effects=True, vmem_limit_bytes=61 << 20
        ),
    )(normals, owners.reshape(1, P_DEV), cells.reshape(1, P_DEV), levels, rows, columns, depth)
    return iterate, implicit.reshape(P_DEV)


def solution(mesh):
    placed = (
        P(None, ("bx", "by")),
        P(("bx", "by"), None),
        P(("bx", "by")),
        P("bx", "by"),
        P(),
        P(),
        P(),
    )
    return jax.shard_map(
        local,
        mesh=mesh,
        in_specs=placed,
        out_specs=(P("bx", "by", None), P(("bx", "by"))),
        check_vma=False,
    )
```

```python
import functools
import jax
import jax.numpy as jnp
from jax import lax
from jax.experimental import pallas as pl
from jax.experimental.pallas import tpu as pltpu
from jax.sharding import PartitionSpec as P

CX, CY, NZ, ITERS = 16, 64, 256, 4
NI, NJ = 16, 8
NB, P_DEV, CAP = 128, 4096, 64
MESH = pl.DeviceIdType.MESH
F32, BF16 = jnp.float32, jnp.bfloat16


def split(v):
    hi = v.astype(BF16)
    return hi, (v - hi.astype(F32)).astype(BF16)


def dot3(a_hi, a_lo, b_hi, b_lo, dims=(((1,), (0,)), ((), ()))):
    mul = functools.partial(lax.dot_general, dimension_numbers=dims, preferred_element_type=F32)
    return mul(a_hi, b_hi) + (mul(a_lo, b_hi) + mul(a_hi, b_lo))


def remote(src, dst, send, recv, device):
    return pltpu.make_async_remote_copy(
        src_ref=src, dst_ref=dst, send_sem=send, recv_sem=recv, device_id=device, device_id_type=MESH
    )


def bx_peer(bx, t):
    y, z = bx // 4, bx % 4
    return ((y + t // 4) % 4) * 4 + (z + t % 4) % 4


BX_ORDER = (5, 10, 15, 1, 6, 11, 12, 2, 7, 8, 13, 3, 4, 9, 14, 0)


def al(v, m):
    return pl.multiple_of(v * m, m)


def held(j):
    return 4 * (j % 2) + j // 2


def greet(bx, by):
    barrier = pltpu.get_barrier_semaphore()
    count = 0
    for side in (0, 1, NJ - 1):
        for t in range(NI):
            if side == 0 and t == 0:
                continue
            pl.semaphore_signal(
                barrier, inc=1, device_id=(bx_peer(bx, t), (by + side) % NJ), device_id_type=MESH
            )
            count += 1
    for t in range(2, NJ - 1):
        pl.semaphore_signal(barrier, inc=1, device_id=(bx, (by + t) % NJ), device_id_type=MESH)
        count += 1
    return functools.partial(pl.semaphore_wait, barrier, count)


def relax(
    nrm, own, cel, lev_ref, mx_ref, my_ref, mz_ref, u_ref, imp_ref,
    r, xin, dxp, dx, edge, yhx, yin, dyl, dy, ye, yhy, dz, ze, yhz,
    mxv, myv, mzv, mxs, mys, mzs,
    box, rank, in1, out2, in2, slot, vx, vy, vz, fe, fh, ut, back1, got1, back2, got2,
    xs, xr, bs, br, es, er, ys, yr, cs, cr, ns, nr, hs, hr, zs, zr,
    ps, pr, qs, qr, fs, fr, gs, gr, ks, kr, ms,
):
    bx, by = lax.axis_index("bx"), lax.axis_index("by")
    yg, zh = bx // 2, bx % 2
    zero = jnp.zeros((8, 128), F32)
    dxp[0] = zero
    dxp[257] = zero
    for ref in (yhx, yhy, yhz):
        ref[...] = jnp.zeros(ref.shape, F32)
    ye[...] = jnp.zeros(ye.shape, F32)
    for it in range(ITERS):
        for ref in (dy, dz):
            ref[it, 0] = jnp.zeros((CY, NZ), F32)
            ref[it, CX + 1] = jnp.zeros((CY, NZ), F32)
    vx[0] = jnp.zeros((CY, NZ), F32)
    vx[CX + 1] = jnp.zeros((CY, NZ), F32)
    fh[...] = jnp.zeros(fh.shape, F32)
    back1[...] = jnp.zeros(back1.shape, F32)
    all_here = greet(bx, by)
    fetches = [
        pltpu.make_async_copy(m, v, ms.at[n])
        for n, (m, v) in enumerate(((mx_ref, mxv), (my_ref, myv), (mz_ref, mzv)))
    ]
    for c in fetches:
        c.start()
    vx[pl.ds(1, CX)] = jnp.zeros((CX, CY, NZ), F32)
    vy[...] = jnp.zeros(vy.shape, F32)
    vz[...] = jnp.zeros(vz.shape, F32)
    u_ref[...] = jnp.zeros(u_ref.shape, F32)
    below, above = jnp.maximum(by - 1, 0), jnp.minimum(by + 1, NJ - 1)
    lanes = (((1,), (1,)), ((), ()))

    def fit(rows, index):
        return lax.broadcasted_iota(jnp.int32, (rows, index.shape[1]), 0) == index

    def hot(mask):
        return jnp.where(mask, 1.0, 0.0).astype(BF16)

    def chop(v, n):
        pieces = []
        for _ in range(n):
            pieces.append(v.astype(BF16).astype(F32))
            v = v - pieces[-1]
        return pieces

    before = lax.broadcasted_iota(jnp.int32, (256, 256), 0) < lax.broadcasted_iota(jnp.int32, (256, 256), 1)
    counter = jnp.concatenate([hot(before), jnp.ones((256, 256), BF16)], axis=1)
    box[...] = jnp.zeros(box.shape, F32)

    def dispatch(c, seen):
        at = pl.ds(al(c, 256), 256)
        mine = fit(NB, own[:, at])
        ones = hot(mine)
        counts = jnp.dot(ones, counter, preferred_element_type=F32)
        place = jnp.sum(jnp.where(mine, counts[:, :256] + seen, 0.0), axis=0, keepdims=True)
        place = place.astype(jnp.int32)
        rank[:, at] = place
        there = fit(CAP, place)
        values = [nrm[k : k + 1, at] for k in range(3)] + [cel[:, at].astype(F32)]
        pieces = [chop(v, 3) for v in values]
        for n in range(3):
            w = jnp.concatenate([jnp.where(there, p[n], 0.0) for p in pieces], axis=0).astype(BF16)
            d = lax.dot_general(ones, w, lanes, preferred_element_type=F32)
            box[0] += d[:, :128]
            box[1] += d[:, 128:]
        return seen + counts[:, 256:]

    lax.fori_loop(0, P_DEV // 256, dispatch, jnp.zeros((NB, 256), F32), unroll=4)

    all_here()
    copies = []
    for t in range(NI):
        k = bx_peer(bx, t)
        src, dst = box.at[:, pl.ds(al(k, 8), 8)], in1.at[:, pl.ds(al(bx, 8), 8)]
        if t:
            copies.append(remote(src, dst, ps.at[t], pr.at[t], (k, by)))
        else:
            copies.append(pltpu.make_async_copy(src, dst, ps.at[0]))
        copies[-1].start()
    for c in copies:
        c.wait()
    for j in range(NJ):
        for h in range(2):
            out2[j, h] = in1.at[h][pl.ds(j, NI, stride=NJ), :]
    copies = []
    for t in range(NJ):
        j = (by + t) % NJ
        if t:
            copies.append(remote(out2.at[j], in2.at[by], qs.at[t], qr.at[t], (bx, j)))
        else:
            copies.append(pltpu.make_async_copy(out2.at[j], in2.at[by], qr.at[0]))
        copies[-1].start()
    for c, (v, vs) in zip(fetches, ((mxv, mxs), (myv, mys), (mzv, mzs))):
        c.wait()
        vs[0], vs[1] = split(v[...])

    @pl.loop(0, NJ)
    def _(t):
        j = (by + NJ - t) % NJ
        remote(out2.at[0], in2.at[j], qs.at[0], qr.at[t], (bx, by)).wait_recv()
        rows = []
        for k in range(4):
            v = in2[j, k // 2][:, CAP * (k % 2) : CAP * (k % 2 + 1)]
            rows.append(jnp.concatenate([v[i : i + 1] for i in range(NI)], axis=1))
        cell = rows[3].astype(jnp.int32)
        slot[pl.ds(j, 1), :] = cell
        depth = fit(NZ, cell % NZ)
        weighted = jnp.concatenate(
            [
                jnp.concatenate([jnp.where(depth, p, 0.0).astype(BF16) for p in chop(v, 2)], axis=1)
                for v in rows[:3]
            ],
            axis=0,
        )
        for q in range(4):
            a = hot(fit(256, cell // NZ - 256 * q))
            d = lax.dot_general(
                jnp.concatenate([a, a], axis=1), weighted, lanes, preferred_element_type=F32
            ).reshape(4, CY, 3 * NZ)
            vx[pl.ds(1 + 4 * q, 4)] += d[:, :, :NZ]
            vy[pl.ds(4 * q, 4)] += d[:, :, NZ : 2 * NZ]
            vz[pl.ds(4 * q, 4)] += d[:, :, 2 * NZ :]

    for c in copies[1:]:
        c.wait_send()

    down = remote(vx.at[1], vx.at[CX + 1], fs.at[0], fr.at[0], (jnp.maximum(bx - 1, 0), by))
    up = remote(vx.at[CX], vx.at[0], fs.at[1], fr.at[1], (jnp.minimum(bx + 1, NI - 1), by))
    for x in range(CX):
        fe[0, x : x + 1] = vy[x, 0:1]
        fe[1, x : x + 1] = vy[x, CY - 1 : CY]
    low = remote(fe.at[0], fh.at[0], fs.at[2], fr.at[2], (bx, below))
    high = remote(fe.at[1], fh.at[1], fs.at[3], fr.at[3], (bx, above))

    @pl.when(bx > 0)
    def _():
        down.start()

    @pl.when(bx < NI - 1)
    def _():
        up.start()

    @pl.when(by > 0)
    def _():
        low.start()

    @pl.when(by < NJ - 1)
    def _():
        high.start()

    @pl.when(by > 0)
    def _():
        low.wait_send()
        high.wait_recv()

    @pl.when(by < NJ - 1)
    def _():
        high.wait_send()
        low.wait_recv()

    @pl.when(bx > 0)
    def _():
        down.wait_send()
        up.wait_recv()

    @pl.when(bx < NI - 1)
    def _():
        up.wait_send()
        down.wait_recv()

    @pl.loop(0, CX)
    def _(x):
        zi = lax.broadcasted_iota(jnp.int32, (CY, NZ), 1)
        yi = lax.broadcasted_iota(jnp.int32, (CY, NZ), 0)
        b, c = vy[x], vz[x]
        total = vx[x + 2] - vx[x]
        total = total + jnp.where(yi == CY - 1, fh[0, pl.ds(x, 1), :], pltpu.roll(b, CY - 1, 0))
        total = total - jnp.where(yi == 0, fh[1, pl.ds(x, 1), :], pltpu.roll(b, 1, 0))
        total = total + jnp.where(zi == NZ - 1, 0.0, pltpu.roll(c, NZ - 1, 1))
        total = total - jnp.where(zi == 0, 0.0, pltpu.roll(c, 1, 1))
        r[x] = -0.5 * total

    diagonal = 6.0 + (1.0 + lev_ref[0, 0].astype(F32))

    def plane(d, x, low=None, high=None):
        c = d[x + 1]
        zi = lax.broadcasted_iota(jnp.int32, (CY, NZ), 1)
        yi = lax.broadcasted_iota(jnp.int32, (CY, NZ), 0)
        near = d[x] + d[x + 2]
        near = near + jnp.where(zi == 0, 0.0, pltpu.roll(c, 1, 1))
        near = near + jnp.where(zi == NZ - 1, 0.0, pltpu.roll(c, NZ - 1, 1))
        near = near + jnp.where(yi == 0, low(x) if low else 0.0, pltpu.roll(c, 1, 0))
        near = near + jnp.where(yi == CY - 1, high(x) if high else 0.0, pltpu.roll(c, CY - 1, 0))
        r[x] = r[x] - (diagonal * c - near)
        u_ref[x] = u_ref[x] + c

    def x_planes(d, send, recv):
        down = remote(d.at[1], d.at[CX + 1], send.at[0], recv.at[0], (jnp.maximum(bx - 1, 0), by))
        up = remote(d.at[CX], d.at[0], send.at[1], recv.at[1], (jnp.minimum(bx + 1, NI - 1), by))
        return down, up

    @pl.loop(0, ITERS)
    def _(it):
        there = []
        for h in range(2):
            for t in BX_ORDER:
                k = bx_peer(bx, t)
                src = r.at[:, pl.ds(al(2 * (k // 2) + h, 4), 4), pl.ds(al(k % 2, 128), 128)]
                dst = xin.at[it, pl.ds(bx * 16, 16), pl.ds(4 * h, 4)]
                if t:
                    there.append(remote(src, dst, xs.at[h, t], xr.at[h, t], (k, by)))
                else:
                    there.append(pltpu.make_async_copy(src, dst, xs.at[h, 0]))
                there[-1].start()
        lines = xin.at[it].reshape(NI * CX * 8, 128)
        moved = dxp.reshape((NI * CX + 2) * 8, 128)
        copies = []

        def edges(side, beside):
            out = []
            for t in range(NI):
                k = bx_peer(bx, t)
                out.append(
                    remote(
                        edge.at[side, pl.ds(al(k, 16), 16)],
                        yhx.at[it, side, :, pl.ds(al(zh, 128), 128)],
                        es.at[side, t],
                        er.at[side, zh],
                        (k, beside),
                    )
                )
            return out

        def half(side, z):
            return remote(
                edge.at[side, pl.ds(0, 16)], yhx.at[it, side, :, pl.ds(128 * z, 128)],
                es.at[side, 0], er.at[side, z], (bx, by),
            )

        def back(part, h):
            low, planes = ((0, 6), (6, 4), (10, 4), (14, 4))[part]
            for t in BX_ORDER:
                k = bx_peer(bx, t)
                if part:
                    src = dxp.at[pl.ds(k * 16 + low, planes)]
                    dst = dx.at[it, pl.ds(low, planes), pl.ds(al(yg, 8), 8), pl.ds(al(zh, 128), 128)]
                else:
                    src = dxp.at[pl.ds(k * 16, planes), pl.ds(4 * h, 4)]
                    dst = dx.at[it, pl.ds(0, planes), pl.ds(al(2 * yg + h, 4), 4), pl.ds(al(zh, 128), 128)]
                n = part + h
                if t:
                    copies.append(remote(src, dst, bs.at[n, t], br.at[n, t], (k, by)))
                else:
                    copies.append(pltpu.make_async_copy(src, dst, bs.at[n, 0]))
                copies[-1].start()

        for h in range(2):
            for c in there[NI * h : NI * (h + 1)]:
                c.wait()
            for y in range(4 * h, 4 * h + 4, 2):
                v = jnp.concatenate([lines[pl.ds(y + n, 256, stride=8), :] for n in range(2)], axis=1)
                d = dot3(mxs[0], mxs[1], *split(v))
                moved[pl.ds(8 + y, 256, stride=8), :] = d[:, :128]
                moved[pl.ds(9 + y, 256, stride=8), :] = d[:, 128:]
                if y == 0:
                    edge[0] = d[:, :128]
                if y == 6:
                    edge[1] = d[:, 128:]
            back(0, h)
            if h == 0:

                @pl.when((yg == 0) & (by > 0))
                def _():
                    for c in edges(0, below):
                        c.start()

            else:

                @pl.when((yg == 7) & (by < NJ - 1))
                def _():
                    for c in edges(1, above):
                        c.start()

        for part in range(1, 4):
            back(part, 1)
        for c in copies[: 2 * NI]:
            c.wait()

        @pl.when(by < NJ - 1)
        def _():
            half(0, 0).wait_recv()
            half(0, 1).wait_recv()

        @pl.when(by > 0)
        def _():
            half(1, 0).wait_recv()
            half(1, 1).wait_recv()

        for part in range(4):
            if part:
                for c in copies[NI * (part + 1) : NI * (part + 2)]:
                    c.wait()
            e = part // 2
            for t in (1, 2, 3, 0):
                i = (by // 2 + t) % 4
                x, j = 4 * part + i, 2 * i + part % 2
                plane(
                    dx.at[it],
                    x,
                    lambda x: yhx[it, 1, pl.ds(x, 1), :],
                    lambda x: yhx[it, 0, pl.ds(x, 1), :],
                )
                src, dst = r.at[x], yin.at[it, e, pl.ds(al(by, 64), 64)]

                def away():
                    remote(src, dst, ys.at[e, j], yr.at[e, by], (bx, j)).start()

                if t:
                    away()
                else:
                    pl.when(by % 2 != part % 2)(away)

                    @pl.when(by % 2 == part % 2)
                    def _():
                        pltpu.make_async_copy(src, dst, yr.at[e, by]).start()

        def gone(e, j):
            return remote(r.at[0], yin.at[it, e, pl.ds(al(j, 64), 64)], ys.at[e, j], yr.at[e, j], (bx, by))

        @pl.when((yg == 0) & (by > 0))
        def _():
            for c in edges(0, below):
                c.wait_send()

        @pl.when((yg == 7) & (by < NJ - 1))
        def _():
            for c in edges(1, above):
                c.wait_send()

        copies = []
        for e in range(2):
            for j in range(NJ):
                gone(e, j).wait_recv()
            d = dot3(mys[0], mys[1], *split(yin[it, e]))
            dyl[e] = d
            for j in range(NJ):
                for n in range(2):
                    if j:
                        ye[e, j, n : n + 1] = d[64 * j - 1 : 64 * j, 128 * n : 128 * (n + 1)]
                    if j < NJ - 1:
                        ye[e, j, 2 + n : 3 + n] = d[64 * j + 64 : 64 * j + 65, 128 * n : 128 * (n + 1)]
            for t in [*range(1, NJ), 0]:
                j = (by + t) % NJ
                main = (dyl.at[e, pl.ds(al(j, 64), 64)], dy.at[it, 1 + held(by) + NJ * e])
                outer = (ye.at[e, j], yhy.at[it, e, by])
                if t:
                    copies.append(remote(*main, cs.at[e, t], cr.at[e, by], (bx, j)))
                    copies.append(remote(*outer, ns.at[e, t], nr.at[e, t], (bx, j)))
                else:
                    copies.append(pltpu.make_async_copy(*main, cr.at[e, by]))
                    copies.append(pltpu.make_async_copy(*outer, ns.at[e, 0]))
                copies[-2].start()
                copies[-1].start()

        for t in range(1, NJ):
            for e in range(2):
                gone(e, (by + t) % NJ).wait_send()

        def arrived(e, m):
            remote(
                dyl.at[e, pl.ds(0, 64)], dy.at[it, 1 + held(m) + NJ * e], cs.at[e, 0], cr.at[e, m], (bx, by)
            ).wait_recv()

        def rest(e):
            for n in range(2 * NJ * e, 2 * NJ * (e + 1) - 2, 2):
                copies[n].wait_send()
                copies[n + 1].wait()
            copies[2 * NJ * (e + 1) - 1].wait()

        def outer_row(side):
            def load(x):
                at = (it, x // NJ, 2 * (x % 4) + x // 4 % 2)
                return jnp.concatenate(
                    [yhy[(*at, pl.ds(2 * side + n, 1), slice(None))] for n in range(2)], axis=1
                )

            return load

        rows = (outer_row(0), outer_row(1))
        down, up = x_planes(dy.at[it], hs, hr)
        arrived(0, 0)

        @pl.when(bx > 0)
        def _():
            down.start()

        for m in range(1, NJ):
            arrived(0, m)
        rest(0)

        def z_planes(x, n):
            v = r[pl.ds(x, n)].reshape(n * CY, NZ)
            d = dot3(*split(v), mzs[0], mzs[1], lanes)
            dz[it, pl.ds(x + 1, n)] = d.reshape(n, CY, NZ)

        @pl.loop(1, NJ - 1)
        def _(x):
            plane(dy.at[it], x, *rows)

        for x in range(1, NJ - 1, 2):
            z_planes(x, 2)
        arrived(1, NJ - 1)

        @pl.when(bx < NI - 1)
        def _():
            up.start()

        for m in range(NJ - 1):
            arrived(1, m)
        rest(1)

        @pl.loop(NJ - 1, CX - 1)
        def _(x):
            plane(dy.at[it], x, *rows)

        @pl.when(bx > 0)
        def _():
            down.wait_send()
            up.wait_recv()

        @pl.when(bx < NI - 1)
        def _():
            up.wait_send()
            down.wait_recv()

        for x in (0, CX - 1):
            plane(dy.at[it], x, *rows)

        z_planes(0, 1)
        z_planes(CX - 1, 1)
        down, up = x_planes(dz.at[it], zs, zr)
        low = remote(ze.at[0], yhz.at[it, 0], zs.at[2], zr.at[2], (bx, below))
        high = remote(ze.at[1], yhz.at[it, 1], zs.at[3], zr.at[3], (bx, above))
        more = it < ITERS - 1

        @pl.when(more & (bx > 0))
        def _():
            down.start()

        @pl.when(more & (bx < NI - 1))
        def _():
            up.start()

        outer = jnp.concatenate(
            [r[x, y : y + 1, :] for y in (0, CY - 1) for x in range(CX)], axis=0
        )
        outer = dot3(*split(outer), mzs[0], mzs[1], lanes)
        ze[0] = outer[:CX]
        ze[1] = outer[CX:]

        @pl.when(more & (by > 0))
        def _():
            low.start()

        @pl.when(more & (by < NJ - 1))
        def _():
            high.start()

        for x in range(NJ - 1, CX - 1, 2):
            z_planes(x, 2)

        @pl.when(more)
        def _():
            @pl.loop(1, CX - 1)
            def _(x):
                plane(dz.at[it], x)

            @pl.when(bx > 0)
            def _():
                down.wait_send()
                up.wait_recv()

            @pl.when(bx < NI - 1)
            def _():
                up.wait_send()
                down.wait_recv()

            for x in (0, CX - 1):
                plane(dz.at[it], x)

            @pl.when(by > 0)
            def _():
                low.wait_send()
                high.wait_recv()

            @pl.when(by < NJ - 1)
            def _():
                high.wait_send()
                low.wait_recv()

            for x in range(CX):
                r[x, 0:1] += yhz[it, 1, x : x + 1, :]
                r[x, CY - 1 : CY] += yhz[it, 0, x : x + 1, :]

        @pl.when(it == ITERS - 1)
        def _():
            u_ref[...] = u_ref[...] + dz[it, pl.ds(1, CX)]

    for q in range(4):
        block = jnp.transpose(u_ref[pl.ds(4 * q, 4)].reshape(256, NZ))
        for n, piece in enumerate(chop(block, 2)):
            ut[pl.ds(256 * n, 256), pl.ds(256 * q, 256)] = piece.astype(BF16)

    def returned(j, t):
        return remote(back1.at[j], got1.at[pl.ds(al(by, 16), 16)], gs.at[t], gr.at[t], (bx, j))

    def sampled(t):
        j = (by + t) % NJ
        cell = slot[pl.ds(j, 1), :]
        a = hot(fit(CX * CY, cell // NZ))
        v = jnp.dot(ut[...], a, preferred_element_type=F32)
        v = jnp.where(fit(NZ, cell % NZ), v[:NZ] + v[NZ:], 0.0)
        v = jnp.sum(v, axis=0, keepdims=True)
        for i in range(NI):
            back1[j, i : i + 1, :CAP] = v[:, CAP * i : CAP * (i + 1)]

    @pl.loop(1, NJ)
    def _(t):
        sampled(t)
        returned((by + t) % NJ, t).start()

    sampled(0)
    mine = pltpu.make_async_copy(back1.at[by], got1.at[pl.ds(al(by, 16), 16)], gs.at[0])
    mine.start()
    for t in range(1, NJ):
        returned((by + t) % NJ, t).wait()
    mine.wait()
    for k in range(NI):
        back2[k] = got1[pl.ds(k, NJ, stride=NI), :]
    copies = []
    for t in range(NI):
        k = bx_peer(bx, t)
        src, dst = back2.at[k], got2.at[pl.ds(al(bx, 8), 8)]
        if t:
            copies.append(remote(src, dst, ks.at[t], kr.at[t], (k, by)))
        else:
            copies.append(pltpu.make_async_copy(src, dst, ks.at[0]))
        copies[-1].start()
    for c in copies:
        c.wait()
    found = [p.astype(BF16) for p in chop(jnp.transpose(got2[...])[:CAP], 3)]

    @pl.loop(0, P_DEV // 256, unroll=4)
    def _(c):
        at = pl.ds(al(c, 256), 256)
        ones = hot(fit(NB, own[:, at]))
        v = sum(jnp.dot(p, ones, preferred_element_type=F32) for p in found)
        imp_ref[:, at] = jnp.sum(jnp.where(fit(CAP, rank[:, at]), v, 0.0), axis=0, keepdims=True)


def local(normals, owners, cells, levels, rows, columns, depth):
    vm = pl.BlockSpec(memory_space=pltpu.VMEM)
    hb = pl.BlockSpec(memory_space=pl.ANY)
    brick = (CX, CY, NZ)
    tall = (ITERS, CX + 2, CY, NZ)
    dma = pltpu.SemaphoreType.DMA
    iterate, implicit = pl.pallas_call(
        relax,
        name="relax",
        out_shape=(jax.ShapeDtypeStruct(brick, F32), jax.ShapeDtypeStruct((1, P_DEV), F32)),
        in_specs=[vm, vm, vm, pl.BlockSpec(memory_space=pltpu.SMEM), hb, hb, hb],
        out_specs=(vm, vm),
        scratch_shapes=[
            pltpu.VMEM(brick, F32),
            pltpu.VMEM((ITERS, NI * CX, 8, 128), F32),
            pltpu.VMEM((NI * CX + 2, 8, 128), F32),
            pltpu.VMEM(tall, F32),
            pltpu.VMEM((2, NI * CX, 128), F32),
            pltpu.VMEM((ITERS, 2, CX, NZ), F32),
            pltpu.VMEM((ITERS, 2, NJ * CY, NZ), F32),
            pltpu.VMEM((2, NJ * CY, NZ), F32),
            pltpu.VMEM(tall, F32),
            pltpu.VMEM((2, NJ, 8, 128), F32),
            pltpu.VMEM((ITERS, 2, NJ, 8, 128), F32),
            pltpu.VMEM(tall, F32),
            pltpu.VMEM((2, CX, NZ), F32),
            pltpu.VMEM((ITERS, 2, CX, NZ), F32),
            pltpu.VMEM((256, 256), F32),
            pltpu.VMEM((512, 512), F32),
            pltpu.VMEM((256, 256), F32),
            pltpu.VMEM((2, 256, 256), BF16),
            pltpu.VMEM((2, 512, 512), BF16),
            pltpu.VMEM((2, 256, 256), BF16),
            pltpu.VMEM((2, NB, 128), F32),
            pltpu.VMEM((1, P_DEV), jnp.int32),
            pltpu.VMEM((2, NB, 128), F32),
            pltpu.VMEM((NJ, 2, NI, 128), F32),
            pltpu.VMEM((NJ, 2, NI, 128), F32),
            pltpu.VMEM((NJ, NI * CAP), jnp.int32),
            pltpu.VMEM((CX + 2, CY, NZ), F32),
            pltpu.VMEM(brick, F32),
            pltpu.VMEM(brick, F32),
            pltpu.VMEM((2, CX, NZ), F32),
            pltpu.VMEM((2, CX, NZ), F32),
            pltpu.VMEM((512, CX * CY), BF16),
            pltpu.VMEM((NJ, NI, 128), F32),
            pltpu.VMEM((NB, 128), F32),
            pltpu.VMEM((NI, NJ, 128), F32),
            pltpu.VMEM((NB, 128), F32),
            dma((2, NI)), dma((2, NI)), dma((5, NI)), dma((5, NI)),
            dma((2, NI)), dma((2, 2)),
            dma((2, NJ)), dma((2, NJ)), dma((2, NJ)), dma((2, NJ)), dma((2, NJ)), dma((2, NJ)),
            dma((2,)), dma((2,)), dma((4,)), dma((4,)),
            dma((NI,)), dma((NI,)), dma((NJ,)), dma((NJ,)), dma((4,)), dma((4,)),
            dma((NJ,)), dma((NJ,)), dma((NI,)), dma((NI,)), dma((3,)),
        ],
        compiler_params=pltpu.CompilerParams(
            collective_id=0, has_side_effects=True, vmem_limit_bytes=61 << 20
        ),
    )(normals, owners.reshape(1, P_DEV), cells.reshape(1, P_DEV), levels, rows, columns, depth)
    return iterate, implicit.reshape(P_DEV)


def solution(mesh):
    placed = (
        P(None, ("bx", "by")),
        P(("bx", "by"), None),
        P(("bx", "by")),
        P("bx", "by"),
        P(),
        P(),
        P(),
    )
    return jax.shard_map(
        local,
        mesh=mesh,
        in_specs=placed,
        out_specs=(P("bx", "by", None), P(("bx", "by"))),
        check_vma=False,
    )
```

```python
import functools
import jax
import jax.numpy as jnp
from jax import lax
from jax.experimental import pallas as pl
from jax.experimental.pallas import tpu as pltpu
from jax.sharding import PartitionSpec as P

CX, CY, NZ, ITERS = 16, 64, 256, 4
NI, NJ = 16, 8
NB, P_DEV, CAP = 128, 4096, 64
MESH = pl.DeviceIdType.MESH
F32, BF16 = jnp.float32, jnp.bfloat16


def split(v):
    hi = v.astype(BF16)
    return hi, (v - hi.astype(F32)).astype(BF16)


def dot3(a_hi, a_lo, b_hi, b_lo, dims=(((1,), (0,)), ((), ()))):
    mul = functools.partial(lax.dot_general, dimension_numbers=dims, preferred_element_type=F32)
    return mul(a_hi, b_hi) + (mul(a_lo, b_hi) + mul(a_hi, b_lo))


def remote(src, dst, send, recv, device):
    return pltpu.make_async_remote_copy(
        src_ref=src, dst_ref=dst, send_sem=send, recv_sem=recv, device_id=device, device_id_type=MESH
    )


def bx_peer(bx, t):
    y, z = bx // 4, bx % 4
    return ((y + t // 4) % 4) * 4 + (z + t % 4) % 4


BX_ORDER = (5, 10, 15, 1, 6, 11, 12, 2, 7, 8, 13, 3, 4, 9, 14, 0)


def al(v, m):
    return pl.multiple_of(v * m, m)


def held(j):
    return 4 * (j % 2) + j // 2


def greet(bx, by):
    barrier = pltpu.get_barrier_semaphore()
    count = 0
    for side in (0, 1, NJ - 1):
        for t in range(NI):
            if side == 0 and t == 0:
                continue
            pl.semaphore_signal(
                barrier, inc=1, device_id=(bx_peer(bx, t), (by + side) % NJ), device_id_type=MESH
            )
            count += 1
    for t in range(2, NJ - 1):
        pl.semaphore_signal(barrier, inc=1, device_id=(bx, (by + t) % NJ), device_id_type=MESH)
        count += 1
    return functools.partial(pl.semaphore_wait, barrier, count)


def relax(
    nrm, own, cel, lev_ref, mx_ref, my_ref, mz_ref, u_ref, imp_ref,
    r, xin, dxp, dx, edge, yhx, yin, dyl, dy, ye, yhy, dz, ze, yhz,
    mxv, myv, mzv, mxs, mys, mzs, zpart,
    box, rank, in1, out2, in2, slot, vx, vy, vz, fe, fh, ut, back1, got1, back2, got2,
    xs, xr, bs, br, es, er, ys, yr, cs, cr, ns, nr, hs, hr, zs, zr,
    ps, pr, qs, qr, fs, fr, gs, gr, ks, kr, ms,
):
    bx, by = lax.axis_index("bx"), lax.axis_index("by")
    yg, zh = bx // 2, bx % 2
    zero = jnp.zeros((8, 128), F32)
    dxp[0] = zero
    dxp[257] = zero
    for ref in (yhx, yhy, yhz):
        ref[...] = jnp.zeros(ref.shape, F32)
    ye[...] = jnp.zeros(ye.shape, F32)
    for it in range(ITERS):
        for ref in (dy, dz):
            ref[it, 0] = jnp.zeros((CY, NZ), F32)
            ref[it, CX + 1] = jnp.zeros((CY, NZ), F32)
    vx[0] = jnp.zeros((CY, NZ), F32)
    vx[CX + 1] = jnp.zeros((CY, NZ), F32)
    fh[...] = jnp.zeros(fh.shape, F32)
    back1[...] = jnp.zeros(back1.shape, F32)
    all_here = greet(bx, by)
    fetches = [
        pltpu.make_async_copy(m, v, ms.at[n])
        for n, (m, v) in enumerate(((mx_ref, mxv), (my_ref, myv), (mz_ref, mzv)))
    ]
    for c in fetches:
        c.start()
    vx[pl.ds(1, CX)] = jnp.zeros((CX, CY, NZ), F32)
    vy[...] = jnp.zeros(vy.shape, F32)
    vz[...] = jnp.zeros(vz.shape, F32)
    u_ref[...] = jnp.zeros(u_ref.shape, F32)
    below, above = jnp.maximum(by - 1, 0), jnp.minimum(by + 1, NJ - 1)
    lanes = (((1,), (1,)), ((), ()))

    def fit(rows, index):
        return lax.broadcasted_iota(jnp.int32, (rows, index.shape[1]), 0) == index

    def hot(mask):
        return jnp.where(mask, 1.0, 0.0).astype(BF16)

    def chop(v, n):
        pieces = []
        for _ in range(n):
            pieces.append(v.astype(BF16).astype(F32))
            v = v - pieces[-1]
        return pieces

    before = lax.broadcasted_iota(jnp.int32, (256, 256), 0) < lax.broadcasted_iota(jnp.int32, (256, 256), 1)
    counter = jnp.concatenate([hot(before), jnp.ones((256, 256), BF16)], axis=1)
    box[...] = jnp.zeros(box.shape, F32)

    def dispatch(c, seen):
        at = pl.ds(al(c, 256), 256)
        mine = fit(NB, own[:, at])
        ones = hot(mine)
        counts = jnp.dot(ones, counter, preferred_element_type=F32)
        place = jnp.sum(jnp.where(mine, counts[:, :256] + seen, 0.0), axis=0, keepdims=True)
        place = place.astype(jnp.int32)
        rank[:, at] = place
        there = fit(CAP, place)
        values = [nrm[k : k + 1, at] for k in range(3)] + [cel[:, at].astype(F32)]
        pieces = [chop(v, 3) for v in values]
        for n in range(3):
            w = jnp.concatenate([jnp.where(there, p[n], 0.0) for p in pieces], axis=0).astype(BF16)
            d = lax.dot_general(ones, w, lanes, preferred_element_type=F32)
            box[0] += d[:, :128]
            box[1] += d[:, 128:]
        return seen + counts[:, 256:]

    lax.fori_loop(0, P_DEV // 256, dispatch, jnp.zeros((NB, 256), F32), unroll=4)

    all_here()
    copies = []
    for t in range(NI):
        k = bx_peer(bx, t)
        src, dst = box.at[:, pl.ds(al(k, 8), 8)], in1.at[:, pl.ds(al(bx, 8), 8)]
        if t:
            copies.append(remote(src, dst, ps.at[t], pr.at[t], (k, by)))
        else:
            copies.append(pltpu.make_async_copy(src, dst, ps.at[0]))
        copies[-1].start()
    for c in copies:
        c.wait()
    for j in range(NJ):
        for h in range(2):
            out2[j, h] = in1.at[h][pl.ds(j, NI, stride=NJ), :]
    copies = []
    for t in range(NJ):
        j = (by + t) % NJ
        if t:
            copies.append(remote(out2.at[j], in2.at[by], qs.at[t], qr.at[t], (bx, j)))
        else:
            copies.append(pltpu.make_async_copy(out2.at[j], in2.at[by], qr.at[0]))
        copies[-1].start()
    for c, (v, vs) in zip(fetches, ((mxv, mxs), (myv, mys), (mzv, mzs))):
        c.wait()
        vs[0], vs[1] = split(v[...])

    @pl.loop(0, NJ)
    def _(t):
        j = (by + NJ - t) % NJ
        remote(out2.at[0], in2.at[j], qs.at[0], qr.at[t], (bx, by)).wait_recv()
        rows = []
        for k in range(4):
            v = in2[j, k // 2][:, CAP * (k % 2) : CAP * (k % 2 + 1)]
            rows.append(jnp.concatenate([v[i : i + 1] for i in range(NI)], axis=1))
        cell = rows[3].astype(jnp.int32)
        slot[pl.ds(j, 1), :] = cell
        depth = fit(NZ, cell % NZ)
        weighted = jnp.concatenate(
            [
                jnp.concatenate([jnp.where(depth, p, 0.0).astype(BF16) for p in chop(v, 2)], axis=1)
                for v in rows[:3]
            ],
            axis=0,
        )
        for q in range(4):
            a = hot(fit(256, cell // NZ - 256 * q))
            d = lax.dot_general(
                jnp.concatenate([a, a], axis=1), weighted, lanes, preferred_element_type=F32
            ).reshape(4, CY, 3 * NZ)
            vx[pl.ds(1 + 4 * q, 4)] += d[:, :, :NZ]
            vy[pl.ds(4 * q, 4)] += d[:, :, NZ : 2 * NZ]
            vz[pl.ds(4 * q, 4)] += d[:, :, 2 * NZ :]

    for c in copies[1:]:
        c.wait_send()

    down = remote(vx.at[1], vx.at[CX + 1], fs.at[0], fr.at[0], (jnp.maximum(bx - 1, 0), by))
    up = remote(vx.at[CX], vx.at[0], fs.at[1], fr.at[1], (jnp.minimum(bx + 1, NI - 1), by))
    for x in range(CX):
        fe[0, x : x + 1] = vy[x, 0:1]
        fe[1, x : x + 1] = vy[x, CY - 1 : CY]
    low = remote(fe.at[0], fh.at[0], fs.at[2], fr.at[2], (bx, below))
    high = remote(fe.at[1], fh.at[1], fs.at[3], fr.at[3], (bx, above))

    @pl.when(bx > 0)
    def _():
        down.start()

    @pl.when(bx < NI - 1)
    def _():
        up.start()

    @pl.when(by > 0)
    def _():
        low.start()

    @pl.when(by < NJ - 1)
    def _():
        high.start()

    @pl.when(by > 0)
    def _():
        low.wait_send()
        high.wait_recv()

    @pl.when(by < NJ - 1)
    def _():
        high.wait_send()
        low.wait_recv()

    @pl.when(bx > 0)
    def _():
        down.wait_send()
        up.wait_recv()

    @pl.when(bx < NI - 1)
    def _():
        up.wait_send()
        down.wait_recv()

    @pl.loop(0, CX)
    def _(x):
        zi = lax.broadcasted_iota(jnp.int32, (CY, NZ), 1)
        yi = lax.broadcasted_iota(jnp.int32, (CY, NZ), 0)
        b, c = vy[x], vz[x]
        total = vx[x + 2] - vx[x]
        total = total + jnp.where(yi == CY - 1, fh[0, pl.ds(x, 1), :], pltpu.roll(b, CY - 1, 0))
        total = total - jnp.where(yi == 0, fh[1, pl.ds(x, 1), :], pltpu.roll(b, 1, 0))
        total = total + jnp.where(zi == NZ - 1, 0.0, pltpu.roll(c, NZ - 1, 1))
        total = total - jnp.where(zi == 0, 0.0, pltpu.roll(c, 1, 1))
        r[x] = -0.5 * total

    diagonal = 6.0 + (1.0 + lev_ref[0, 0].astype(F32))

    def plane(d, x, low=None, high=None, under=True):
        c = d[x + 1]
        zi = lax.broadcasted_iota(jnp.int32, (CY, NZ), 1)
        yi = lax.broadcasted_iota(jnp.int32, (CY, NZ), 0)
        near = d[x] + d[x + 2] if under else d[x + 2]
        near = near + jnp.where(zi == 0, 0.0, pltpu.roll(c, 1, 1))
        near = near + jnp.where(zi == NZ - 1, 0.0, pltpu.roll(c, NZ - 1, 1))
        near = near + jnp.where(yi == 0, low(x) if low else 0.0, pltpu.roll(c, 1, 0))
        near = near + jnp.where(yi == CY - 1, high(x) if high else 0.0, pltpu.roll(c, CY - 1, 0))
        r[x] = r[x] - (diagonal * c - near)
        u_ref[x] = u_ref[x] + c

    def x_planes(d, send, recv):
        down = remote(d.at[1], d.at[CX + 1], send.at[0], recv.at[0], (jnp.maximum(bx - 1, 0), by))
        up = remote(d.at[CX], d.at[0], send.at[1], recv.at[1], (jnp.minimum(bx + 1, NI - 1), by))
        return down, up

    @pl.loop(0, ITERS)
    def _(it):
        there = []
        for h in range(2):
            for t in BX_ORDER:
                k = bx_peer(bx, t)
                src = r.at[:, pl.ds(al(2 * (k // 2) + h, 4), 4), pl.ds(al(k % 2, 128), 128)]
                dst = xin.at[it, pl.ds(bx * 16, 16), pl.ds(4 * h, 4)]
                if t:
                    there.append(remote(src, dst, xs.at[h, t], xr.at[h, t], (k, by)))
                else:
                    there.append(pltpu.make_async_copy(src, dst, xs.at[h, 0]))
                there[-1].start()
        lines = xin.at[it].reshape(NI * CX * 8, 128)
        moved = dxp.reshape((NI * CX + 2) * 8, 128)
        copies = []

        def edges(side, beside):
            out = []
            for t in range(NI):
                k = bx_peer(bx, t)
                out.append(
                    remote(
                        edge.at[side, pl.ds(al(k, 16), 16)],
                        yhx.at[it, side, :, pl.ds(al(zh, 128), 128)],
                        es.at[side, t],
                        er.at[side, zh],
                        (k, beside),
                    )
                )
            return out

        def half(side, z):
            return remote(
                edge.at[side, pl.ds(0, 16)], yhx.at[it, side, :, pl.ds(128 * z, 128)],
                es.at[side, 0], er.at[side, z], (bx, by),
            )

        def back(part, h):
            low, planes = ((0, 6), (6, 4), (10, 4), (14, 4))[part]
            for t in BX_ORDER:
                k = bx_peer(bx, t)
                if part:
                    src = dxp.at[pl.ds(k * 16 + low, planes)]
                    dst = dx.at[it, pl.ds(low, planes), pl.ds(al(yg, 8), 8), pl.ds(al(zh, 128), 128)]
                else:
                    src = dxp.at[pl.ds(k * 16, planes), pl.ds(4 * h, 4)]
                    dst = dx.at[it, pl.ds(0, planes), pl.ds(al(2 * yg + h, 4), 4), pl.ds(al(zh, 128), 128)]
                n = part + h
                if t:
                    copies.append(remote(src, dst, bs.at[n, t], br.at[n, t], (k, by)))
                else:
                    copies.append(pltpu.make_async_copy(src, dst, bs.at[n, 0]))
                copies[-1].start()

        for h in range(2):
            for c in there[NI * h : NI * (h + 1)]:
                c.wait()
            for y in range(4 * h, 4 * h + 4, 2):
                v = jnp.concatenate([lines[pl.ds(y + n, 256, stride=8), :] for n in range(2)], axis=1)
                d = dot3(mxs[0], mxs[1], *split(v))
                moved[pl.ds(8 + y, 256, stride=8), :] = d[:, :128]
                moved[pl.ds(9 + y, 256, stride=8), :] = d[:, 128:]
                if y == 0:
                    edge[0] = d[:, :128]
                if y == 6:
                    edge[1] = d[:, 128:]
            back(0, h)
            if h == 0:

                @pl.when((yg == 0) & (by > 0))
                def _():
                    for c in edges(0, below):
                        c.start()

            else:

                @pl.when((yg == 7) & (by < NJ - 1))
                def _():
                    for c in edges(1, above):
                        c.start()

        for part in range(1, 4):
            back(part, 1)
        for c in copies[: 2 * NI]:
            c.wait()

        @pl.when(by < NJ - 1)
        def _():
            half(0, 0).wait_recv()
            half(0, 1).wait_recv()

        @pl.when(by > 0)
        def _():
            half(1, 0).wait_recv()
            half(1, 1).wait_recv()

        for part in range(4):
            if part:
                for c in copies[NI * (part + 1) : NI * (part + 2)]:
                    c.wait()
            e = part // 2
            for t in (1, 2, 3, 0):
                i = (by // 2 + t) % 4
                x, j = 4 * part + i, 2 * i + part % 2
                plane(
                    dx.at[it],
                    x,
                    lambda x: yhx[it, 1, pl.ds(x, 1), :],
                    lambda x: yhx[it, 0, pl.ds(x, 1), :],
                )
                src, dst = r.at[x], yin.at[it, e, pl.ds(al(by, 64), 64)]

                def away():
                    remote(src, dst, ys.at[e, j], yr.at[e, by], (bx, j)).start()

                if t:
                    away()
                else:
                    pl.when(by % 2 != part % 2)(away)

                    @pl.when(by % 2 == part % 2)
                    def _():
                        pltpu.make_async_copy(src, dst, yr.at[e, by]).start()

        def gone(e, j):
            return remote(r.at[0], yin.at[it, e, pl.ds(al(j, 64), 64)], ys.at[e, j], yr.at[e, j], (bx, by))

        @pl.when((yg == 0) & (by > 0))
        def _():
            for c in edges(0, below):
                c.wait_send()

        @pl.when((yg == 7) & (by < NJ - 1))
        def _():
            for c in edges(1, above):
                c.wait_send()

        copies = []
        for e in range(2):
            for j in range(NJ):
                gone(e, j).wait_recv()
            d = dot3(mys[0], mys[1], *split(yin[it, e]))
            dyl[e] = d
            for j in range(NJ):
                for n in range(2):
                    if j:
                        ye[e, j, n : n + 1] = d[64 * j - 1 : 64 * j, 128 * n : 128 * (n + 1)]
                    if j < NJ - 1:
                        ye[e, j, 2 + n : 3 + n] = d[64 * j + 64 : 64 * j + 65, 128 * n : 128 * (n + 1)]
            for t in [*range(1, NJ), 0]:
                j = (by + t) % NJ
                main = (dyl.at[e, pl.ds(al(j, 64), 64)], dy.at[it, 1 + held(by) + NJ * e])
                outer = (ye.at[e, j], yhy.at[it, e, by])
                if t:
                    copies.append(remote(*main, cs.at[e, t], cr.at[e, by], (bx, j)))
                    copies.append(remote(*outer, ns.at[e, t], nr.at[e, t], (bx, j)))
                else:
                    copies.append(pltpu.make_async_copy(*main, cr.at[e, by]))
                    copies.append(pltpu.make_async_copy(*outer, ns.at[e, 0]))
                copies[-2].start()
                copies[-1].start()

        for t in range(1, NJ):
            for e in range(2):
                gone(e, (by + t) % NJ).wait_send()

        def arrived(e, m):
            remote(
                dyl.at[e, pl.ds(0, 64)], dy.at[it, 1 + held(m) + NJ * e], cs.at[e, 0], cr.at[e, m], (bx, by)
            ).wait_recv()

        def rest(e):
            for n in range(2 * NJ * e, 2 * NJ * (e + 1) - 2, 2):
                copies[n].wait_send()
                copies[n + 1].wait()
            copies[2 * NJ * (e + 1) - 1].wait()

        def outer_row(side):
            def load(x):
                at = (it, x // NJ, 2 * (x % 4) + x // 4 % 2)
                return jnp.concatenate(
                    [yhy[(*at, pl.ds(2 * side + n, 1), slice(None))] for n in range(2)], axis=1
                )

            return load

        rows = (outer_row(0), outer_row(1))
        down, up = x_planes(dy.at[it], hs, hr)
        arrived(0, 0)

        @pl.when(bx > 0)
        def _():
            down.start()

        for m in range(1, NJ):
            arrived(0, m)
        rest(0)

        def z_lines(v):
            return dot3(*split(v), mzs[0], mzs[1], lanes)

        def z_planes(x, n):
            v = r[pl.ds(x, n)].reshape(n * CY, NZ)
            d = z_lines(v)
            dz[it, pl.ds(x + 1, n)] = d.reshape(n, CY, NZ)

        @pl.loop(1, NJ - 1)
        def _(x):
            plane(dy.at[it], x, *rows)

        for x in range(1, NJ - 1, 2):
            z_planes(x, 2)
        plane(dy.at[it], 0, *rows, under=False)
        zpart[...] = z_lines(r[0])
        z_down = remote(zpart, dz.at[it, CX + 1], zs.at[0], zr.at[0], (jnp.maximum(bx - 1, 0), by))
        z_up = remote(dz.at[it, CX], dz.at[it, 0], zs.at[1], zr.at[1], (jnp.minimum(bx + 1, NI - 1), by))
        low = remote(ze.at[0], yhz.at[it, 0], zs.at[2], zr.at[2], (bx, below))
        high = remote(ze.at[1], yhz.at[it, 1], zs.at[3], zr.at[3], (bx, above))
        more = it < ITERS - 1

        @pl.when(more & (bx > 0))
        def _():
            z_down.start()

        arrived(1, NJ - 1)

        @pl.when(bx < NI - 1)
        def _():
            up.start()

        for m in range(NJ - 1):
            arrived(1, m)
        rest(1)

        @pl.when(bx < NI - 1)
        def _():
            down.wait_recv()

        plane(dy.at[it], CX - 1, *rows)
        z_planes(CX - 1, 1)

        @pl.when(more & (bx < NI - 1))
        def _():
            z_up.start()

        @pl.loop(NJ - 1, CX - 1)
        def _(x):
            plane(dy.at[it], x, *rows)

        for x in range(NJ - 1, CX - 1, 2):
            z_planes(x, 2)

        @pl.when(bx > 0)
        def _():
            down.wait_send()
            up.wait_recv()
            r[0] += dy[it, 0]

        @pl.when(bx < NI - 1)
        def _():
            up.wait_send()

        z_planes(0, 1)
        outer = jnp.concatenate(
            [r[x, y : y + 1, :] for y in (0, CY - 1) for x in range(CX)], axis=0
        )
        outer = dot3(*split(outer), mzs[0], mzs[1], lanes)
        ze[0] = outer[:CX]
        ze[1] = outer[CX:]

        @pl.when(more & (by > 0))
        def _():
            low.start()

        @pl.when(more & (by < NJ - 1))
        def _():
            high.start()

        @pl.when(more)
        def _():
            @pl.loop(1, CX - 1)
            def _(x):
                plane(dz.at[it], x)

            @pl.when(bx > 0)
            def _():
                z_down.wait_send()
                z_up.wait_recv()

            @pl.when(bx < NI - 1)
            def _():
                z_up.wait_send()
                z_down.wait_recv()
                dz[it, CX + 1] += z_lines(dy[it, CX])

            for x in (0, CX - 1):
                plane(dz.at[it], x)

            @pl.when(by > 0)
            def _():
                low.wait_send()
                high.wait_recv()

            @pl.when(by < NJ - 1)
            def _():
                high.wait_send()
                low.wait_recv()

            for x in range(CX):
                r[x, 0:1] += yhz[it, 1, x : x + 1, :]
                r[x, CY - 1 : CY] += yhz[it, 0, x : x + 1, :]

        @pl.when(it == ITERS - 1)
        def _():
            u_ref[...] = u_ref[...] + dz[it, pl.ds(1, CX)]

    for q in range(4):
        block = jnp.transpose(u_ref[pl.ds(4 * q, 4)].reshape(256, NZ))
        for n, piece in enumerate(chop(block, 2)):
            ut[pl.ds(256 * n, 256), pl.ds(256 * q, 256)] = piece.astype(BF16)

    def returned(j, t):
        return remote(back1.at[j], got1.at[pl.ds(al(by, 16), 16)], gs.at[t], gr.at[t], (bx, j))

    def sampled(t):
        j = (by + t) % NJ
        cell = slot[pl.ds(j, 1), :]
        a = hot(fit(CX * CY, cell // NZ))
        v = jnp.dot(ut[...], a, preferred_element_type=F32)
        v = jnp.where(fit(NZ, cell % NZ), v[:NZ] + v[NZ:], 0.0)
        v = jnp.sum(v, axis=0, keepdims=True)
        for i in range(NI):
            back1[j, i : i + 1, :CAP] = v[:, CAP * i : CAP * (i + 1)]

    @pl.loop(1, NJ)
    def _(t):
        sampled(t)
        returned((by + t) % NJ, t).start()

    sampled(0)
    mine = pltpu.make_async_copy(back1.at[by], got1.at[pl.ds(al(by, 16), 16)], gs.at[0])
    mine.start()
    for t in range(1, NJ):
        returned((by + t) % NJ, t).wait()
    mine.wait()
    for k in range(NI):
        back2[k] = got1[pl.ds(k, NJ, stride=NI), :]
    copies = []
    for t in range(NI):
        k = bx_peer(bx, t)
        src, dst = back2.at[k], got2.at[pl.ds(al(bx, 8), 8)]
        if t:
            copies.append(remote(src, dst, ks.at[t], kr.at[t], (k, by)))
        else:
            copies.append(pltpu.make_async_copy(src, dst, ks.at[0]))
        copies[-1].start()
    for c in copies:
        c.wait()
    found = [p.astype(BF16) for p in chop(jnp.transpose(got2[...])[:CAP], 3)]

    @pl.loop(0, P_DEV // 256, unroll=4)
    def _(c):
        at = pl.ds(al(c, 256), 256)
        ones = hot(fit(NB, own[:, at]))
        v = sum(jnp.dot(p, ones, preferred_element_type=F32) for p in found)
        imp_ref[:, at] = jnp.sum(jnp.where(fit(CAP, rank[:, at]), v, 0.0), axis=0, keepdims=True)


def local(normals, owners, cells, levels, rows, columns, depth):
    vm = pl.BlockSpec(memory_space=pltpu.VMEM)
    hb = pl.BlockSpec(memory_space=pl.ANY)
    brick = (CX, CY, NZ)
    tall = (ITERS, CX + 2, CY, NZ)
    dma = pltpu.SemaphoreType.DMA
    iterate, implicit = pl.pallas_call(
        relax,
        name="relax",
        out_shape=(jax.ShapeDtypeStruct(brick, F32), jax.ShapeDtypeStruct((1, P_DEV), F32)),
        in_specs=[vm, vm, vm, pl.BlockSpec(memory_space=pltpu.SMEM), hb, hb, hb],
        out_specs=(vm, vm),
        scratch_shapes=[
            pltpu.VMEM(brick, F32),
            pltpu.VMEM((ITERS, NI * CX, 8, 128), F32),
            pltpu.VMEM((NI * CX + 2, 8, 128), F32),
            pltpu.VMEM(tall, F32),
            pltpu.VMEM((2, NI * CX, 128), F32),
            pltpu.VMEM((ITERS, 2, CX, NZ), F32),
            pltpu.VMEM((ITERS, 2, NJ * CY, NZ), F32),
            pltpu.VMEM((2, NJ * CY, NZ), F32),
            pltpu.VMEM(tall, F32),
            pltpu.VMEM((2, NJ, 8, 128), F32),
            pltpu.VMEM((ITERS, 2, NJ, 8, 128), F32),
            pltpu.VMEM(tall, F32),
            pltpu.VMEM((2, CX, NZ), F32),
            pltpu.VMEM((ITERS, 2, CX, NZ), F32),
            pltpu.VMEM((256, 256), F32),
            pltpu.VMEM((512, 512), F32),
            pltpu.VMEM((256, 256), F32),
            pltpu.VMEM((2, 256, 256), BF16),
            pltpu.VMEM((2, 512, 512), BF16),
            pltpu.VMEM((2, 256, 256), BF16),
            pltpu.VMEM((CY, NZ), F32),
            pltpu.VMEM((2, NB, 128), F32),
            pltpu.VMEM((1, P_DEV), jnp.int32),
            pltpu.VMEM((2, NB, 128), F32),
            pltpu.VMEM((NJ, 2, NI, 128), F32),
            pltpu.VMEM((NJ, 2, NI, 128), F32),
            pltpu.VMEM((NJ, NI * CAP), jnp.int32),
            pltpu.VMEM((CX + 2, CY, NZ), F32),
            pltpu.VMEM(brick, F32),
            pltpu.VMEM(brick, F32),
            pltpu.VMEM((2, CX, NZ), F32),
            pltpu.VMEM((2, CX, NZ), F32),
            pltpu.VMEM((512, CX * CY), BF16),
            pltpu.VMEM((NJ, NI, 128), F32),
            pltpu.VMEM((NB, 128), F32),
            pltpu.VMEM((NI, NJ, 128), F32),
            pltpu.VMEM((NB, 128), F32),
            dma((2, NI)), dma((2, NI)), dma((5, NI)), dma((5, NI)),
            dma((2, NI)), dma((2, 2)),
            dma((2, NJ)), dma((2, NJ)), dma((2, NJ)), dma((2, NJ)), dma((2, NJ)), dma((2, NJ)),
            dma((2,)), dma((2,)), dma((4,)), dma((4,)),
            dma((NI,)), dma((NI,)), dma((NJ,)), dma((NJ,)), dma((4,)), dma((4,)),
            dma((NJ,)), dma((NJ,)), dma((NI,)), dma((NI,)), dma((3,)),
        ],
        compiler_params=pltpu.CompilerParams(
            collective_id=0, has_side_effects=True, vmem_limit_bytes=61 << 20
        ),
    )(normals, owners.reshape(1, P_DEV), cells.reshape(1, P_DEV), levels, rows, columns, depth)
    return iterate, implicit.reshape(P_DEV)


def solution(mesh):
    placed = (
        P(None, ("bx", "by")),
        P(("bx", "by"), None),
        P(("bx", "by")),
        P("bx", "by"),
        P(),
        P(),
        P(),
    )
    return jax.shard_map(
        local,
        mesh=mesh,
        in_specs=placed,
        out_specs=(P("bx", "by", None), P(("bx", "by"))),
        check_vma=False,
    )
```

```python
import functools
import jax
import jax.numpy as jnp
from jax import lax
from jax.experimental import pallas as pl
from jax.experimental.pallas import tpu as pltpu
from jax.sharding import PartitionSpec as P

CX, CY, NZ, ITERS = 16, 64, 256, 4
NI, NJ = 16, 8
NB, P_DEV, CAP = 128, 4096, 64
MESH = pl.DeviceIdType.MESH
F32, BF16 = jnp.float32, jnp.bfloat16


def split(v):
    hi = v.astype(BF16)
    return hi, (v - hi.astype(F32)).astype(BF16)


def dot3(a_hi, a_lo, b_hi, b_lo, dims=(((1,), (0,)), ((), ()))):
    mul = functools.partial(lax.dot_general, dimension_numbers=dims, preferred_element_type=F32)
    return mul(a_hi, b_hi) + (mul(a_lo, b_hi) + mul(a_hi, b_lo))


def remote(src, dst, send, recv, device):
    return pltpu.make_async_remote_copy(
        src_ref=src, dst_ref=dst, send_sem=send, recv_sem=recv, device_id=device, device_id_type=MESH
    )


def bx_peer(bx, t):
    y, z = bx // 4, bx % 4
    return ((y + t // 4) % 4) * 4 + (z + t % 4) % 4


BX_ORDER = (5, 10, 15, 1, 6, 11, 12, 2, 7, 8, 13, 3, 4, 9, 14, 0)


def al(v, m):
    return pl.multiple_of(v * m, m)


def held(j):
    return 4 * (j % 2) + j // 2


def greet(bx, by):
    barrier = pltpu.get_barrier_semaphore()
    count = 0
    for side in (0, 1, NJ - 1):
        for t in range(NI):
            if side == 0 and t == 0:
                continue
            pl.semaphore_signal(
                barrier, inc=1, device_id=(bx_peer(bx, t), (by + side) % NJ), device_id_type=MESH
            )
            count += 1
    for t in range(2, NJ - 1):
        pl.semaphore_signal(barrier, inc=1, device_id=(bx, (by + t) % NJ), device_id_type=MESH)
        count += 1
    return functools.partial(pl.semaphore_wait, barrier, count)


def relax(
    nrm, own, cel, lev_ref, mx_ref, my_ref, mz_ref, u_ref, imp_ref,
    r, xin, dxp, dx, edge, yhx, yin, dyl, dy, ye, yhy, dz, ze, yhz,
    mxv, myv, mzv, mxs, mys, mzs, zpart,
    box, rank, in1, out2, in2, slot, vx, vy, vz, fe, fh, ut, back1, got1, back2, got2,
    xs, xr, bs, br, es, er, ys, yr, cs, cr, ns, nr, hs, hr, zs, zr,
    ps, pr, qs, qr, fs, fr, gs, gr, ks, kr, ms,
):
    bx, by = lax.axis_index("bx"), lax.axis_index("by")
    yg, zh = bx // 2, bx % 2
    zero = jnp.zeros((8, 128), F32)
    dxp[0] = zero
    dxp[257] = zero
    for ref in (yhx, yhy, yhz):
        ref[...] = jnp.zeros(ref.shape, F32)
    ye[...] = jnp.zeros(ye.shape, F32)
    for it in range(ITERS):
        for ref in (dy, dz):
            ref[it, 0] = jnp.zeros((CY, NZ), F32)
            ref[it, CX + 1] = jnp.zeros((CY, NZ), F32)
    vx[0] = jnp.zeros((CY, NZ), F32)
    vx[CX + 1] = jnp.zeros((CY, NZ), F32)
    fh[...] = jnp.zeros(fh.shape, F32)
    back1[...] = jnp.zeros(back1.shape, F32)
    all_here = greet(bx, by)
    fetches = [
        pltpu.make_async_copy(m, v, ms.at[n])
        for n, (m, v) in enumerate(((mx_ref, mxv), (my_ref, myv), (mz_ref, mzv)))
    ]
    for c in fetches:
        c.start()
    vx[pl.ds(1, CX)] = jnp.zeros((CX, CY, NZ), F32)
    vy[...] = jnp.zeros(vy.shape, F32)
    vz[...] = jnp.zeros(vz.shape, F32)
    u_ref[...] = jnp.zeros(u_ref.shape, F32)
    below, above = jnp.maximum(by - 1, 0), jnp.minimum(by + 1, NJ - 1)
    lanes = (((1,), (1,)), ((), ()))

    def fit(rows, index):
        return lax.broadcasted_iota(jnp.int32, (rows, index.shape[1]), 0) == index

    def hot(mask):
        return jnp.where(mask, 1.0, 0.0).astype(BF16)

    def chop(v, n):
        pieces = []
        for _ in range(n):
            pieces.append(v.astype(BF16).astype(F32))
            v = v - pieces[-1]
        return pieces

    before = lax.broadcasted_iota(jnp.int32, (256, 256), 0) < lax.broadcasted_iota(jnp.int32, (256, 256), 1)
    counter = jnp.concatenate([hot(before), jnp.ones((256, 256), BF16)], axis=1)
    box[...] = jnp.zeros(box.shape, F32)

    def dispatch(c, seen):
        at = pl.ds(al(c, 256), 256)
        mine = fit(NB, own[:, at])
        ones = hot(mine)
        counts = jnp.dot(ones, counter, preferred_element_type=F32)
        place = jnp.sum(jnp.where(mine, counts[:, :256] + seen, 0.0), axis=0, keepdims=True)
        place = place.astype(jnp.int32)
        rank[:, at] = place
        there = fit(CAP, place)
        values = [nrm[k : k + 1, at] for k in range(3)] + [cel[:, at].astype(F32)]
        pieces = [chop(v, 3) for v in values]
        for n in range(3):
            w = jnp.concatenate([jnp.where(there, p[n], 0.0) for p in pieces], axis=0).astype(BF16)
            d = lax.dot_general(ones, w, lanes, preferred_element_type=F32)
            box[0] += d[:, :128]
            box[1] += d[:, 128:]
        return seen + counts[:, 256:]

    lax.fori_loop(0, P_DEV // 256, dispatch, jnp.zeros((NB, 256), F32), unroll=4)

    all_here()
    copies = []
    for t in BX_ORDER:
        k = bx_peer(bx, t)
        src, dst = box.at[:, pl.ds(al(k, 8), 8)], in1.at[:, pl.ds(al(bx, 8), 8)]
        if t:
            copies.append(remote(src, dst, ps.at[t], pr.at[t], (k, by)))
        else:
            copies.append(pltpu.make_async_copy(src, dst, ps.at[0]))
        copies[-1].start()
    for c in copies:
        c.wait()
    for j in range(NJ):
        for h in range(2):
            out2[j, h] = in1.at[h][pl.ds(j, NI, stride=NJ), :]
    copies = []
    for t in range(NJ):
        j = (by + t) % NJ
        if t:
            copies.append(remote(out2.at[j], in2.at[by], qs.at[t], qr.at[t], (bx, j)))
        else:
            copies.append(pltpu.make_async_copy(out2.at[j], in2.at[by], qr.at[0]))
        copies[-1].start()
    for c, (v, vs) in zip(fetches, ((mxv, mxs), (myv, mys), (mzv, mzs))):
        c.wait()
        vs[0], vs[1] = split(v[...])

    @pl.loop(0, NJ)
    def _(t):
        j = (by + NJ - t) % NJ
        remote(out2.at[0], in2.at[j], qs.at[0], qr.at[t], (bx, by)).wait_recv()
        rows = []
        for k in range(4):
            v = in2[j, k // 2][:, CAP * (k % 2) : CAP * (k % 2 + 1)]
            rows.append(jnp.concatenate([v[i : i + 1] for i in range(NI)], axis=1))
        cell = rows[3].astype(jnp.int32)
        slot[pl.ds(j, 1), :] = cell
        depth = fit(NZ, cell % NZ)
        weighted = jnp.concatenate(
            [
                jnp.concatenate([jnp.where(depth, p, 0.0).astype(BF16) for p in chop(v, 2)], axis=1)
                for v in rows[:3]
            ],
            axis=0,
        )
        for q in range(4):
            a = hot(fit(256, cell // NZ - 256 * q))
            d = lax.dot_general(
                jnp.concatenate([a, a], axis=1), weighted, lanes, preferred_element_type=F32
            ).reshape(4, CY, 3 * NZ)
            vx[pl.ds(1 + 4 * q, 4)] += d[:, :, :NZ]
            vy[pl.ds(4 * q, 4)] += d[:, :, NZ : 2 * NZ]
            vz[pl.ds(4 * q, 4)] += d[:, :, 2 * NZ :]

    for c in copies[1:]:
        c.wait_send()

    down = remote(vx.at[1], vx.at[CX + 1], fs.at[0], fr.at[0], (jnp.maximum(bx - 1, 0), by))
    up = remote(vx.at[CX], vx.at[0], fs.at[1], fr.at[1], (jnp.minimum(bx + 1, NI - 1), by))
    for x in range(CX):
        fe[0, x : x + 1] = vy[x, 0:1]
        fe[1, x : x + 1] = vy[x, CY - 1 : CY]
    low = remote(fe.at[0], fh.at[0], fs.at[2], fr.at[2], (bx, below))
    high = remote(fe.at[1], fh.at[1], fs.at[3], fr.at[3], (bx, above))

    @pl.when(bx > 0)
    def _():
        down.start()

    @pl.when(bx < NI - 1)
    def _():
        up.start()

    @pl.when(by > 0)
    def _():
        low.start()

    @pl.when(by < NJ - 1)
    def _():
        high.start()

    @pl.when(by > 0)
    def _():
        low.wait_send()
        high.wait_recv()

    @pl.when(by < NJ - 1)
    def _():
        high.wait_send()
        low.wait_recv()

    @pl.when(bx > 0)
    def _():
        down.wait_send()
        up.wait_recv()

    @pl.when(bx < NI - 1)
    def _():
        up.wait_send()
        down.wait_recv()

    @pl.loop(0, CX)
    def _(x):
        zi = lax.broadcasted_iota(jnp.int32, (CY, NZ), 1)
        yi = lax.broadcasted_iota(jnp.int32, (CY, NZ), 0)
        b, c = vy[x], vz[x]
        total = vx[x + 2] - vx[x]
        total = total + jnp.where(yi == CY - 1, fh[0, pl.ds(x, 1), :], pltpu.roll(b, CY - 1, 0))
        total = total - jnp.where(yi == 0, fh[1, pl.ds(x, 1), :], pltpu.roll(b, 1, 0))
        total = total + jnp.where(zi == NZ - 1, 0.0, pltpu.roll(c, NZ - 1, 1))
        total = total - jnp.where(zi == 0, 0.0, pltpu.roll(c, 1, 1))
        r[x] = -0.5 * total

    diagonal = 6.0 + (1.0 + lev_ref[0, 0].astype(F32))

    def plane(d, x, low=None, high=None, under=True):
        c = d[x + 1]
        zi = lax.broadcasted_iota(jnp.int32, (CY, NZ), 1)
        yi = lax.broadcasted_iota(jnp.int32, (CY, NZ), 0)
        near = d[x] + d[x + 2] if under else d[x + 2]
        near = near + jnp.where(zi == 0, 0.0, pltpu.roll(c, 1, 1))
        near = near + jnp.where(zi == NZ - 1, 0.0, pltpu.roll(c, NZ - 1, 1))
        near = near + jnp.where(yi == 0, low(x) if low else 0.0, pltpu.roll(c, 1, 0))
        near = near + jnp.where(yi == CY - 1, high(x) if high else 0.0, pltpu.roll(c, CY - 1, 0))
        r[x] = r[x] - (diagonal * c - near)
        u_ref[x] = u_ref[x] + c

    def x_planes(d, send, recv):
        down = remote(d.at[1], d.at[CX + 1], send.at[0], recv.at[0], (jnp.maximum(bx - 1, 0), by))
        up = remote(d.at[CX], d.at[0], send.at[1], recv.at[1], (jnp.minimum(bx + 1, NI - 1), by))
        return down, up

    @pl.loop(0, ITERS)
    def _(it):
        there = []
        for h in range(2):
            for t in BX_ORDER:
                k = bx_peer(bx, t)
                src = r.at[:, pl.ds(al(2 * (k // 2) + h, 4), 4), pl.ds(al(k % 2, 128), 128)]
                dst = xin.at[it, pl.ds(bx * 16, 16), pl.ds(4 * h, 4)]
                if t:
                    there.append(remote(src, dst, xs.at[h, t], xr.at[h, t], (k, by)))
                else:
                    there.append(pltpu.make_async_copy(src, dst, xs.at[h, 0]))
                there[-1].start()
        lines = xin.at[it].reshape(NI * CX * 8, 128)
        moved = dxp.reshape((NI * CX + 2) * 8, 128)
        copies = []

        def edges(side, beside):
            out = []
            for t in range(NI):
                k = bx_peer(bx, t)
                out.append(
                    remote(
                        edge.at[side, pl.ds(al(k, 16), 16)],
                        yhx.at[it, side, :, pl.ds(al(zh, 128), 128)],
                        es.at[side, t],
                        er.at[side, zh],
                        (k, beside),
                    )
                )
            return out

        def half(side, z):
            return remote(
                edge.at[side, pl.ds(0, 16)], yhx.at[it, side, :, pl.ds(128 * z, 128)],
                es.at[side, 0], er.at[side, z], (bx, by),
            )

        def back(part, h):
            low, planes = ((0, 6), (6, 4), (10, 4), (14, 4))[part]
            for t in BX_ORDER:
                k = bx_peer(bx, t)
                if part:
                    src = dxp.at[pl.ds(k * 16 + low, planes)]
                    dst = dx.at[it, pl.ds(low, planes), pl.ds(al(yg, 8), 8), pl.ds(al(zh, 128), 128)]
                else:
                    src = dxp.at[pl.ds(k * 16, planes), pl.ds(4 * h, 4)]
                    dst = dx.at[it, pl.ds(0, planes), pl.ds(al(2 * yg + h, 4), 4), pl.ds(al(zh, 128), 128)]
                n = part + h
                if t:
                    copies.append(remote(src, dst, bs.at[n, t], br.at[n, t], (k, by)))
                else:
                    copies.append(pltpu.make_async_copy(src, dst, bs.at[n, 0]))
                copies[-1].start()

        for h in range(2):
            for c in there[NI * h : NI * (h + 1)]:
                c.wait()
            for y in range(4 * h, 4 * h + 4, 2):
                v = jnp.concatenate([lines[pl.ds(y + n, 256, stride=8), :] for n in range(2)], axis=1)
                d = dot3(mxs[0], mxs[1], *split(v))
                moved[pl.ds(8 + y, 256, stride=8), :] = d[:, :128]
                moved[pl.ds(9 + y, 256, stride=8), :] = d[:, 128:]
                if y == 0:
                    edge[0] = d[:, :128]
                if y == 6:
                    edge[1] = d[:, 128:]
            back(0, h)
            if h == 0:

                @pl.when((yg == 0) & (by > 0))
                def _():
                    for c in edges(0, below):
                        c.start()

            else:

                @pl.when((yg == 7) & (by < NJ - 1))
                def _():
                    for c in edges(1, above):
                        c.start()

        for part in range(1, 4):
            back(part, 1)
        for c in copies[: 2 * NI]:
            c.wait()

        @pl.when(by < NJ - 1)
        def _():
            half(0, 0).wait_recv()
            half(0, 1).wait_recv()

        @pl.when(by > 0)
        def _():
            half(1, 0).wait_recv()
            half(1, 1).wait_recv()

        for part in range(4):
            if part:
                for c in copies[NI * (part + 1) : NI * (part + 2)]:
                    c.wait()
            e = part // 2
            for t in (1, 2, 3, 0):
                i = (by // 2 + t) % 4
                x, j = 4 * part + i, 2 * i + part % 2
                plane(
                    dx.at[it],
                    x,
                    lambda x: yhx[it, 1, pl.ds(x, 1), :],
                    lambda x: yhx[it, 0, pl.ds(x, 1), :],
                )
                src, dst = r.at[x], yin.at[it, e, pl.ds(al(by, 64), 64)]

                def away():
                    remote(src, dst, ys.at[e, j], yr.at[e, by], (bx, j)).start()

                if t:
                    away()
                else:
                    pl.when(by % 2 != part % 2)(away)

                    @pl.when(by % 2 == part % 2)
                    def _():
                        pltpu.make_async_copy(src, dst, yr.at[e, by]).start()

        def gone(e, j):
            return remote(r.at[0], yin.at[it, e, pl.ds(al(j, 64), 64)], ys.at[e, j], yr.at[e, j], (bx, by))

        copies = []
        for e in range(2):
            for j in range(NJ):
                gone(e, j).wait_recv()
            d = dot3(mys[0], mys[1], *split(yin[it, e]))
            dyl[e] = d
            for j in range(NJ):
                for n in range(2):
                    if j:
                        ye[e, j, n : n + 1] = d[64 * j - 1 : 64 * j, 128 * n : 128 * (n + 1)]
                    if j < NJ - 1:
                        ye[e, j, 2 + n : 3 + n] = d[64 * j + 64 : 64 * j + 65, 128 * n : 128 * (n + 1)]
            for t in [*range(1, NJ), 0]:
                j = (by + t) % NJ
                main = (dyl.at[e, pl.ds(al(j, 64), 64)], dy.at[it, 1 + held(by) + NJ * e])
                outer = (ye.at[e, j], yhy.at[it, e, by])
                if t:
                    copies.append(remote(*main, cs.at[e, t], cr.at[e, by], (bx, j)))
                    copies.append(remote(*outer, ns.at[e, t], nr.at[e, t], (bx, j)))
                else:
                    copies.append(pltpu.make_async_copy(*main, cr.at[e, by]))
                    copies.append(pltpu.make_async_copy(*outer, ns.at[e, 0]))
                copies[-2].start()
                copies[-1].start()

        for t in range(1, NJ):
            for e in range(2):
                gone(e, (by + t) % NJ).wait_send()

        @pl.when((yg == 0) & (by > 0))
        def _():
            for c in edges(0, below):
                c.wait_send()

        @pl.when((yg == 7) & (by < NJ - 1))
        def _():
            for c in edges(1, above):
                c.wait_send()

        def arrived(e, m):
            remote(
                dyl.at[e, pl.ds(0, 64)], dy.at[it, 1 + held(m) + NJ * e], cs.at[e, 0], cr.at[e, m], (bx, by)
            ).wait_recv()

        def rest(e):
            for n in range(2 * NJ * e + 1, 2 * NJ * (e + 1) - 1, 2):
                copies[n].wait_recv()
            copies[2 * NJ * (e + 1) - 1].wait()

        def outer_row(side):
            def load(x):
                at = (it, x // NJ, 2 * (x % 4) + x // 4 % 2)
                return jnp.concatenate(
                    [yhy[(*at, pl.ds(2 * side + n, 1), slice(None))] for n in range(2)], axis=1
                )

            return load

        rows = (outer_row(0), outer_row(1))
        down, up = x_planes(dy.at[it], hs, hr)
        arrived(0, 0)

        @pl.when(bx > 0)
        def _():
            down.start()

        for m in range(1, NJ):
            arrived(0, m)
        rest(0)

        def z_lines(v):
            return dot3(*split(v), mzs[0], mzs[1], lanes)

        def z_planes(x, n):
            v = r[pl.ds(x, n)].reshape(n * CY, NZ)
            d = z_lines(v)
            dz[it, pl.ds(x + 1, n)] = d.reshape(n, CY, NZ)

        @pl.loop(1, NJ - 1)
        def _(x):
            plane(dy.at[it], x, *rows)

        for x in range(1, NJ - 1, 2):
            z_planes(x, 2)
        plane(dy.at[it], 0, *rows, under=False)
        zpart[...] = z_lines(r[0])
        z_down = remote(zpart, dz.at[it, CX + 1], zs.at[0], zr.at[0], (jnp.maximum(bx - 1, 0), by))
        z_up = remote(dz.at[it, CX], dz.at[it, 0], zs.at[1], zr.at[1], (jnp.minimum(bx + 1, NI - 1), by))
        low = remote(ze.at[0], yhz.at[it, 0], zs.at[2], zr.at[2], (bx, below))
        high = remote(ze.at[1], yhz.at[it, 1], zs.at[3], zr.at[3], (bx, above))
        more = it < ITERS - 1

        @pl.when(more & (bx > 0))
        def _():
            z_down.start()

        arrived(1, NJ - 1)

        @pl.when(bx < NI - 1)
        def _():
            up.start()

        for m in range(NJ - 1):
            arrived(1, m)
        rest(1)

        @pl.when(bx < NI - 1)
        def _():
            down.wait_recv()

        plane(dy.at[it], CX - 1, *rows)
        z_planes(CX - 1, 1)

        @pl.when(more & (bx < NI - 1))
        def _():
            z_up.start()

        @pl.loop(NJ - 1, CX - 1)
        def _(x):
            plane(dy.at[it], x, *rows)

        for x in range(NJ - 1, CX - 1, 2):
            z_planes(x, 2)

        @pl.when(bx > 0)
        def _():
            down.wait_send()
            up.wait_recv()
            r[0] += dy[it, 0]

        @pl.when(bx < NI - 1)
        def _():
            up.wait_send()

        z_planes(0, 1)
        outer = jnp.concatenate(
            [r[x, y : y + 1, :] for y in (0, CY - 1) for x in range(CX)], axis=0
        )
        outer = dot3(*split(outer), mzs[0], mzs[1], lanes)
        ze[0] = outer[:CX]
        ze[1] = outer[CX:]

        @pl.when(more & (by > 0))
        def _():
            low.start()

        @pl.when(more & (by < NJ - 1))
        def _():
            high.start()

        for e in range(2):
            for n in range(2 * NJ * e, 2 * NJ * (e + 1) - 2):
                copies[n].wait_send()

        @pl.when(more)
        def _():
            @pl.loop(1, CX - 1)
            def _(x):
                plane(dz.at[it], x)

            @pl.when(bx > 0)
            def _():
                z_down.wait_send()
                z_up.wait_recv()

            @pl.when(bx < NI - 1)
            def _():
                z_up.wait_send()
                z_down.wait_recv()
                dz[it, CX + 1] += z_lines(dy[it, CX])

            for x in (0, CX - 1):
                plane(dz.at[it], x)

            @pl.when(by > 0)
            def _():
                low.wait_send()
                high.wait_recv()

            @pl.when(by < NJ - 1)
            def _():
                high.wait_send()
                low.wait_recv()

            for x in range(CX):
                r[x, 0:1] += yhz[it, 1, x : x + 1, :]
                r[x, CY - 1 : CY] += yhz[it, 0, x : x + 1, :]

        @pl.when(it == ITERS - 1)
        def _():
            u_ref[...] = u_ref[...] + dz[it, pl.ds(1, CX)]

    for q in range(4):
        block = jnp.transpose(u_ref[pl.ds(4 * q, 4)].reshape(256, NZ))
        for n, piece in enumerate(chop(block, 2)):
            ut[pl.ds(256 * n, 256), pl.ds(256 * q, 256)] = piece.astype(BF16)

    def returned(j, t):
        return remote(back1.at[j], got1.at[pl.ds(al(by, 16), 16)], gs.at[t], gr.at[t], (bx, j))

    def sampled(t):
        j = (by + t) % NJ
        cell = slot[pl.ds(j, 1), :]
        a = hot(fit(CX * CY, cell // NZ))
        v = jnp.dot(ut[...], a, preferred_element_type=F32)
        v = jnp.where(fit(NZ, cell % NZ), v[:NZ] + v[NZ:], 0.0)
        v = jnp.sum(v, axis=0, keepdims=True)
        for i in range(NI):
            back1[j, i : i + 1, :CAP] = v[:, CAP * i : CAP * (i + 1)]

    @pl.loop(1, NJ)
    def _(t):
        sampled(t)
        returned((by + t) % NJ, t).start()

    sampled(0)
    mine = pltpu.make_async_copy(back1.at[by], got1.at[pl.ds(al(by, 16), 16)], gs.at[0])
    mine.start()
    for t in range(1, NJ):
        returned((by + t) % NJ, t).wait()
    mine.wait()
    for k in range(NI):
        back2[k] = got1[pl.ds(k, NJ, stride=NI), :]
    copies = []
    for t in BX_ORDER:
        k = bx_peer(bx, t)
        src, dst = back2.at[k], got2.at[pl.ds(al(bx, 8), 8)]
        if t:
            copies.append(remote(src, dst, ks.at[t], kr.at[t], (k, by)))
        else:
            copies.append(pltpu.make_async_copy(src, dst, ks.at[0]))
        copies[-1].start()
    for c in copies:
        c.wait()
    found = [p.astype(BF16) for p in chop(jnp.transpose(got2[...])[:CAP], 3)]

    @pl.loop(0, P_DEV // 256, unroll=4)
    def _(c):
        at = pl.ds(al(c, 256), 256)
        ones = hot(fit(NB, own[:, at]))
        v = sum(jnp.dot(p, ones, preferred_element_type=F32) for p in found)
        imp_ref[:, at] = jnp.sum(jnp.where(fit(CAP, rank[:, at]), v, 0.0), axis=0, keepdims=True)


def local(normals, owners, cells, levels, rows, columns, depth):
    vm = pl.BlockSpec(memory_space=pltpu.VMEM)
    hb = pl.BlockSpec(memory_space=pl.ANY)
    brick = (CX, CY, NZ)
    tall = (ITERS, CX + 2, CY, NZ)
    dma = pltpu.SemaphoreType.DMA
    iterate, implicit = pl.pallas_call(
        relax,
        name="relax",
        out_shape=(jax.ShapeDtypeStruct(brick, F32), jax.ShapeDtypeStruct((1, P_DEV), F32)),
        in_specs=[vm, vm, vm, pl.BlockSpec(memory_space=pltpu.SMEM), hb, hb, hb],
        out_specs=(vm, vm),
        scratch_shapes=[
            pltpu.VMEM(brick, F32),
            pltpu.VMEM((ITERS, NI * CX, 8, 128), F32),
            pltpu.VMEM((NI * CX + 2, 8, 128), F32),
            pltpu.VMEM(tall, F32),
            pltpu.VMEM((2, NI * CX, 128), F32),
            pltpu.VMEM((ITERS, 2, CX, NZ), F32),
            pltpu.VMEM((ITERS, 2, NJ * CY, NZ), F32),
            pltpu.VMEM((2, NJ * CY, NZ), F32),
            pltpu.VMEM(tall, F32),
            pltpu.VMEM((2, NJ, 8, 128), F32),
            pltpu.VMEM((ITERS, 2, NJ, 8, 128), F32),
            pltpu.VMEM(tall, F32),
            pltpu.VMEM((2, CX, NZ), F32),
            pltpu.VMEM((ITERS, 2, CX, NZ), F32),
            pltpu.VMEM((256, 256), F32),
            pltpu.VMEM((512, 512), F32),
            pltpu.VMEM((256, 256), F32),
            pltpu.VMEM((2, 256, 256), BF16),
            pltpu.VMEM((2, 512, 512), BF16),
            pltpu.VMEM((2, 256, 256), BF16),
            pltpu.VMEM((CY, NZ), F32),
            pltpu.VMEM((2, NB, 128), F32),
            pltpu.VMEM((1, P_DEV), jnp.int32),
            pltpu.VMEM((2, NB, 128), F32),
            pltpu.VMEM((NJ, 2, NI, 128), F32),
            pltpu.VMEM((NJ, 2, NI, 128), F32),
            pltpu.VMEM((NJ, NI * CAP), jnp.int32),
            pltpu.VMEM((CX + 2, CY, NZ), F32),
            pltpu.VMEM(brick, F32),
            pltpu.VMEM(brick, F32),
            pltpu.VMEM((2, CX, NZ), F32),
            pltpu.VMEM((2, CX, NZ), F32),
            pltpu.VMEM((512, CX * CY), BF16),
            pltpu.VMEM((NJ, NI, 128), F32),
            pltpu.VMEM((NB, 128), F32),
            pltpu.VMEM((NI, NJ, 128), F32),
            pltpu.VMEM((NB, 128), F32),
            dma((2, NI)), dma((2, NI)), dma((5, NI)), dma((5, NI)),
            dma((2, NI)), dma((2, 2)),
            dma((2, NJ)), dma((2, NJ)), dma((2, NJ)), dma((2, NJ)), dma((2, NJ)), dma((2, NJ)),
            dma((2,)), dma((2,)), dma((4,)), dma((4,)),
            dma((NI,)), dma((NI,)), dma((NJ,)), dma((NJ,)), dma((4,)), dma((4,)),
            dma((NJ,)), dma((NJ,)), dma((NI,)), dma((NI,)), dma((3,)),
        ],
        compiler_params=pltpu.CompilerParams(
            collective_id=0, has_side_effects=True, vmem_limit_bytes=61 << 20
        ),
    )(normals, owners.reshape(1, P_DEV), cells.reshape(1, P_DEV), levels, rows, columns, depth)
    return iterate, implicit.reshape(P_DEV)


def solution(mesh):
    placed = (
        P(None, ("bx", "by")),
        P(("bx", "by"), None),
        P(("bx", "by")),
        P("bx", "by"),
        P(),
        P(),
        P(),
    )
    return jax.shard_map(
        local,
        mesh=mesh,
        in_specs=placed,
        out_specs=(P("bx", "by", None), P(("bx", "by"))),
        check_vma=False,
    )
```
